32 devices in a mesh: tx: 8 (over z, core), ty: 4 (over y, x).
Axes of the slice: x: 2, y: 2, z: 4, core: 2. Of those that a mesh axis runs over, the one named last changes fastest.
Arguments:
- camera: int32 [64, 128], P('ty', 'tx'), may hold values from 0 to 99
- ray_mask: int32 [64, 128], P('ty', 'tx'), may hold values 0 or 1
- ray_direction: float32 [3, 64, 128], P(None, 'ty', 'tx'), may hold values from -1 to 1
- anchors: float32 [3, 100], replicated, may hold values from -1 to 1
- target: float32 [3, 64, 128], P(None, 'ty', 'tx'), may hold values from 0 to 1
- fine_levels: int32 [128, 64, 128], P(None, 'ty', 'tx'), may hold values from 0 to 1023, as said below
- density_bins: int32 [128, 64, 128], P(None, 'ty', 'tx'), may hold values from 0 to 63
- owners: int32 [5, 2], replicated, may hold values from 0 to 31
- encoder: float32 [32, 2, 256, 63], P(('tx', 'ty')), may hold values from -0.75 to 0.75
- middle: float32 [32, 2, 256, 256], P(('tx', 'ty')), may hold values from -0.375 to 0.375
- viewer: float32 [32, 2, 128, 283], P(('tx', 'ty')), may hold values from -0.375 to 0.375
- colour: float32 [32, 2, 3, 128], P(('tx', 'ty')), may hold values from -0.5 to 0.5
- scalars: float32 [32, 2, 900], P(('tx', 'ty')), may hold values from -0.375 to 0.375
- moment_encoder: float32 [32, 2, 256, 63], P(('tx', 'ty')), may hold values from -0.00061035156 to 0.00061035156
- moment_middle: float32 [32, 2, 256, 256], P(('tx', 'ty')), may hold values from -0.00061035156 to 0.00061035156
- moment_viewer: float32 [32, 2, 128, 283], P(('tx', 'ty')), may hold values from -0.00061035156 to 0.00061035156
- moment_colour: float32 [32, 2, 3, 128], P(('tx', 'ty')), may hold values from -0.00061035156 to 0.00061035156
- moment_scalars: float32 [32, 2, 900], P(('tx', 'ty')), may hold values from -0.00061035156 to 0.00061035156
- square_encoder: float32 [32, 2, 256, 63], P(('tx', 'ty')), may hold values from 9.536744e-10 to 3.8146974e-09
- square_middle: float32 [32, 2, 256, 256], P(('tx', 'ty')), may hold values from 9.536744e-10 to 3.8146974e-09
- square_viewer: float32 [32, 2, 128, 283], P(('tx', 'ty')), may hold values from 9.536744e-10 to 3.8146974e-09
- square_colour: float32 [32, 2, 3, 128], P(('tx', 'ty')), may hold values from 9.536744e-10 to 3.8146974e-09
- square_scalars: float32 [32, 2, 900], P(('tx', 'ty')), may hold values from 9.536744e-10 to 3.8146974e-09
Outputs:
- total_loss: float32 [], replicated
- density_histogram: float32 [64], replicated
- next_encoder: float32 [32, 2, 256, 63], P(('tx', 'ty'))
- next_middle: float32 [32, 2, 256, 256], P(('tx', 'ty'))
- next_viewer: float32 [32, 2, 128, 283], P(('tx', 'ty'))
- next_colour: float32 [32, 2, 3, 128], P(('tx', 'ty'))
- next_scalars: float32 [32, 2, 900], P(('tx', 'ty'))
- encoder_moment: float32 [32, 2, 256, 63], P(('tx', 'ty'))
- middle_moment: float32 [32, 2, 256, 256], P(('tx', 'ty'))
- viewer_moment: float32 [32, 2, 128, 283], P(('tx', 'ty'))
- colour_moment: float32 [32, 2, 3, 128], P(('tx', 'ty'))
- scalars_moment: float32 [32, 2, 900], P(('tx', 'ty'))
- encoder_square: float32 [32, 2, 256, 63], P(('tx', 'ty'))
- middle_square: float32 [32, 2, 256, 256], P(('tx', 'ty'))
- viewer_square: float32 [32, 2, 128, 283], P(('tx', 'ty'))
- colour_square: float32 [32, 2, 3, 128], P(('tx', 'ty'))
- scalars_square: float32 [32, 2, 900], P(('tx', 'ty'))
The draws below stay inside these ranges and needn't reach their ends.
Inputs may be any that keep to these rules, and one draw needn't show every extreme that they name: `fine_levels`: each ray's 128 fine levels never fall along the first dimension.
All inputs are finite; a program needn't handle non-finite values. No bound on the sum of `ray_mask` on one device may be relied on, other than what follows from the above.
Results may differ from the reference program's by a relative error of at most 0.0003.
The reference program's roundings to bfloat16 on the way count: a program that leaves them out, or rounds other values in their place, can miss the bound.
Values may be sent and summed in bfloat16 or wider, within the bound.
A program may use at most 64 MiB of HBM per device.

```python
import math
import jax
import jax.numpy as jnp
import numpy as np
from jax import lax

HID = 256
VIEW = 128
LPOS = 10
LDIR = 4
SC = 64
SF = 128
NT = 1024
NCAM = 100
NHIST = 64
ENC = 63
DENC = 27
NSMALL = 900
IMH = 64
IMW = 128
DEVICES = 32


def draw_fine_levels(key, part):
    levels = jax.random.randint(key, (SF, IMH, IMW), 0, NT)
    return jnp.sort(levels, axis=0).astype(jnp.int32)


def set_ends(result, key, low, largest):
    longest = result.shape.index(max(result.shape))
    spots = []
    for shift in (0, 1):
        where = [jax.random.randint(jax.random.fold_in(key, axis), (), 0, length) for axis, length in enumerate(result.shape)]
        where[longest] = (where[longest] + shift) % result.shape[longest]
        spots.append(tuple(where))
    return result.at[spots[0]].set(low).at[spots[1]].set(largest)


def shard_levels(key, shape, shards, low, largest):
    def one(axis_at, blocks):
        draws = jax.random.uniform(jax.random.fold_in(jax.random.fold_in(key, 6), axis_at), (blocks,), jnp.float32, low / len(shards), largest / len(shards))
        return jnp.repeat(jnp.exp(draws), shape[axis_at] // blocks).reshape((-1,) + (1,) * (len(shape) - axis_at - 1))

    factor_of = one(*shards[0])
    for cut in shards[1:]:
        factor_of = factor_of * one(*cut)
    return factor_of


def rank_bounds(number_of, slope):
    weights = [(1 << 20) // math.isqrt(standing ** slope) + 1 for standing in range(1, number_of + 1)]
    spread = 1 + sum(weights) // (1 << 30)
    return np.cumsum(np.array([max(1, weight // spread) for weight in weights]))


def ranked_ids(key, shape, count, slope):
    grid = rank_bounds(count, slope)
    ticket = jax.random.randint(jax.random.fold_in(key, 1), shape, 0, int(grid[count - 1]))
    rank = jnp.searchsorted(jnp.asarray(grid, jnp.int32), ticket, side="right")
    return jax.random.permutation(jax.random.fold_in(key, 2), count)[rank].astype(jnp.int32)


def centred(rng, dims, width, limit, cuts=(), kind=jnp.bfloat16):
    level = shard_levels(rng, dims, cuts, -0.22, 0.18) if cuts else 1.0
    array = jax.random.normal(rng, dims, jnp.float32) * width * level
    return jnp.minimum(jnp.maximum(array, -limit), limit).astype(kind)


def setup_inputs(seed: int = 0) -> dict:
    keys = jax.random.split(jax.random.key(seed), 24)
    camera = set_ends(ranked_ids(keys[0], (IMH, IMW), NCAM, 2), jax.random.fold_in(keys[0], 3), 0, NCAM - 1).astype(jnp.int32)
    ray_mask = set_ends((jax.random.randint(keys[1], (IMH, IMW), 0, 4) < 3).astype(jnp.int32), jax.random.fold_in(keys[1], 1), 0, 1)
    ray_direction = jnp.clip(jax.random.uniform(keys[2], (3, IMH, IMW), jnp.float32, -1.0, 1.0) * shard_levels(keys[2], (3, IMH, IMW), ((1, 4), (2, 8)), -0.4, 0.0), -1.0, 1.0)
    anchors = jnp.clip(jax.random.uniform(keys[3], (3, NCAM), jnp.float32, -1.0, 1.0), -1.0, 1.0)
    target = jnp.clip(1.0 * jax.random.uniform(keys[4], (3, IMH, IMW), jnp.float32) ** shard_levels(keys[4], (3, IMH, IMW), ((1, 4), (2, 8)), -0.2, 0.2), 0.0, 1.0)
    fine_levels = draw_fine_levels(jax.random.fold_in(keys[23], 71), 0)
    density_bins = set_ends(jax.random.randint(keys[6], (SF, IMH, IMW), 0, NHIST), jax.random.fold_in(keys[6], 1), 0, NHIST - 1).astype(jnp.int32)
    owners = set_ends(jax.random.randint(keys[7], (5, 2), 0, DEVICES), jax.random.fold_in(keys[7], 1), 0, DEVICES - 1).astype(jnp.int32)
    encoder = centred(keys[8], (DEVICES, 2, HID, ENC), ENC ** -0.5, 0.75, ((0, 32),), jnp.float32)
    middle = centred(keys[9], (DEVICES, 2, HID, HID), HID ** -0.5, 0.375, ((0, 32),), jnp.float32)
    viewer = centred(keys[10], (DEVICES, 2, VIEW, HID + DENC), (HID + DENC) ** -0.5, 0.375, ((0, 32),), jnp.float32)
    colour = centred(keys[11], (DEVICES, 2, 3, VIEW), VIEW ** -0.5, 0.5, ((0, 32),), jnp.float32)
    scalars = centred(keys[12], (DEVICES, 2, NSMALL), HID ** -0.5, 0.375, ((0, 32),), jnp.float32)
    moment_encoder = centred(keys[13], (DEVICES, 2, HID, ENC), (0.1 / (IMH * IMW * SF) ** 0.5), 0.00061035156, ((0, 32),), jnp.float32)
    moment_middle = centred(keys[14], (DEVICES, 2, HID, HID), (0.1 / (IMH * IMW * SF) ** 0.5), 0.00061035156, ((0, 32),), jnp.float32)
    moment_viewer = centred(keys[15], (DEVICES, 2, VIEW, HID + DENC), (0.1 / (IMH * IMW * SF) ** 0.5), 0.00061035156, ((0, 32),), jnp.float32)
    moment_colour = centred(keys[16], (DEVICES, 2, 3, VIEW), (0.1 / (IMH * IMW * SF) ** 0.5), 0.00061035156, ((0, 32),), jnp.float32)
    moment_scalars = centred(keys[17], (DEVICES, 2, NSMALL), (0.1 / (IMH * IMW * SF) ** 0.5), 0.00061035156, ((0, 32),), jnp.float32)
    square_encoder = jnp.clip(jnp.exp(math.log(3.814697446813398e-09) - 1.3862944 * jax.random.uniform(keys[18], (DEVICES, 2, HID, ENC), jnp.float32) ** shard_levels(keys[18], (DEVICES, 2, HID, ENC), ((0, 32),), -0.2, 0.2)), 9.536743617033494e-10, 3.814697446813398e-09)
    square_middle = jnp.clip(jnp.exp(math.log(3.814697446813398e-09) - 1.3862944 * jax.random.uniform(keys[19], (DEVICES, 2, HID, HID), jnp.float32) ** shard_levels(keys[19], (DEVICES, 2, HID, HID), ((0, 32),), -0.2, 0.2)), 9.536743617033494e-10, 3.814697446813398e-09)
    square_viewer = jnp.clip(jnp.exp(math.log(3.814697446813398e-09) - 1.3862944 * jax.random.uniform(keys[20], (DEVICES, 2, VIEW, HID + DENC), jnp.float32) ** shard_levels(keys[20], (DEVICES, 2, VIEW, HID + DENC), ((0, 32),), -0.2, 0.2)), 9.536743617033494e-10, 3.814697446813398e-09)
    square_colour = jnp.clip(jnp.exp(math.log(3.814697446813398e-09) - 1.3862944 * jax.random.uniform(keys[21], (DEVICES, 2, 3, VIEW), jnp.float32) ** shard_levels(keys[21], (DEVICES, 2, 3, VIEW), ((0, 32),), -0.2, 0.2)), 9.536743617033494e-10, 3.814697446813398e-09)
    square_scalars = jnp.clip(jnp.exp(math.log(3.814697446813398e-09) - 1.3862944 * jax.random.uniform(keys[22], (DEVICES, 2, NSMALL), jnp.float32) ** shard_levels(keys[22], (DEVICES, 2, NSMALL), ((0, 32),), -0.2, 0.2)), 9.536743617033494e-10, 3.814697446813398e-09)
    return dict(camera=camera, ray_mask=ray_mask, ray_direction=ray_direction, anchors=anchors, target=target, fine_levels=fine_levels, density_bins=density_bins, owners=owners, encoder=encoder, middle=middle, viewer=viewer, colour=colour, scalars=scalars, moment_encoder=moment_encoder, moment_middle=moment_middle, moment_viewer=moment_viewer, moment_colour=moment_colour, moment_scalars=moment_scalars, square_encoder=square_encoder, square_middle=square_middle, square_viewer=square_viewer, square_colour=square_colour, square_scalars=square_scalars)


@jax.custom_vjp
def low(v):
    return lax.optimization_barrier(v.astype(jnp.bfloat16)).astype(jnp.float32)

@jax.custom_vjp
def low_back(v):
    return v

def low_keep(v):
    return (low(v), None)

def low_pass(kept, grad):
    return (grad,)

def back_keep(v):
    return (v, None)

def back_low(kept, grad):
    return (low(grad),)
low.defvjp(low_keep, low_pass)
low_back.defvjp(back_keep, back_low)
near_plane = 2.0
far_plane = 6.0
shrink = 0.125
smooth_weight = 0.1
entropy_weight = 0.1
beta_first = 0.9
beta_second = 0.999
adam_epsilon = 1e-08
decay_rate = 0.01
learn_rate = 0.05
step_count = 10

def product(former, latter):
    return jnp.dot(former, latter, precision=lax.Precision.HIGHEST, preferred_element_type=jnp.float32)

def encode(points, levels):
    scales = 2.0 ** jnp.arange(levels, dtype=jnp.float32) * math.pi
    angles = points[None] * scales.reshape((levels,) + (1,) * points.ndim)
    wavesets = jnp.stack([jnp.sin(angles), jnp.cos(angles)], axis=1)
    return jnp.concatenate([points, wavesets.reshape((6 * levels,) + points.shape[1:])], axis=0)

def split_scalars(scalars, hidden, view_width):
    offset = 3 * hidden + 1
    return (scalars[:hidden], scalars[hidden:2 * hidden], scalars[2 * hidden:3 * hidden], scalars[3 * hidden], scalars[offset:offset + view_width], scalars[offset + view_width:])

def composite(density, colours, depths):
    spacing = jnp.concatenate([depths[1:] - depths[:-1], far_plane - depths[-1:]], 0)
    optical = density * spacing
    before = jnp.cumsum(optical, 0) - optical
    weights = jnp.exp(-before) * (1.0 - jnp.exp(-optical))
    return (spacing, optical, before, weights, lax.optimization_barrier(jnp.sum(weights[None] * colours, 1)), lax.optimization_barrier(jnp.sum(weights * depths, 0)), lax.optimization_barrier(jnp.sum(weights, 0)))

def radiance(params, encoded, view_code, samples):
    encoder, middle, viewer, colour, scalars = params
    ray_width = view_code.shape[1]
    bias_one, bias_two, sigma_row, sigma_bias, view_bias, colour_bias = split_scalars(scalars, HID, VIEW)
    pre_one = low_back(product(encoder, encoded) + bias_one[:, None])
    hidden_one = low(jax.nn.relu(pre_one))
    pre_two = low_back(product(middle, hidden_one) + bias_two[:, None])
    hidden_two = low(jax.nn.relu(pre_two))
    pre_sigma = low_back(product(sigma_row[None], hidden_two)[0] + sigma_bias)
    per_ray = product(viewer[:, HID:], view_code)
    pre_view = product(viewer[:, :HID], hidden_two).reshape(VIEW, samples, ray_width) + per_ray[:, None, :] + view_bias[:, None, None]
    pre_view = low_back(pre_view.reshape(VIEW, samples * ray_width))
    view_hidden = low(jax.nn.relu(pre_view))
    pre_colour = low_back(product(colour, view_hidden) + colour_bias[:, None])
    return (jax.nn.softplus(pre_sigma), jax.nn.sigmoid(pre_colour))

def render(params, anchor, direction_row, view_code, depths):
    samples, ray_width = depths.shape
    points = (anchor[:, None, :] + depths[None] * direction_row[:, None, :]) * shrink
    encoded = low(encode(points, LPOS)).reshape(ENC, samples * ray_width)
    density, colours = radiance(params, encoded, view_code, samples)
    density = density.reshape(samples, ray_width)
    parts = composite(density, colours.reshape(3, samples, ray_width), depths)
    return (parts[4], parts[5], parts[6], density)

def adamw_update(weight, moment, square, gradient):
    moment_next = beta_first * moment + (1.0 - beta_first) * gradient
    square_next = beta_second * square + (1.0 - beta_second) * gradient * gradient
    first_hat = moment_next / (1.0 - beta_first ** step_count)
    second_hat = square_next / (1.0 - beta_second ** step_count)
    weight_next = weight - learn_rate * (first_hat / (jnp.sqrt(second_hat) + adam_epsilon) + decay_rate * weight)
    return (weight_next, moment_next, square_next)

def reference(camera, ray_mask, ray_direction, anchors, target, fine_levels, density_bins, owners, encoder, middle, viewer, colour, scalars, moment_encoder, moment_middle, moment_viewer, moment_colour, moment_scalars, square_encoder, square_middle, square_viewer, square_colour, square_scalars):
    masters = (encoder, middle, viewer, colour, scalars)
    moments = (moment_encoder, moment_middle, moment_viewer, moment_colour, moment_scalars)
    squares = (square_encoder, square_middle, square_viewer, square_colour, square_scalars)

    def owner_slots(stacked, group_index):
        return jnp.stack([stacked[owners[group_index, net_index], net_index] for net_index in range(2)])
    chosen = tuple((owner_slots(masters[group_index], group_index) for group_index in range(5)))
    mask_float = ray_mask.astype(jnp.float32)
    mask_floor = jnp.maximum(jnp.sum(mask_float), 1.0)
    camera_count = lax.optimization_barrier(jnp.sum(jnp.where(camera[None] == jnp.arange(NCAM)[:, None, None], mask_float[None], 0.0), axis=(1, 2)))
    inverse = 1.0 / jnp.maximum(camera_count, 1.0)
    ray_weight = inverse[camera] * mask_float / NCAM
    coarse_line = near_plane + (far_plane - near_plane) * (jnp.arange(SC, dtype=jnp.float32) + 0.5) / SC
    coarse_depths = jnp.broadcast_to(coarse_line[:, None], (SC, IMW))
    fine_depths = near_plane + (far_plane - near_plane) * (fine_levels.astype(jnp.float32) + 0.5) / NT
    row_inputs = (camera, jnp.transpose(ray_direction, (1, 0, 2)), jnp.transpose(fine_depths, (1, 0, 2)), jnp.transpose(density_bins, (1, 0, 2)), mask_float)

    def objective(weights_now):
        lowered = tuple((low(member) for member in weights_now))
        coarse_params = tuple((member[0] for member in lowered))
        fine_params = tuple((member[1] for member in lowered))

        def render_row(row_data):
            camera_row, direction_row, fine_row, bucket_row, mask_row = row_data
            anchor = anchors[:, camera_row]
            view_code = low(encode(direction_row, LDIR))
            coarse_out = render(coarse_params, anchor, direction_row, view_code, coarse_depths)
            fine_out = render(fine_params, anchor, direction_row, view_code, fine_row)
            matches = bucket_row[None] == jnp.arange(NHIST)[:, None, None]
            density_row = lax.optimization_barrier(jnp.sum(jnp.where(matches, (fine_out[3] * mask_row[None])[None], 0.0), axis=(1, 2)))
            return coarse_out[:3] + fine_out[:3] + (density_row,)
        results = lax.map(jax.checkpoint(render_row), row_inputs)
        colour_coarse = jnp.transpose(results[0], (1, 0, 2))
        colour_fine = jnp.transpose(results[3], (1, 0, 2))
        depth_fine = results[4]
        opacity_fine = results[5]
        miss_coarse = colour_coarse - target
        miss_fine = colour_fine - target
        loss = jnp.sum(ray_weight * lax.optimization_barrier(jnp.sum(miss_coarse * miss_coarse, 0))) + jnp.sum(ray_weight * lax.optimization_barrier(jnp.sum(miss_fine * miss_fine, 0)))
        values = jnp.concatenate([colour_fine, depth_fine[None]], 0)
        across = values[:, :, 1:] - values[:, :, :-1]
        across_pair = mask_float[:, 1:] * mask_float[:, :-1]
        downward = values[:, 1:] - values[:, :-1]
        down_pair = mask_float[1:] * mask_float[:-1]
        smooth = jnp.sum(across_pair[None] * across * across) + jnp.sum(down_pair[None] * downward * downward)
        opacity = 0.01 + 0.98 * opacity_fine
        entropy = -jnp.sum(mask_float * (opacity * jnp.log(opacity) + (1.0 - opacity) * jnp.log(1.0 - opacity)))
        loss = loss + (smooth_weight * smooth + entropy_weight * entropy) / mask_floor
        histogram = lax.optimization_barrier(jnp.sum(results[6], 0)) / mask_floor
        return (loss, histogram)
    loss, pull, histogram = jax.vjp(objective, chosen, has_aux=True)
    gradients = pull(jnp.ones_like(loss))[0]
    next_list = []
    moment_list = []
    square_list = []
    for group_index in range(5):
        updates = adamw_update(chosen[group_index], owner_slots(moments[group_index], group_index), owner_slots(squares[group_index], group_index), gradients[group_index])
        sources = (masters[group_index], moments[group_index], squares[group_index])
        written = []
        for stacked, updated in zip(sources, updates):
            for net_index in range(2):
                stacked = stacked.at[owners[group_index, net_index], net_index].set(updated[net_index])
            written.append(stacked)
        next_list.append(written[0])
        moment_list.append(written[1])
        square_list.append(written[2])
    return (loss, histogram, next_list[0], next_list[1], next_list[2], next_list[3], next_list[4], moment_list[0], moment_list[1], moment_list[2], moment_list[3], moment_list[4], square_list[0], square_list[1], square_list[2], square_list[3], square_list[4])
```

```python
import functools
import math

import jax
import jax.numpy as jnp
from jax import lax
from jax.experimental import pallas as pl
from jax.experimental.pallas import tpu as pltpu
from jax.sharding import PartitionSpec as P

LPOS = 10
LDIR = 4
SC = 64
NT = 1024
NHIST = 64

near_plane = 2.0
far_plane = 6.0
shrink = 0.125
smooth_weight = 0.1
entropy_weight = 0.1
beta_first = 0.9
beta_second = 0.999
adam_epsilon = 1e-08
decay_rate = 0.01
learn_rate = 0.05
step_count = 10

MESH = pl.DeviceIdType.MESH
F32 = jnp.float32
BF16 = jnp.bfloat16
HIGH = lax.Precision.HIGHEST
GROUP = 8
ROWS = 512
LIMIT = 66_000_000

ROW_M, ROW_V, ROW_S, ROW_E, ROW_D = 0, 256, 384, 400, 464

PI_A = 3.140625
PI_B = 0.0009670257568359375
PI_C = math.pi - PI_A - PI_B
SIN = (-0.16666656732559204, 0.008333015255630016, -0.00019806479394901544, 2.5997517241194146e-06)
COS = (-0.5, 0.04166664183139801, -0.0013888400280848145, 2.4761729946476407e-05, -2.607421833999979e-07)


def dot(a, b, precision=None):
    return lax.dot_general(a, b, (((1,), (0,)), ((), ())), preferred_element_type=F32, precision=precision)


def dot_nt(a, b, precision=None):
    return lax.dot_general(a, b, (((1,), (1,)), ((), ())), preferred_element_type=F32, precision=precision)


def dot_tn(a, b, precision=None):
    return lax.dot_general(a, b, (((0,), (0,)), ((), ())), preferred_element_type=F32, precision=precision)


def iota(shape, axis):
    return lax.broadcasted_iota(jnp.int32, shape, axis)


def sin_cos_twice(y):
    k = jnp.round(y * (1.0 / math.pi))
    y = ((y - k * PI_A) - k * PI_B) - k * PI_C
    t = y * y
    s = y * (1.0 + t * (SIN[0] + t * (SIN[1] + t * (SIN[2] + t * SIN[3]))))
    c = 1.0 + t * (COS[0] + t * (COS[1] + t * (COS[2] + t * (COS[3] + t * COS[4]))))
    d = s + s
    return d * c, 1.0 - d * s


def code_column(row, levels, pad):
    half = row % pad
    third = 3 * levels
    wave = 3 + 6 * (half // 3) + half % 3 + jnp.where(row >= pad, 3, 0)
    if levels == LPOS:
        rest = jnp.where(row == 30, 0, jnp.where(row == 31, 1, jnp.where(row == 62, 2, -1)))
    else:
        rest = jnp.where((row >= 12) & (row < 15), row - 12, jnp.where(row == 28, -1, -2))
    return jnp.where(half < third, wave, rest)


def selector(rows, columns, levels, pad, dtype):
    return (iota((rows, columns), 1) == code_column(iota((rows, columns), 0), levels, pad)).astype(dtype)


def mesh_bits(sizes):
    bits = [("tx", 0)] if sizes["tx"] > 1 else []
    bits += [("ty", b) for b in range(sizes["ty"].bit_length() - 1)]
    bits += [("tx", b) for b in range(1, sizes["tx"].bit_length() - 1)]
    return bits


def partner_of(axis, bit):
    me = lax.axis_index(axis)
    side = (me // (1 << bit)) % 2
    return side, {axis: me + (1 - 2 * side) * (1 << bit)}


def greet(partners):
    barrier = pltpu.get_barrier_semaphore()
    for where in partners:
        pl.semaphore_signal(barrier, inc=1, device_id=where, device_id_type=MESH)
    pl.semaphore_wait(barrier, len(partners))


def all_sum(bits, least, big, arrived, whole, small, small_arrived, sems):
    send, recv, send_small, recv_small = sems
    rows = big.shape[0]
    offset, size, at = 0, rows, 0
    plan = []
    for i, (axis, bit) in enumerate(bits):
        side, where = partner_of(axis, bit)
        tiny = pltpu.make_async_remote_copy(
            small.at[i % 2], small_arrived.at[i], send_small.at[i], recv_small.at[i], device_id=where, device_id_type=MESH
        )
        tiny.start()
        halve = size // 2 >= least
        length = size // 2 if halve else size
        keep = pl.multiple_of(offset + side * length, least) if halve else offset
        give = pl.multiple_of(offset + (1 - side) * length, least) if halve else offset
        copy = pltpu.make_async_remote_copy(
            big.at[pl.ds(give, length)],
            arrived.at[pl.ds(at, length)],
            send.at[i],
            recv.at[i],
            device_id=where,
            device_id_type=MESH,
        )
        copy.start()
        tiny.wait()
        small[(i + 1) % 2] = small[i % 2] + small_arrived[i]
        copy.wait()
        big[pl.ds(keep, length)] = big[pl.ds(keep, length)] + arrived[at : at + length]
        at += length
        if halve:
            plan.append((axis, bit, offset, keep, length))
            offset, size = keep, length
    whole[pl.ds(offset, size)] = big[pl.ds(offset, size)]
    for j, (axis, bit, before, keep, length) in enumerate(reversed(plan)):
        _, where = partner_of(axis, bit)
        copy = pltpu.make_async_remote_copy(
            whole.at[pl.ds(keep, length)],
            whole.at[pl.ds(keep, length)],
            send.at[len(bits) + j],
            recv.at[len(bits) + j],
            device_id=where,
            device_id_type=MESH,
        )
        copy.start()
        copy.wait()


def sum_scratch(bits, rows, dtype):
    n = len(bits)
    return [
        pltpu.VMEM((rows, 256), dtype),
        pltpu.VMEM((2 * rows, 256), dtype),
        pltpu.VMEM((rows, 256), dtype),
        pltpu.VMEM((2, 8, 128), F32),
        pltpu.VMEM((n, 8, 128), F32),
        pltpu.SemaphoreType.DMA((2 * n,)),
        pltpu.SemaphoreType.DMA((2 * n,)),
        pltpu.SemaphoreType.DMA((n,)),
        pltpu.SemaphoreType.DMA((n,)),
    ]


def spread_kernel(bits, tiles_y, owners, rays, encoder, middle, viewer, colour, scalars, out, counts, big, arrived, whole, small, small_arrived, *sems):
    device = lax.axis_index("tx") * tiles_y + lax.axis_index("ty")
    lanes = rays.shape[1]
    choose_e = selector(64, encoder.shape[2], LPOS, 32, BF16)
    choose_d = selector(32, viewer.shape[2] - 256, LDIR, 16, BF16)

    def rounded(group, net, value):
        return jnp.where(owners[group, net] == device, value, 0.0).astype(BF16)

    for net in range(2):
        base = net * ROWS
        big[base + ROW_M : base + ROW_M + 256] = rounded(1, net, middle[net])
        views = rounded(2, net, viewer[net])
        big[base + ROW_V : base + ROW_V + 128] = views[:, :256]
        row = rounded(4, net, scalars[net : net + 1]).astype(F32)
        empty = jnp.zeros((1, 256), F32)
        block = iota((16, 256), 0)
        picked = jnp.where(block == 0, row[:, 512:768], jnp.where(block == 1, row[:, 256:512], empty))
        tail = jnp.concatenate([row[:, 768:], jnp.zeros((1, 124), F32)], 1)
        picked = jnp.where(block == 2, tail, picked)
        big[base + ROW_S : base + ROW_S + 16] = picked.astype(BF16)
        first = dot_nt(choose_e, rounded(0, net, encoder[net]))
        first = jnp.where(iota((64, 256), 0) == 63, row[:, :256], first)
        big[base + ROW_E : base + ROW_E + 64] = first.astype(BF16)
        views_d = dot_nt(choose_d, views[:, 256:])
        paint = jnp.concatenate([rounded(3, net, colour[net]).astype(F32), jnp.zeros((29, 128), F32)], 0)
        big[base + ROW_D : base + ROW_D + 32, 0:128] = views_d.astype(BF16)
        big[base + ROW_D : base + ROW_D + 32, 128:256] = paint.astype(BF16)
        big[base + ROW_D + 32 : base + ROWS] = jnp.zeros((ROWS - ROW_D - 32, 256), BF16)
    camera, mask = rays[7:8], rays[6:7]
    picks = (camera == iota((128, lanes), 0).astype(F32)) | (iota((128, lanes), 0) == 127)
    small[0] = dot_nt(jnp.broadcast_to(mask, (8, lanes)).astype(BF16), picks.astype(BF16))
    greet([partner_of(axis, bit)[1] for axis, bit in bits])
    all_sum(bits, 16, big, arrived, whole, small, small_arrived, sems)
    out[...] = whole[...]
    counts[...] = small[len(bits) % 2]


def total_kernel(bits, grads, stats, out, sums, big, arrived, whole, small, small_arrived, *sems):
    big[...] = grads[...]
    small[0] = stats[...]
    greet([partner_of(axis, bit)[1] for axis, bit in bits])
    all_sum(bits, 8, big, arrived, whole, small, small_arrived, sems)
    out[...] = whole[...]
    sums[...] = small[len(bits) % 2]


def running(block):
    row = iota(block.shape, 0)
    for shift in (1, 2, 4):
        block = block + jnp.where(row >= shift, pltpu.roll(block, shift, 0), 0.0)
    return block


def running_back(block):
    row = iota(block.shape, 0)
    for shift in (1, 2, 4):
        block = block + jnp.where(row < 8 - shift, pltpu.roll(block, 8 - shift, 0), 0.0)
    return block


def total(block):
    return jnp.sum(block, 0, keepdims=True)


def rays_kernel(
    sizes, tile, cameras, levels, bins, rays, spread, anchors, params, counts, grads, stats,
    enc, h1, h2, hv, raw, tints, depth, weight, passed, back, hist, w_e, w_m, w_mt, w_v, w_vt, w_c, w_ct, bias, per_ray,
    g_e, g_m, g_v, g_c, g_r, mine, halo, send, recv,
):
    lanes = rays.shape[1]
    points = GROUP * lanes
    tile_rows, tile_cols = tile
    tx, ty = lax.axis_index("tx"), lax.axis_index("ty")
    sides = (
        ({"tx": tx - 1}, tx > 0),
        ({"tx": tx + 1}, tx < sizes["tx"] - 1),
        ({"ty": ty - 1}, ty > 0),
        ({"ty": ty + 1}, ty < sizes["ty"] - 1),
    )
    barrier = pltpu.get_barrier_semaphore()
    expected = 0
    for where, there in sides:
        expected = expected + there.astype(jnp.int32)

        @pl.when(there)
        def _(where=where):
            pl.semaphore_signal(barrier, inc=1, device_id=where, device_id_type=MESH)

    pl.semaphore_wait(barrier, expected)

    camera, mask = rays[7:8], rays[6:7]
    picks = (camera == iota((128, lanes), 0).astype(F32)).astype(F32)
    origin = dot(anchors[...], picks, HIGH)
    heading = spread[...]
    o_main, d_main = origin[:32], heading[:32]
    row8 = iota((8, lanes), 0)
    o_last, d_last = jnp.where(row8 == 7, 1.0 / shrink, origin[32:]), heading[32:]
    row32 = iota((32, lanes), 0)
    half_pi = jnp.float32(math.pi) * 0.5
    scale = jnp.zeros((32, lanes), F32)
    for level in range(LPOS):
        scale = jnp.where((row32 >= 3 * level) & (row32 < 3 * level + 3), half_pi * (2.0**level), scale)

    row16 = iota((16, lanes), 0)
    scale_d = jnp.zeros((16, lanes), F32)
    for level in range(LDIR):
        scale_d = jnp.where((row16 >= 3 * level) & (row16 < 3 * level + 3), half_pi * (2.0**level), scale_d)
    sin_d, cos_d = sin_cos_twice(d_main[:16] * scale_d)
    top = jnp.where(row16 >= 12, jnp.where(row16 < 15, d_main[:16], 0.0), sin_d)
    bottom = jnp.where(row16 >= 12, jnp.where(row16 == 12, 1.0, 0.0), cos_d)
    view_code = jnp.concatenate([top, bottom], 0).astype(BF16)

    count = counts[...]
    mask_floor = jnp.maximum(count[0:1, 127:128], 1.0)
    inverse = 1.0 / jnp.maximum(count, 1.0)
    ray_weight = dot(inverse, picks, HIGH)[0:1] * mask / cameras
    target = rays[3:6]
    ones = jnp.full((16, points), 1.0, BF16)
    stats[...] = jnp.zeros_like(stats)
    loss = jnp.zeros((1, lanes), F32)

    for net, samples in ((0, SC), (1, levels.shape[0])):
        blocks = samples // GROUP
        base = net * ROWS
        middle = params[base + ROW_M : base + ROW_M + 256]
        w_m[...] = middle
        w_mt[...] = middle.astype(F32).T.astype(BF16)
        misc = params[base + ROW_S : base + ROW_S + 16]
        row = iota((16, 256), 0)
        misc32 = misc.astype(F32)
        sigma = jnp.where(row == 0, misc32, 0.0)
        w_v[0:128] = params[base + ROW_V : base + ROW_V + 128]
        w_v[128:144] = sigma.astype(BF16)
        views_t = params[base + ROW_V : base + ROW_V + 128].astype(F32).T
        w_vt[:, 0:128] = views_t.astype(BF16)
        sigma_t = jnp.concatenate([jnp.zeros((3, 256), F32), misc32[0:1], jnp.zeros((124, 256), F32)], 0).T
        w_vt[:, 128:144] = sigma_t[:, :16].astype(BF16)
        w_e[...] = params[base + ROW_E : base + ROW_E + 64].astype(F32).T.astype(BF16)
        last = params[base + ROW_D : base + ROW_D + 32].astype(F32)
        paint = last[:16, 128:]
        tail = misc32[2:3]
        sigma_bias = tail[:, 0:1]
        lane = iota((16, 128), 1)
        row_c = iota((16, 128), 0)
        tint_bias = jnp.zeros((16, 128), F32)
        for k in range(3):
            tint_bias = jnp.where((row_c == k) & (lane == 0), tail[:, 129 + k : 130 + k], tint_bias)
        w_c[:, 0:128] = paint.astype(BF16)
        w_c[:, 128:144] = tint_bias[:, :16].astype(BF16)
        w_ct[...] = jnp.concatenate([paint, jnp.zeros((112, 128), F32)], 0).T[:, :16].astype(BF16)
        bias[...] = jnp.broadcast_to(misc32[1:2], (128, 256)).T
        views_d = last[:, :128]
        shifted = pltpu.roll(jnp.broadcast_to(tail, (8, 256)), 255, 1)[0:1, :128]
        views_d = jnp.where(iota((32, 128), 0) == 28, shifted, views_d)
        per_ray[...] = dot_tn(views_d.astype(BF16), view_code)

        if net == 0:
            for b in range(blocks):
                at = (row8 + b * GROUP).astype(F32)
                depth[b] = near_plane + (far_plane - near_plane) * (at + 0.5) / SC
        else:
            for b in range(blocks):
                at = levels[b * GROUP : b * GROUP + GROUP].astype(F32)
                depth[b] = near_plane + (far_plane - near_plane) * (at + 0.5) / NT

        def encode(c):
            for s in range(GROUP):
                t = depth[c, s : s + 1]
                place = (o_main + t * d_main) * shrink
                wave, cowave = sin_cos_twice(place * scale)
                wave = jnp.where(row32 >= 30, place, wave)
                extra = (o_last + t * d_last) * shrink
                end = jnp.where(row8 >= 6, extra, cowave[24:])
                cowave = jnp.concatenate([cowave[:24], end], 0)
                enc[c, 0:32, s * lanes : s * lanes + lanes] = wave.astype(BF16)
                enc[c, 32:64, s * lanes : s * lanes + lanes] = cowave.astype(BF16)

        def forward(c, carry):
            one = jnp.maximum(dot(w_e[...], enc[c]).astype(BF16), 0)
            h1[c] = one
            two = dot(w_m[...], one) + jnp.tile(bias[...], (1, points // 128))
            two = jnp.maximum(two.astype(BF16), 0)
            h2[c] = two
            out = dot(w_v[...], two)
            view = out[:128] + jnp.tile(per_ray[...], (1, GROUP))
            view = jnp.maximum(view.astype(BF16), 0)
            hv[c] = view
            paint = dot(w_c[...], jnp.concatenate([view, ones], 0))
            for s in range(GROUP):
                part = slice(s * lanes, s * lanes + lanes)
                for k in range(3):
                    raw[k, c, s : s + 1] = paint[k : k + 1, part]
                raw[3, c, s : s + 1] = out[128:129, part]
            encode(jnp.minimum(c + 1, blocks - 1))
            return carry

        encode(0)
        lax.fori_loop(0, blocks, forward, 0)

        before = jnp.zeros((1, lanes), F32)
        colour = [jnp.zeros((8, lanes), F32) for _ in range(3)]
        far, opaque = jnp.zeros((8, lanes), F32), jnp.zeros((8, lanes), F32)

        def spacing(b):
            t = depth[b]
            after = depth[b + 1, 0:1] if b + 1 < blocks else jnp.full((1, lanes), far_plane, F32)
            return jnp.where(row8 == 7, after, pltpu.roll(t, 7, 0)) - t

        for b in range(blocks):
            zs = raw[3, b] + sigma_bias
            density = jnp.maximum(zs, 0.0) + jnp.log1p(jnp.exp(-jnp.abs(zs)))
            q = density * spacing(b)
            inclusive = running(q) + before
            before = inclusive[7:8]
            lit = jnp.exp(-(inclusive - q))
            w = lit * (1.0 - jnp.exp(-q))
            weight[b] = w
            passed[b] = jnp.exp(-inclusive)
            if net == 1:
                back[3, b] = density * mask
            for k in range(3):
                tint = jax.nn.sigmoid(raw[k, b])
                tints[k, b] = tint
                colour[k] = colour[k] + w * tint
            far = far + w * depth[b]
            opaque = opaque + w
        colour = [total(x) for x in colour]
        far, opaque = total(far), total(opaque)
        miss = [colour[k] - target[k : k + 1] for k in range(3)]
        loss = loss + ray_weight * (miss[0] * miss[0] + miss[1] * miss[1] + miss[2] * miss[2])
        seed = [2.0 * ray_weight * miss[k] for k in range(3)]
        seed_depth = seed_opaque = None
        if net == 1:
            for k in range(3):
                mine[k : k + 1] = colour[k]
            mine[3:4] = far
            mine[4:5] = mask
            mine[5:8] = jnp.zeros((3, lanes), F32)
            for i, (where, there) in enumerate(sides):

                @pl.when(there)
                def _(i=i, where=where):
                    pltpu.make_async_remote_copy(
                        mine, halo.at[i], send.at[i], recv.at[i], device_id=where, device_id_type=MESH
                    ).start()

            def count_bin(b, carry):
                sums = jnp.zeros((8, lanes), F32)
                for s in range(blocks):
                    sums = sums + jnp.where(bins[s * GROUP : s * GROUP + GROUP] == b, back[3, s], 0.0)
                hist[b] = sums
                return carry

            lax.fori_loop(0, NHIST, count_bin, 0)
            sums = jnp.sum(hist[...], 1)
            stats[0:1, 0:NHIST] = dot_nt(jnp.full((8, lanes), 1.0, F32), sums, HIGH)[0:1]
            solid = 0.01 + 0.98 * opaque
            entropy = -mask * (solid * jnp.log(solid) + (1.0 - solid) * jnp.log(1.0 - solid))
            seed_opaque = -(entropy_weight / mask_floor) * mask * 0.98 * (jnp.log(solid) - jnp.log(1.0 - solid))
            for i, (where, there) in enumerate(sides):
                j = i ^ 1

                @pl.when(there)
                def _(i=i, j=j, where=where):
                    pltpu.make_async_remote_copy(
                        mine, halo.at[i], send.at[i], recv.at[i], device_id=where, device_id_type=MESH
                    ).wait_send()
                    pltpu.make_async_remote_copy(
                        mine, halo.at[j], send.at[i], recv.at[j], device_id=where, device_id_type=MESH
                    ).wait_recv()

            values = mine[...]
            lane = iota((8, lanes), 1)
            col, tile_row = lane % tile_cols, lane // tile_cols

            def beside(i, inner, shift, wrap):
                other = jnp.where(
                    inner, pltpu.roll(values, shift % lanes, 1), pltpu.roll(halo[i ^ 1], wrap % lanes, 1)
                )
                known = inner | sides[i][1]
                return jnp.where(known, other, 0.0)

            smooth = jnp.zeros((8, lanes), F32)
            pull = jnp.zeros((8, lanes), F32)
            for i, inner, shift, wrap in (
                (0, col > 0, 1, 1 - tile_cols),
                (1, col < tile_cols - 1, -1, tile_cols - 1),
                (2, tile_row > 0, tile_cols, tile_cols - lanes),
                (3, tile_row < tile_rows - 1, -tile_cols, lanes - tile_cols),
            ):
                other = beside(i, inner, shift, wrap)
                pair = other[4:5] * mask
                gap = jnp.where(row8 < 4, values - other, 0.0)
                pull = pull + pair * gap
                if i % 2 == 1:
                    smooth = smooth + pair * gap * gap
            smooth_scale = 2.0 * smooth_weight / mask_floor
            pull = smooth_scale * pull
            seed = [seed[k] + pull[k : k + 1] for k in range(3)]
            seed_depth = pull[3:4]
            loss = loss + (smooth_weight * total(smooth) + entropy_weight * entropy) / mask_floor

        later = jnp.zeros((1, lanes), F32)
        for b in reversed(range(blocks)):
            w = weight[b]
            tint = [tints[k, b] for k in range(3)]
            pulled = seed[0] * tint[0] + seed[1] * tint[1] + seed[2] * tint[2]
            if net == 1:
                pulled = pulled + seed_depth * depth[b] + seed_opaque
            weighted = pulled * w
            onward = running_back(weighted) + later
            later = onward[0:1]
            dq = pulled * passed[b] - (onward - weighted)
            zs = raw[3, b] + sigma_bias
            back[3, b] = dq * spacing(b) * jax.nn.sigmoid(zs)
            for k in range(3):
                back[k, b] = w * seed[k] * tint[k] * (1.0 - tint[k])

        g_e[...] = jnp.zeros_like(g_e)
        g_m[...] = jnp.zeros_like(g_m)
        g_v[...] = jnp.zeros_like(g_v)
        g_c[...] = jnp.zeros_like(g_c)
        g_r[...] = jnp.zeros_like(g_r)

        def backward(c, carry):
            parts = []
            for s in range(GROUP):
                parts.append(jnp.concatenate([back[k, c, s : s + 1] for k in range(4)] + [jnp.zeros((12, lanes), F32)], 0))
            gate = jnp.concatenate(parts, 1).astype(BF16)
            view = hv[c]
            gv = jnp.where(view > 0, dot(w_ct[...], gate).astype(BF16), 0)
            sums = g_r[...]
            for s in range(GROUP):
                sums = sums + gv[:, s * lanes : s * lanes + lanes].astype(F32)
            g_r[...] = sums
            g_c[...] += dot_nt(gate, jnp.concatenate([view, ones], 0))
            both = jnp.concatenate([gv, gate], 0)
            two = h2[c]
            g_v[...] += dot_nt(both, two)
            g2 = jnp.where(two > 0, dot(w_vt[...], both).astype(BF16), 0)
            one = h1[c]
            g_m[...] += dot_nt(jnp.concatenate([one, ones], 0), g2)
            g1 = jnp.where(one > 0, dot(w_mt[...], g2).astype(BF16), 0)
            g_e[...] += dot_nt(enc[c], g1)
            return carry

        lax.fori_loop(0, blocks, backward, 0)

        grads[base + ROW_M : base + ROW_M + 256] = g_m[0:256]
        grads[base + ROW_V : base + ROW_V + 128] = g_v[0:128]
        row = iota((16, 256), 0)
        lane = iota((16, 256), 1)
        grad_misc = jnp.where(row == 0, g_v[131:132], jnp.where(row == 1, g_m[256:257], 0.0))
        sums_c = g_c[:, 128:129]
        for k, spot in ((3, 0), (0, 129), (1, 130), (2, 131)):
            grad_misc = jnp.where((row == 2) & (lane == spot), sums_c[k : k + 1], grad_misc)
        grads[base + ROW_S : base + ROW_S + 16] = grad_misc
        grads[base + ROW_E : base + ROW_E + 64] = g_e[...]
        grads[base + ROW_D : base + ROW_D + 32, 0:128] = dot_nt(view_code.astype(F32), g_r[...], HIGH)
        grads[base + ROW_D : base + ROW_D + 32, 128:256] = jnp.concatenate([g_c[:, :128], jnp.zeros((16, 128), F32)], 0)
        grads[base + ROW_D + 32 : base + ROWS] = jnp.zeros((ROWS - ROW_D - 32, 256), F32)
    fold = loss[:, :128]
    for k in range(1, lanes // 128):
        fold = fold + loss[:, k * 128 : k * 128 + 128]
    stats[1:2] = fold


def adamw_update(weight, moment, square, gradient):
    moment_next = beta_first * moment + (1.0 - beta_first) * gradient
    square_next = beta_second * square + (1.0 - beta_second) * gradient * gradient
    first_hat = moment_next / (1.0 - beta_first**step_count)
    second_hat = square_next / (1.0 - beta_second**step_count)
    weight_next = weight - learn_rate * (
        first_hat / (jnp.sqrt(second_hat) + adam_epsilon) + decay_rate * weight
    )
    return (weight_next, moment_next, square_next)


def update_kernel(tiles_y, owners, grads, stats, counts, *refs):
    masters, moments, squares = refs[0:5], refs[5:10], refs[10:15]
    loss, histogram = refs[15], refs[16]
    nexts, next_moments, next_squares = refs[17:22], refs[22:27], refs[27:32]
    device = lax.axis_index("tx") * tiles_y + lax.axis_index("ty")
    mask_floor = jnp.maximum(counts[0:1, 127:128], 1.0)
    histogram[...] = stats[0:1] / mask_floor
    loss[...] = jnp.sum(stats[1:2], 1, keepdims=True)
    choose_e = selector(64, masters[0].shape[2], LPOS, 32, F32)
    choose_d = selector(32, masters[2].shape[2] - 256, LDIR, 16, F32)

    def step(group, net, at, gradient):
        owned = owners[group, net] == device
        old = [ref[at] for ref in (masters[group], moments[group], squares[group])]
        new = adamw_update(*old, gradient)
        for ref, was, now in zip((nexts[group], next_moments[group], next_squares[group]), old, new):
            ref[at] = jnp.where(owned, now, was)

    for net in range(2):
        base = net * ROWS
        step(0, net, (net,), dot_tn(grads[base + ROW_E : base + ROW_E + 64], choose_e, HIGH))
        step(1, net, (net,), grads[base + ROW_M : base + ROW_M + 256].T)
        step(2, net, (net, slice(None), slice(0, 256)), grads[base + ROW_V : base + ROW_V + 128])
        last = grads[base + ROW_D : base + ROW_D + 32]
        step(2, net, (net, slice(None), slice(256, 283)), dot_tn(last[:, :128], choose_d, HIGH))
        step(3, net, (net,), last[0:3, 128:])
        misc = grads[base + ROW_S : base + ROW_S + 16]
        spot = slice(net, net + 1)
        step(4, net, (spot, slice(0, 256)), grads[base + ROW_E + 63 : base + ROW_E + 64])
        step(4, net, (spot, slice(256, 512)), misc[1:2])
        step(4, net, (spot, slice(512, 768)), misc[0:1])
        views = jnp.concatenate([last[28:29, :128], jnp.zeros((1, 128), F32)], 1)
        views = pltpu.roll(jnp.broadcast_to(views, (8, 256)), 1, 1)[0:1]
        step(4, net, (spot, slice(768, 900)), (misc[2:3] + views)[:, :132])


VMEM_SPEC = pl.BlockSpec(memory_space=pltpu.VMEM)
SMEM_SPEC = pl.BlockSpec(memory_space=pltpu.SMEM)


def per_device(sizes, camera, ray_mask, ray_direction, anchors, target, fine_levels, density_bins, owners, *trees):
    masters = [x[0] for x in trees[0:5]]
    moments = [x[0] for x in trees[5:10]]
    squares = [x[0] for x in trees[10:15]]
    tile = camera.shape
    lanes = tile[0] * tile[1]
    cameras = anchors.shape[1]
    samples = fine_levels.shape[0]
    bits = mesh_bits(sizes)
    levels = fine_levels.reshape(samples, lanes)
    bins = density_bins.reshape(samples, lanes)
    direction = ray_direction.reshape(3, lanes)
    rays = jnp.concatenate(
        [
            direction,
            target.reshape(3, lanes),
            ray_mask.reshape(1, lanes).astype(F32),
            camera.reshape(1, lanes).astype(F32),
        ],
        0,
    )

    def widened(rows):
        tall = jnp.concatenate([rows] * 11, 0)[:32]
        gap = jnp.zeros((6,) + rows.shape[1:], F32)
        return jnp.concatenate([tall, gap, rows[2:3], gap[:1]], 0)

    heading = widened(direction)
    centres = jnp.pad(widened(anchors), ((0, 0), (0, 128 - cameras)))

    params, counts = pl.pallas_call(
        functools.partial(spread_kernel, bits, sizes["ty"]),
        out_shape=(jax.ShapeDtypeStruct((2 * ROWS, 256), BF16), jax.ShapeDtypeStruct((8, 128), F32)),
        in_specs=[SMEM_SPEC] + [VMEM_SPEC] * 6,
        out_specs=(VMEM_SPEC, VMEM_SPEC),
        scratch_shapes=sum_scratch(bits, 2 * ROWS, BF16),
        compiler_params=pltpu.CompilerParams(collective_id=0, has_side_effects=True),
        name="spread",
    )(owners, rays, *masters)

    points = GROUP * lanes
    blocks = samples // GROUP
    grads, stats = pl.pallas_call(
        functools.partial(rays_kernel, sizes, tile, cameras),
        out_shape=(jax.ShapeDtypeStruct((2 * ROWS, 256), F32), jax.ShapeDtypeStruct((8, 128), F32)),
        in_specs=[VMEM_SPEC] * 7,
        out_specs=(VMEM_SPEC, VMEM_SPEC),
        scratch_shapes=[
            pltpu.VMEM((blocks, 64, points), BF16),
            pltpu.VMEM((blocks, 256, points), BF16),
            pltpu.VMEM((blocks, 256, points), BF16),
            pltpu.VMEM((blocks, 128, points), BF16),
            pltpu.VMEM((4, blocks, GROUP, lanes), F32),
            pltpu.VMEM((3, blocks, GROUP, lanes), F32),
            pltpu.VMEM((blocks, GROUP, lanes), F32),
            pltpu.VMEM((blocks, GROUP, lanes), F32),
            pltpu.VMEM((blocks, GROUP, lanes), F32),
            pltpu.VMEM((4, blocks, GROUP, lanes), F32),
            pltpu.VMEM((NHIST, 8, lanes), F32),
            pltpu.VMEM((256, 64), BF16),
            pltpu.VMEM((256, 256), BF16),
            pltpu.VMEM((256, 256), BF16),
            pltpu.VMEM((144, 256), BF16),
            pltpu.VMEM((256, 144), BF16),
            pltpu.VMEM((16, 144), BF16),
            pltpu.VMEM((128, 16), BF16),
            pltpu.VMEM((256, 128), F32),
            pltpu.VMEM((128, lanes), F32),
            pltpu.VMEM((64, 256), F32),
            pltpu.VMEM((272, 256), F32),
            pltpu.VMEM((144, 256), F32),
            pltpu.VMEM((16, 144), F32),
            pltpu.VMEM((128, lanes), F32),
            pltpu.VMEM((8, lanes), F32),
            pltpu.VMEM((4, 8, lanes), F32),
            pltpu.SemaphoreType.DMA((4,)),
            pltpu.SemaphoreType.DMA((4,)),
        ],
        compiler_params=pltpu.CompilerParams(collective_id=1, has_side_effects=True, vmem_limit_bytes=LIMIT),
        name="rays",
    )(levels, bins, rays, heading, centres, params, counts)

    grads, stats = pl.pallas_call(
        functools.partial(total_kernel, bits),
        out_shape=(jax.ShapeDtypeStruct((2 * ROWS, 256), F32), jax.ShapeDtypeStruct((8, 128), F32)),
        in_specs=[VMEM_SPEC] * 2,
        out_specs=(VMEM_SPEC, VMEM_SPEC),
        scratch_shapes=sum_scratch(bits, 2 * ROWS, F32),
        compiler_params=pltpu.CompilerParams(collective_id=2, has_side_effects=True),
        name="total",
    )(grads, stats)

    states = masters + moments + squares
    results = pl.pallas_call(
        functools.partial(update_kernel, sizes["ty"]),
        out_shape=[jax.ShapeDtypeStruct((1, 1), F32), jax.ShapeDtypeStruct((1, 128), F32)]
        + [jax.ShapeDtypeStruct(x.shape, F32) for x in states],
        in_specs=[SMEM_SPEC] + [VMEM_SPEC] * 18,
        out_specs=[VMEM_SPEC] * 17,
        name="update",
    )(owners, grads, stats, counts, *states)
    return (results[0][0, 0], results[1][0, :NHIST]) + tuple(x[None] for x in results[2:])


def solution(mesh):
    sizes = dict(mesh.shape)
    tiled, tiled3 = P("ty", "tx"), P(None, "ty", "tx")
    slots = P(("tx", "ty"), None, None, None)
    trees = (slots, slots, slots, slots, P(("tx", "ty"), None, None))
    return jax.shard_map(
        functools.partial(per_device, sizes),
        mesh=mesh,
        in_specs=(tiled, tiled, tiled3, P(), tiled3, tiled3, tiled3, P()) + trees * 3,
        out_specs=(P(), P()) + trees * 3,
        check_vma=False,
    )
```

```python
import functools
import math

import jax
import jax.numpy as jnp
from jax import lax
from jax.experimental import pallas as pl
from jax.experimental.pallas import tpu as pltpu
from jax.sharding import PartitionSpec as P

LPOS = 10
LDIR = 4
SC = 64
NT = 1024
NHIST = 64

near_plane = 2.0
far_plane = 6.0
shrink = 0.125
smooth_weight = 0.1
entropy_weight = 0.1
beta_first = 0.9
beta_second = 0.999
adam_epsilon = 1e-08
decay_rate = 0.01
learn_rate = 0.05
step_count = 10

MESH = pl.DeviceIdType.MESH
F32 = jnp.float32
BF16 = jnp.bfloat16
HIGH = lax.Precision.HIGHEST
GROUP = 8
CHUNK = 8
ROWS = 512
LIMIT = 66_000_000

ROW_M, ROW_V, ROW_S, ROW_E, ROW_D = 0, 256, 384, 400, 464

PI_A = 3.140625
PI_B = 0.0009670257568359375
PI_C = math.pi - PI_A - PI_B
SIN = (-0.16666656732559204, 0.008333015255630016, -0.00019806479394901544, 2.5997517241194146e-06)
COS = (-0.5, 0.04166664183139801, -0.0013888400280848145, 2.4761729946476407e-05, -2.607421833999979e-07)


def dot(a, b, precision=None):
    return lax.dot_general(a, b, (((1,), (0,)), ((), ())), preferred_element_type=F32, precision=precision)


def dot_nt(a, b, precision=None):
    return lax.dot_general(a, b, (((1,), (1,)), ((), ())), preferred_element_type=F32, precision=precision)


def dot_tn(a, b, precision=None):
    return lax.dot_general(a, b, (((0,), (0,)), ((), ())), preferred_element_type=F32, precision=precision)


def iota(shape, axis):
    return lax.broadcasted_iota(jnp.int32, shape, axis)


def sin_cos_twice(y):
    k = jnp.round(y * (1.0 / math.pi))
    y = ((y - k * PI_A) - k * PI_B) - k * PI_C
    t = y * y
    s = y * (1.0 + t * (SIN[0] + t * (SIN[1] + t * (SIN[2] + t * SIN[3]))))
    c = 1.0 + t * (COS[0] + t * (COS[1] + t * (COS[2] + t * (COS[3] + t * COS[4]))))
    d = s + s
    return d * c, 1.0 - d * s


def code_column(row, levels, pad):
    half = row % pad
    third = 3 * levels
    wave = 3 + 6 * (half // 3) + half % 3 + jnp.where(row >= pad, 3, 0)
    if levels == LPOS:
        rest = jnp.where(row == 30, 0, jnp.where(row == 31, 1, jnp.where(row == 62, 2, -1)))
    else:
        rest = jnp.where((row >= 12) & (row < 15), row - 12, jnp.where(row == 28, -1, -2))
    return jnp.where(half < third, wave, rest)


def selector(rows, columns, levels, pad, dtype):
    return (iota((rows, columns), 1) == code_column(iota((rows, columns), 0), levels, pad)).astype(dtype)


class Members:
    def __init__(self, axis, count, spread):
        self.axis, self.count, self.spread = axis, count, spread

    def place(self):
        return (lax.axis_index(self.axis) // self.spread) % self.count

    def peer(self, step):
        me = self.place()
        other = (me + step) % self.count
        return other, {self.axis: lax.axis_index(self.axis) + (other - me) * self.spread}


def groups_of(sizes):
    cores = 2 if sizes["tx"] % 2 == 0 else 1
    groups = [Members("tx", cores, 1), Members("ty", sizes["ty"], 1), Members("tx", sizes["tx"] // cores, cores)]
    return [g for g in groups if g.count > 1]


def plan_of(groups, rows, least):
    plan = []
    for group in groups:
        after = rows // group.count if rows % (group.count * least) == 0 else rows
        plan.append((group, rows, after))
        rows = after
    return plan


def sum_scratch(plan, dtype, width=256):
    copies = sum(group.count - 1 for group, _, _ in plan)
    rows = plan[0][1]
    return (
        [pltpu.VMEM((rows, width), dtype), pltpu.VMEM((rows, width), dtype)]
        + [pltpu.VMEM((group.count, after, width), dtype) for group, _, after in plan]
        + [pltpu.VMEM((after, width), dtype) for _, _, after in plan]
        + [pltpu.SemaphoreType.DMA((2 * copies,)), pltpu.SemaphoreType.DMA((2 * copies,))]
    )


class Sum:
    def __init__(self, plan, least, refs):
        n = len(plan)
        self.plan, self.least = plan, least
        self.source, self.whole = refs[0], refs[1]
        self.landing, self.part = refs[2 : 2 + n], refs[2 + n : 2 + 2 * n]
        self.send, self.recv = refs[2 + 2 * n :]
        self.steps = 2 * n + 1

    def rows_at(self, start, length):
        return pl.ds(pl.multiple_of(start, self.least), length)

    def offsets(self):
        at, result = 0, [0]
        for group, before, after in self.plan:
            if after != before:
                at = at + group.place() * after
            result.append(at)
        return result

    def base(self, stage, back):
        copies = [group.count - 1 for group, _, _ in self.plan]
        return sum(copies[:stage]) + (sum(copies) if back else 0)

    def scatter(self, stage):
        group, before, after = self.plan[stage]
        held = self.source if stage == 0 else self.part[stage - 1]
        copies = []
        for step in range(1, group.count):
            other, where = group.peer(step)
            k = self.base(stage, False) + step - 1
            piece = held if after == before else held.at[self.rows_at(other * after, after)]
            copies.append(
                pltpu.make_async_remote_copy(
                    piece,
                    self.landing[stage].at[group.place()],
                    self.send.at[k],
                    self.recv.at[k],
                    device_id=where,
                    device_id_type=MESH,
                )
            )
        return copies

    def gather(self, stage):
        group, before, after = self.plan[stage]
        if after == before:
            return []
        mine = self.rows_at(self.offsets()[stage + 1], after)
        copies = []
        for step in range(1, group.count):
            _, where = group.peer(step)
            k = self.base(stage, True) + step - 1
            copies.append(
                pltpu.make_async_remote_copy(
                    self.whole.at[mine],
                    self.whole.at[mine],
                    self.send.at[k],
                    self.recv.at[k],
                    device_id=where,
                    device_id_type=MESH,
                )
            )
        return copies

    def step(self, k):
        n = len(self.plan)
        if 0 < k <= n:
            stage = k - 1
            group, before, after = self.plan[stage]
            held = self.source if stage == 0 else self.part[stage - 1]
            for copy in self.scatter(stage):
                copy.wait()
            own = held[...] if after == before else held[self.rows_at(group.place() * after, after)]
            self.landing[stage][group.place()] = own
            total = self.landing[stage][0]
            for j in range(1, group.count):
                total = total + self.landing[stage][j]
            self.part[stage][...] = total
            if stage == n - 1:
                self.whole[self.rows_at(self.offsets()[n], after)] = total
        elif k > n:
            for copy in self.gather(2 * n - k):
                copy.wait()
        if k < n:
            for copy in self.scatter(k):
                copy.start()
        elif k < 2 * n:
            for copy in self.gather(2 * n - 1 - k):
                copy.start()


def greet(groups, sides):
    barrier = pltpu.get_barrier_semaphore()
    expected = 0
    for group in groups:
        for step in range(1, group.count):
            pl.semaphore_signal(barrier, inc=1, device_id=group.peer(step)[1], device_id_type=MESH)
            expected = expected + 1
    for where, there in sides:
        expected = expected + there.astype(jnp.int32)

        @pl.when(there)
        def _(where=where):
            pl.semaphore_signal(barrier, inc=1, device_id=where, device_id_type=MESH)

    pl.semaphore_wait(barrier, expected)


def running(block):
    row = iota(block.shape, 0)
    for shift in (1, 2, 4):
        block = block + jnp.where(row >= shift, pltpu.roll(block, shift, 0), 0.0)
    return block


def running_back(block):
    row = iota(block.shape, 0)
    for shift in (1, 2, 4):
        block = block + jnp.where(row < 8 - shift, pltpu.roll(block, 8 - shift, 0), 0.0)
    return block


def total(block):
    return jnp.sum(block, 0, keepdims=True)


def pack(owned, net, choose_e, choose_d, big, encoder, middle, viewer, colour, scalars):
    def rounded(group, value):
        return jnp.where(owned[group], value, 0.0).astype(BF16)

    big[ROW_M : ROW_M + 256] = rounded(1, middle[net])
    views = rounded(2, viewer[:, net, :])
    big[ROW_V : ROW_V + 128, 0:128] = views[0:128]
    big[ROW_V : ROW_V + 128, 128:256] = views[128:256]
    row = rounded(4, scalars[net : net + 1]).astype(F32)
    block = iota((16, 256), 0)
    tail = jnp.concatenate([row[:, 768:], jnp.zeros((1, 124), F32)], 1)
    picked = jnp.where(block == 0, row[:, 512:768], jnp.where(block == 1, row[:, 256:512], 0.0))
    big[ROW_S : ROW_S + 16] = jnp.where(block == 2, tail, picked).astype(BF16)
    first = dot(choose_e, rounded(0, encoder[:, net, :]))
    first = jnp.where(iota((64, 256), 0) == 63, row[:, :256], first)
    big[ROW_E : ROW_E + 64] = first.astype(BF16)
    big[ROW_D : ROW_D + 32, 0:128] = dot(choose_d, views[256:]).astype(BF16)
    paint = jnp.concatenate([rounded(3, colour[:, net, :]).astype(F32), jnp.zeros((29, 128), F32)], 0)
    big[ROW_D : ROW_D + 32, 128:256] = paint.astype(BF16)
    big[ROW_D + 32 : ROWS] = jnp.zeros((ROWS - ROW_D - 32, 256), BF16)


def step_kernel(
    sizes, groups, plans, owners, camera, ray_mask, direction, target, levels, bins, anchors,
    encoder, middle, viewer, colour, scalars, result,
    enc, h1, h2, hv, raw, tints, depth, weight, passed, back, hist, w_e, w_m, w_mt, w_v, w_vt, w_c, w_ct, bias, per_ray,
    g_e, g_m, g_v, g_c, g_r, mine, halo, send, recv, *sums,
):
    tile_rows, tile_cols = camera.shape
    lanes = tile_rows * tile_cols
    cameras = anchors.shape[1]
    points = CHUNK * lanes
    per_chunk = CHUNK // GROUP
    tx, ty = lax.axis_index("tx"), lax.axis_index("ty")
    device = tx * sizes["ty"] + ty
    sides = (
        ({"tx": tx - 1}, tx > 0),
        ({"tx": tx + 1}, tx < sizes["tx"] - 1),
        ({"ty": ty - 1}, ty > 0),
        ({"ty": ty + 1}, ty < sizes["ty"] - 1),
    )
    sum_of = []
    at = 0
    for plan, least in plans:
        length = 4 + 2 * len(plan)
        sum_of.append(Sum(plan, least, sums[at : at + length]))
        at += length
    params, params_fine, grads, grads_fine, counting = sum_of

    choose_e = selector(64, encoder.shape[0], LPOS, 32, BF16)
    choose_d = selector(32, viewer.shape[0] - 256, LDIR, 16, BF16)
    trees = (encoder, middle, viewer, colour, scalars)
    for net, where in ((0, params), (1, params_fine)):
        owned = [owners[net, group] == device for group in range(5)]
        pack(owned, net, choose_e, choose_d, where.source, *trees)

    tall = jnp.concatenate(
        [direction[k] for k in range(3)]
        + [target[k] for k in range(3)]
        + [ray_mask[...].astype(F32), camera[...].astype(F32)],
        0,
    )
    repeat = (iota((tile_cols, lanes), 1) % tile_cols == iota((tile_cols, lanes), 0)).astype(F32)
    wide = dot(tall, repeat, HIGH)
    keep = iota((tile_rows, lanes), 1) // tile_cols == iota((tile_rows, lanes), 0)
    rows = [
        jnp.sum(jnp.where(keep, wide[k * tile_rows : k * tile_rows + tile_rows], 0.0), 0, keepdims=True)
        for k in range(8)
    ]
    mask, camera_row = rows[6], rows[7]
    target_rows = rows[3:6]
    number = iota((128, lanes), 0)
    picks = camera_row == number.astype(F32)
    counting.source[...] = dot_nt(
        jnp.broadcast_to(mask, (8, lanes)).astype(BF16), (picks | (number == 127)).astype(BF16)
    )
    picks = picks.astype(F32)
    greet(groups, sides[:2])
    params.step(0)
    counting.step(0)

    centres = jnp.concatenate([anchors[...], jnp.zeros((3, 128 - cameras), F32)], 1)
    origin = dot(centres, picks, HIGH)
    basis = jnp.concatenate([origin] + rows[0:3] + [jnp.zeros((2, lanes), F32)], 0)
    row8 = iota((8, lanes), 0)
    row32 = iota((32, lanes), 0)
    lift = iota((40, 8), 0)
    third = jnp.where(lift < 32, lift % 3, jnp.where(lift == 38, 2, -9))
    o_all = dot((third == iota((40, 8), 1)).astype(F32), basis, HIGH)
    d_all = dot((third + 3 == iota((40, 8), 1)).astype(F32), basis, HIGH)
    o_main, d_main = o_all[:32], d_all[:32]
    o_last, d_last = jnp.where(row8 == 7, 1.0 / shrink, o_all[32:]), d_all[32:]
    half_pi = jnp.float32(math.pi) * 0.5
    scale = jnp.zeros((32, lanes), F32)
    for level in range(LPOS):
        scale = jnp.where((row32 >= 3 * level) & (row32 < 3 * level + 3), half_pi * (2.0**level), scale)

    row16 = iota((16, lanes), 0)
    scale_d = scale[:16]
    sin_d, cos_d = sin_cos_twice(d_main[:16] * scale_d)
    top = jnp.where(row16 >= 12, jnp.where(row16 < 15, d_main[:16], 0.0), sin_d)
    bottom = jnp.where(row16 >= 12, jnp.where(row16 == 12, 1.0, 0.0), cos_d)
    view_code = jnp.concatenate([top, bottom], 0).astype(BF16)

    samples_fine = levels.shape[1]
    blocks_of = (SC // GROUP, samples_fine // GROUP)
    first_block = (0, blocks_of[0])
    for b in range(blocks_of[0]):
        depth[b] = near_plane + (far_plane - near_plane) * ((row8 + b * GROUP).astype(F32) + 0.5) / SC
    turned = levels[...].astype(F32).T
    for b in range(blocks_of[1]):
        at = turned[b * GROUP : b * GROUP + GROUP]
        depth[blocks_of[0] + b] = near_plane + (far_plane - near_plane) * (at + 0.5) / NT
    bins_turned = bins[...].astype(F32).T

    def encode(b, carry):
        for s in range(GROUP):
            t = depth[b, s : s + 1]
            place = (o_main + t * d_main) * shrink
            wave, cowave = sin_cos_twice(place * scale)
            wave = jnp.where(row32 >= 30, place, wave)
            extra = (o_last + t * d_last) * shrink
            end = jnp.where(row8 >= 6, extra, cowave[24:])
            cowave = jnp.concatenate([cowave[:24], end], 0)
            enc[b, 0:32, s * lanes : s * lanes + lanes] = wave.astype(BF16)
            enc[b, 32:64, s * lanes : s * lanes + lanes] = cowave.astype(BF16)
        return carry

    all_blocks = sum(blocks_of)
    cuts = [all_blocks * k // (params.steps - 1) for k in range(params.steps)]
    for k in range(1, params.steps):
        lax.fori_loop(cuts[k - 1], cuts[k], encode, 0)
        params.step(k)
        if k < counting.steps:
            counting.step(k)

    count = counting.whole[...]
    mask_floor = jnp.maximum(count[0:1, 127:128], 1.0)
    inverse = 1.0 / jnp.maximum(count, 1.0)
    ray_weight = dot(inverse, picks, HIGH)[0:1] * mask / cameras
    ones = jnp.full((16, points), 1.0, BF16)
    loss = jnp.zeros((1, lanes), F32)

    chunks_of = [n // per_chunk for n in blocks_of]

    def spread_over(steps, over):
        return {steps[k]: (over * k) // len(steps) for k in range(len(steps))}

    half = params.steps // 2
    beside = {
        (0, "forward"): [(params_fine, spread_over(range(0, half - 1), chunks_of[0]))],
        (0, "backward"): [(params_fine, spread_over(range(half - 1, params.steps), chunks_of[0]))],
        (1, "forward"): [(grads, spread_over(range(0, half + 1), chunks_of[1]))],
        (1, "backward"): [(grads, spread_over(range(half + 1, grads.steps), chunks_of[1]))],
    }

    def send_on(net, name, c):
        for moved, spots in beside[(net, name)]:
            for k, spot in spots.items():

                @pl.when(c == spot)
                def _(moved=moved, k=k):
                    moved.step(k)

    for net in range(2):
        blocks, first, chunks = blocks_of[net], first_block[net], chunks_of[net]
        held = (params, params_fine)[net].whole
        middle_now = held[ROW_M : ROW_M + 256]
        w_m[...] = middle_now
        w_mt[...] = middle_now.astype(F32).T.astype(BF16)
        misc32 = held[ROW_S : ROW_S + 16].astype(F32)
        row = iota((16, 256), 0)
        views = held[ROW_V : ROW_V + 128]
        w_vt[0:128, 0:128] = views[:, 0:128]
        w_vt[128:256, 0:128] = views[:, 128:256]
        w_v[0:128, 0:128] = views[:, 0:128].astype(F32).T.astype(BF16)
        w_v[0:128, 128:256] = views[:, 128:256].astype(F32).T.astype(BF16)
        w_v[128:144] = jnp.where(row == 0, misc32, 0.0).astype(BF16)
        sigma_t = jnp.concatenate([jnp.zeros((3, 256), F32), misc32[0:1], jnp.zeros((124, 256), F32)], 0).T
        w_vt[:, 128:144] = sigma_t[:, :16].astype(BF16)
        w_e[...] = held[ROW_E : ROW_E + 64].astype(F32).T.astype(BF16)
        last = held[ROW_D : ROW_D + 32].astype(F32)
        paint = last[:16, 128:]
        tail = misc32[2:3]
        sigma_bias = tail[:, 0:1]
        lane = iota((16, 128), 1)
        row_c = iota((16, 128), 0)
        tint_bias = jnp.zeros((16, 128), F32)
        for k in range(3):
            tint_bias = jnp.where((row_c == k) & (lane == 0), tail[:, 129 + k : 130 + k], tint_bias)
        w_c[:, 0:128] = paint.astype(BF16)
        w_c[:, 128:144] = tint_bias[:, :16].astype(BF16)
        w_ct[...] = jnp.concatenate([paint, jnp.zeros((112, 128), F32)], 0).T[:, :16].astype(BF16)
        bias[...] = jnp.broadcast_to(misc32[1:2], (128, 256)).T
        views_d = last[:, :128]
        shifted = pltpu.roll(jnp.broadcast_to(tail, (8, 256)), 255, 1)[0:1, :128]
        views_d = jnp.where(iota((32, 128), 0) == 28, shifted, views_d)
        per_ray[...] = dot_tn(views_d.astype(BF16), view_code)

        def code_of(c):
            start = first + c * per_chunk
            return jnp.concatenate([enc[start + i] for i in range(per_chunk)], 1)

        def forward(c, carry):
            send_on(net, "forward", c)
            one = jnp.maximum(dot(w_e[...], code_of(c)).astype(BF16), 0)
            h1[c] = one
            two = dot(w_m[...], one) + jnp.tile(bias[...], (1, points // 128))
            two = jnp.maximum(two.astype(BF16), 0)
            h2[c] = two
            out = dot(w_v[...], two)
            view = out[:128] + jnp.tile(per_ray[...], (1, CHUNK))
            view = jnp.maximum(view.astype(BF16), 0)
            hv[c] = view
            paint = dot(w_c[...], jnp.concatenate([view, ones], 0))
            for s in range(CHUNK):
                part = slice(s * lanes, s * lanes + lanes)
                b, r = c * per_chunk + s // GROUP, s % GROUP
                for k in range(3):
                    raw[k, b, r : r + 1] = paint[k : k + 1, part]
                raw[3, b, r : r + 1] = out[128:129, part]
            return carry

        lax.fori_loop(0, chunks, forward, 0)

        before = jnp.zeros((1, lanes), F32)
        shade = [jnp.zeros((8, lanes), F32) for _ in range(3)]
        far, opaque = jnp.zeros((8, lanes), F32), jnp.zeros((8, lanes), F32)

        def spacing(b):
            t = depth[first + b]
            after = depth[first + b + 1, 0:1] if b + 1 < blocks else jnp.full((1, lanes), far_plane, F32)
            return jnp.where(row8 == 7, after, pltpu.roll(t, 7, 0)) - t

        for b in range(blocks):
            zs = raw[3, b] + sigma_bias
            density = jnp.maximum(zs, 0.0) + jnp.log1p(jnp.exp(-jnp.abs(zs)))
            q = density * spacing(b)
            inclusive = running(q) + before
            before = inclusive[7:8]
            lit = jnp.exp(-(inclusive - q))
            w = lit * (1.0 - jnp.exp(-q))
            weight[b] = w
            passed[b] = jnp.exp(-inclusive)
            if net == 1:
                back[3, b] = density * mask
            for k in range(3):
                tint = jax.nn.sigmoid(raw[k, b])
                tints[k, b] = tint
                shade[k] = shade[k] + w * tint
            far = far + w * depth[first + b]
            opaque = opaque + w
        shade = [total(x) for x in shade]
        far, opaque = total(far), total(opaque)
        miss = [shade[k] - target_rows[k] for k in range(3)]
        loss = loss + ray_weight * (miss[0] * miss[0] + miss[1] * miss[1] + miss[2] * miss[2])
        seed = [2.0 * ray_weight * miss[k] for k in range(3)]
        seed_depth = seed_opaque = None
        if net == 1:
            for k in range(3):
                mine[k : k + 1] = shade[k]
            mine[3:4] = far
            mine[4:5] = mask
            mine[5:8] = jnp.zeros((3, lanes), F32)

            def across(i, slot):
                return pltpu.make_async_remote_copy(
                    mine, halo.at[slot], send.at[i], recv.at[slot], device_id=sides[i][0], device_id_type=MESH
                )

            for i in range(4):
                pl.when(sides[i][1])(lambda i=i: across(i, i).start())

            def count_bin(b, carry):
                sums = jnp.zeros((8, lanes), F32)
                for s in range(blocks):
                    sums = sums + jnp.where(bins_turned[s * GROUP : s * GROUP + GROUP] == b.astype(F32), back[3, s], 0.0)
                hist[b] = sums
                return carry

            lax.fori_loop(0, NHIST, count_bin, 0)
            binned = dot_nt(jnp.full((8, lanes), 1.0, F32), jnp.sum(hist[...], 1), HIGH)[0:1] / mask_floor
            solid = 0.01 + 0.98 * opaque
            entropy = -mask * (solid * jnp.log(solid) + (1.0 - solid) * jnp.log(1.0 - solid))
            seed_opaque = -(entropy_weight / mask_floor) * mask * 0.98 * (jnp.log(solid) - jnp.log(1.0 - solid))
            for i in range(4):
                @pl.when(sides[i][1])
                def _(i=i):
                    across(i, i).wait_send()
                    across(i, i ^ 1).wait_recv()

            values = mine[...]
            lane = iota((8, lanes), 1)
            col, tile_row = lane % tile_cols, lane // tile_cols

            def beyond(i, inner, shift, wrap):
                other = jnp.where(
                    inner, pltpu.roll(values, shift % lanes, 1), pltpu.roll(halo[i ^ 1], wrap % lanes, 1)
                )
                return jnp.where(inner | sides[i][1], other, 0.0)

            smooth = jnp.zeros((8, lanes), F32)
            pull = jnp.zeros((8, lanes), F32)
            for i, inner, shift, wrap in (
                (0, col > 0, 1, 1 - tile_cols),
                (1, col < tile_cols - 1, -1, tile_cols - 1),
                (2, tile_row > 0, tile_cols, tile_cols - lanes),
                (3, tile_row < tile_rows - 1, -tile_cols, lanes - tile_cols),
            ):
                other = beyond(i, inner, shift, wrap)
                pair = other[4:5] * mask
                gap = jnp.where(row8 < 4, values - other, 0.0)
                pull = pull + pair * gap
                if i % 2 == 1:
                    smooth = smooth + pair * gap * gap
            pull = (2.0 * smooth_weight / mask_floor) * pull
            seed = [seed[k] + pull[k : k + 1] for k in range(3)]
            seed_depth = pull[3:4]
            loss = loss + (smooth_weight * total(smooth) + entropy_weight * entropy) / mask_floor

        later = jnp.zeros((1, lanes), F32)
        for b in reversed(range(blocks)):
            w = weight[b]
            tint = [tints[k, b] for k in range(3)]
            pulled = seed[0] * tint[0] + seed[1] * tint[1] + seed[2] * tint[2]
            if net == 1:
                pulled = pulled + seed_depth * depth[first + b] + seed_opaque
            weighted = pulled * w
            onward = running_back(weighted) + later
            later = onward[0:1]
            dq = pulled * passed[b] - (onward - weighted)
            back[3, b] = dq * spacing(b) * jax.nn.sigmoid(raw[3, b] + sigma_bias)
            for k in range(3):
                back[k, b] = w * seed[k] * tint[k] * (1.0 - tint[k])

        for ref in (g_e, g_m, g_v, g_c, g_r):
            ref[...] = jnp.zeros_like(ref)

        def backward(c, carry):
            send_on(net, "backward", c)
            parts = []
            for s in range(CHUNK):
                b, r = c * per_chunk + s // GROUP, s % GROUP
                parts.append(jnp.concatenate([back[k, b, r : r + 1] for k in range(4)] + [jnp.zeros((12, lanes), F32)], 0))
            gate = jnp.concatenate(parts, 1).astype(BF16)
            view = hv[c]
            gv = jnp.where(view > 0, dot(w_ct[...], gate).astype(BF16), 0)
            sums = g_r[...]
            for s in range(CHUNK):
                sums = sums + gv[:, s * lanes : s * lanes + lanes].astype(F32)
            g_r[...] = sums
            g_c[...] += dot_nt(gate, jnp.concatenate([view, ones], 0))
            both = jnp.concatenate([gv, gate], 0)
            two = h2[c]
            g_v[...] += dot_nt(both, two)
            g2 = jnp.where(two > 0, dot(w_vt[...], both).astype(BF16), 0)
            one = h1[c]
            g_m[...] += dot_nt(jnp.concatenate([one, ones], 0), g2)
            g1 = jnp.where(one > 0, dot(w_mt[...], g2).astype(BF16), 0)
            g_e[...] += dot_nt(code_of(c), g1)
            return carry

        lax.fori_loop(0, chunks, backward, 0)

        out = (grads, grads_fine)[net].source
        out[ROW_M : ROW_M + 256] = g_m[0:256]
        out[ROW_V : ROW_V + 128] = g_v[0:128]
        lane = iota((16, 256), 1)
        grad_misc = jnp.where(row == 0, g_v[131:132], jnp.where(row == 1, g_m[256:257], 0.0))
        sums_c = g_c[:, 128:129]
        for k, spot in ((3, 0), (0, 129), (1, 130), (2, 131)):
            grad_misc = jnp.where((row == 2) & (lane == spot), sums_c[k : k + 1], grad_misc)
        out[ROW_S : ROW_S + 16] = grad_misc
        out[ROW_E : ROW_E + 64] = g_e[...]
        out[ROW_D : ROW_D + 32, 0:128] = dot_nt(view_code.astype(F32), g_r[...], HIGH)
        out[ROW_D : ROW_D + 32, 128:256] = jnp.concatenate([g_c[:, :128], jnp.zeros((16, 128), F32)], 0)
        out[ROW_D + 32 : ROWS] = jnp.zeros((ROWS - ROW_D - 32, 256), F32)
    last_rows = grads_fine.source
    last_rows[ROW_D + 32 : ROW_D + 33, 0:NHIST] = binned
    fold = loss[:, :128]
    for k in range(1, lanes // 128):
        fold = fold + loss[:, k * 128 : k * 128 + 128]
    last_rows[ROW_D + 33 : ROW_D + 34, 0:128] = fold
    for k in range(grads_fine.steps):
        grads_fine.step(k)
    result[0:ROWS] = grads.whole[...]
    result[ROWS : 2 * ROWS] = grads_fine.whole[...]


def adamw_update(weight, moment, square, gradient):
    moment_next = beta_first * moment + (1.0 - beta_first) * gradient
    square_next = beta_second * square + (1.0 - beta_second) * gradient * gradient
    first_hat = moment_next / (1.0 - beta_first**step_count)
    second_hat = square_next / (1.0 - beta_second**step_count)
    weight_next = weight - learn_rate * (
        first_hat / (jnp.sqrt(second_hat) + adam_epsilon) + decay_rate * weight
    )
    return (weight_next, moment_next, square_next)


def update_kernel(tiles_y, owners, grads, *refs):
    masters, moments, squares = refs[0:5], refs[5:10], refs[10:15]
    loss, histogram = refs[15], refs[16]
    nexts, next_moments, next_squares = refs[17:22], refs[22:27], refs[27:32]
    device = lax.axis_index("tx") * tiles_y + lax.axis_index("ty")
    histogram[...] = grads[ROWS + ROW_D + 32 : ROWS + ROW_D + 33, 0:NHIST]
    loss[...] = jnp.sum(grads[ROWS + ROW_D + 33 : ROWS + ROW_D + 34, 0:128], 1, keepdims=True)
    choose_e = selector(64, masters[0].shape[0], LPOS, 32, F32)
    choose_d = selector(32, masters[2].shape[0] - 256, LDIR, 16, F32)

    def step(group, net, at, gradient):
        owned = owners[net, group] == device
        old = [ref[at] for ref in (masters[group], moments[group], squares[group])]
        new = adamw_update(*old, gradient)
        for ref, was, now in zip((nexts[group], next_moments[group], next_squares[group]), old, new):
            ref[at] = jnp.where(owned, now, was)

    every = slice(None)
    for net in range(2):
        base = net * ROWS
        step(0, net, (every, net, every), dot_tn(choose_e, grads[base + ROW_E : base + ROW_E + 64], HIGH))
        step(1, net, (net,), grads[base + ROW_M : base + ROW_M + 256].T)
        views = grads[base + ROW_V : base + ROW_V + 128]
        step(2, net, (slice(0, 128), net, every), views[:, 0:128].T)
        step(2, net, (slice(128, 256), net, every), views[:, 128:256].T)
        last = grads[base + ROW_D : base + ROW_D + 32]
        rest = slice(256, masters[2].shape[0])
        step(2, net, (rest, net, every), dot_tn(choose_d, last[:, :128], HIGH))
        step(3, net, (every, net, every), last[0:3, 128:])
        misc = grads[base + ROW_S : base + ROW_S + 16]
        spot = slice(net, net + 1)
        step(4, net, (spot, slice(0, 256)), grads[base + ROW_E + 63 : base + ROW_E + 64])
        step(4, net, (spot, slice(256, 512)), misc[1:2])
        step(4, net, (spot, slice(512, 768)), misc[0:1])
        bias = jnp.concatenate([last[28:29, :128], jnp.zeros((1, 128), F32)], 1)
        bias = pltpu.roll(jnp.broadcast_to(bias, (8, 256)), 1, 1)[0:1]
        step(4, net, (spot, slice(768, 900)), (misc[2:3] + bias)[:, :132])


VMEM_SPEC = pl.BlockSpec(memory_space=pltpu.VMEM)
SMEM_SPEC = pl.BlockSpec(memory_space=pltpu.SMEM)


def per_device(sizes, camera, ray_mask, ray_direction, anchors, target, fine_levels, density_bins, owners, *trees):
    turns = ((2, 0, 1), (0, 1, 2), (2, 0, 1), (1, 0, 2), (0, 1))
    states = [jnp.transpose(x[0], turns[i % 5]) for i, x in enumerate(trees)]
    lanes = camera.shape[0] * camera.shape[1]
    samples = fine_levels.shape[0]
    levels = jnp.transpose(fine_levels, (1, 2, 0)).reshape(lanes, samples)
    bins = jnp.transpose(density_bins, (1, 2, 0)).reshape(lanes, samples)

    groups = groups_of(sizes)
    plans = [(plan_of(groups, ROWS, 16), 16)] * 2 + [(plan_of(groups, ROWS, 8), 8)] * 2 + [(plan_of(groups, 8, 16), 8)]
    sums = []
    for (plan, _), dtype, width in zip(plans, (BF16, BF16, F32, F32, F32), (256, 256, 256, 256, 128)):
        sums += sum_scratch(plan, dtype, width)
    points = CHUNK * lanes
    chunks = samples // CHUNK
    blocks = samples // GROUP
    grads = pl.pallas_call(
        functools.partial(step_kernel, sizes, groups, plans),
        out_shape=jax.ShapeDtypeStruct((2 * ROWS, 256), F32),
        in_specs=[SMEM_SPEC] + [VMEM_SPEC] * 12,
        out_specs=VMEM_SPEC,
        scratch_shapes=[
            pltpu.VMEM((blocks + SC // GROUP, 64, GROUP * lanes), BF16),
            pltpu.VMEM((chunks, 256, points), BF16),
            pltpu.VMEM((chunks, 256, points), BF16),
            pltpu.VMEM((chunks, 128, points), BF16),
            pltpu.VMEM((4, blocks, GROUP, lanes), F32),
            pltpu.VMEM((3, blocks, GROUP, lanes), F32),
            pltpu.VMEM((blocks + SC // GROUP, GROUP, lanes), F32),
            pltpu.VMEM((blocks, GROUP, lanes), F32),
            pltpu.VMEM((blocks, GROUP, lanes), F32),
            pltpu.VMEM((4, blocks, GROUP, lanes), F32),
            pltpu.VMEM((NHIST, 8, lanes), F32),
            pltpu.VMEM((256, 64), BF16),
            pltpu.VMEM((256, 256), BF16),
            pltpu.VMEM((256, 256), BF16),
            pltpu.VMEM((144, 256), BF16),
            pltpu.VMEM((256, 144), BF16),
            pltpu.VMEM((16, 144), BF16),
            pltpu.VMEM((128, 16), BF16),
            pltpu.VMEM((256, 128), F32),
            pltpu.VMEM((128, lanes), F32),
            pltpu.VMEM((64, 256), F32),
            pltpu.VMEM((272, 256), F32),
            pltpu.VMEM((144, 256), F32),
            pltpu.VMEM((16, 144), F32),
            pltpu.VMEM((128, lanes), F32),
            pltpu.VMEM((8, lanes), F32),
            pltpu.VMEM((4, 8, lanes), F32),
            pltpu.SemaphoreType.DMA((4,)),
            pltpu.SemaphoreType.DMA((4,)),
        ]
        + sums,
        compiler_params=pltpu.CompilerParams(collective_id=0, has_side_effects=True, vmem_limit_bytes=LIMIT),
        name="step",
    )(owners.T, camera, ray_mask, ray_direction, target, levels, bins, anchors, *states[:5])

    results = pl.pallas_call(
        functools.partial(update_kernel, sizes["ty"]),
        out_shape=[jax.ShapeDtypeStruct((1, 1), F32), jax.ShapeDtypeStruct((1, NHIST), F32)]
        + [jax.ShapeDtypeStruct(x.shape, F32) for x in states],
        in_specs=[SMEM_SPEC] + [VMEM_SPEC] * 16,
        out_specs=[VMEM_SPEC] * 17,
        name="update",
    )(owners.T, grads, *states)
    turned = []
    for i, x in enumerate(results[2:]):
        turn = turns[i % 5]
        turned.append(jnp.transpose(x, [turn.index(d) for d in range(len(turn))])[None])
    return (results[0].reshape(()), results[1].reshape(NHIST)) + tuple(turned)


def solution(mesh):
    sizes = dict(mesh.shape)
    tiled, tiled3 = P("ty", "tx"), P(None, "ty", "tx")
    slots = P(("tx", "ty"), None, None, None)
    trees = (slots, slots, slots, slots, P(("tx", "ty"), None, None))
    return jax.shard_map(
        functools.partial(per_device, sizes),
        mesh=mesh,
        in_specs=(tiled, tiled, tiled3, P(), tiled3, tiled3, tiled3, P()) + trees * 3,
        out_specs=(P(), P()) + trees * 3,
        check_vma=False,
    )
```

```python
import functools
import math

import jax
import jax.numpy as jnp
from jax import lax
from jax.experimental import pallas as pl
from jax.experimental.pallas import tpu as pltpu
from jax.sharding import PartitionSpec as P

LPOS = 10
LDIR = 4
SC = 64
NT = 1024
NHIST = 64

near_plane = 2.0
far_plane = 6.0
shrink = 0.125
smooth_weight = 0.1
entropy_weight = 0.1
beta_first = 0.9
beta_second = 0.999
adam_epsilon = 1e-08
decay_rate = 0.01
learn_rate = 0.05
step_count = 10

MESH = pl.DeviceIdType.MESH
F32 = jnp.float32
BF16 = jnp.bfloat16
HIGH = lax.Precision.HIGHEST
GROUP = 8
CHUNK = 16
ROWS = 512
LIMIT = 67_000_000
PACE = (0, 0, 7, 19, 19, 24, 24)

ROW_M, ROW_V, ROW_S, ROW_E, ROW_D = 0, 256, 384, 400, 464

PI_A = 3.140625
PI_B = 0.0009670257568359375
PI_C = math.pi - PI_A - PI_B
SIN = (-0.16666656732559204, 0.008333015255630016, -0.00019806479394901544, 2.5997517241194146e-06)
COS = (-0.5, 0.04166664183139801, -0.0013888400280848145, 2.4761729946476407e-05, -2.607421833999979e-07)


def dot(a, b, precision=None):
    return lax.dot_general(a, b, (((1,), (0,)), ((), ())), preferred_element_type=F32, precision=precision)


def dot_nt(a, b, precision=None):
    return lax.dot_general(a, b, (((1,), (1,)), ((), ())), preferred_element_type=F32, precision=precision)


def dot_tn(a, b, precision=None):
    return lax.dot_general(a, b, (((0,), (0,)), ((), ())), preferred_element_type=F32, precision=precision)


def iota(shape, axis):
    return lax.broadcasted_iota(jnp.int32, shape, axis)


def sin_cos_twice(y):
    k = jnp.round(y * (1.0 / math.pi))
    y = ((y - k * PI_A) - k * PI_B) - k * PI_C
    t = y * y
    s = y * (1.0 + t * (SIN[0] + t * (SIN[1] + t * (SIN[2] + t * SIN[3]))))
    c = 1.0 + t * (COS[0] + t * (COS[1] + t * (COS[2] + t * (COS[3] + t * COS[4]))))
    d = s + s
    return d * c, 1.0 - d * s


def code_column(row, levels, pad):
    half = row % pad
    third = 3 * levels
    wave = 3 + 6 * (half // 3) + half % 3 + jnp.where(row >= pad, 3, 0)
    if levels == LPOS:
        rest = jnp.where(row == 30, 0, jnp.where(row == 31, 1, jnp.where(row == 62, 2, -1)))
    else:
        rest = jnp.where((row >= 12) & (row < 15), row - 12, jnp.where(row == 28, -1, -2))
    return jnp.where(half < third, wave, rest)


def selector(rows, columns, levels, pad, dtype):
    return (iota((rows, columns), 1) == code_column(iota((rows, columns), 0), levels, pad)).astype(dtype)


class Members:
    def __init__(self, axis, count, spread):
        self.axis, self.count, self.spread = axis, count, spread

    def place(self):
        return (lax.axis_index(self.axis) // self.spread) % self.count

    def peer(self, step):
        me = self.place()
        other = (me + step) % self.count
        return other, {self.axis: lax.axis_index(self.axis) + (other - me) * self.spread}


def groups_of(sizes):
    cores = 2 if sizes["tx"] % 2 == 0 else 1
    groups = [Members("tx", cores, 1), Members("ty", sizes["ty"], 1), Members("tx", sizes["tx"] // cores, cores)]
    return [g for g in groups if g.count > 1]


def plan_of(groups, rows, least, whole=()):
    plan = []
    for group in groups:
        after = rows // group.count if rows % (group.count * least) == 0 and group not in whole else rows
        plan.append((group, rows, after))
        rows = after
    return plan


def sum_scratch(plan, dtype, width=256):
    copies = sum(group.count - 1 for group, _, _ in plan)
    rows = plan[0][1]
    return (
        [pltpu.VMEM((rows, width), dtype), pltpu.VMEM((rows, width), dtype)]
        + [pltpu.VMEM((group.count, after, width), dtype) for group, _, after in plan]
        + [pltpu.VMEM((after, width), dtype) for _, _, after in plan]
        + [pltpu.SemaphoreType.DMA((2 * copies,)), pltpu.SemaphoreType.DMA((2 * copies,))]
    )


class Sum:
    def __init__(self, plan, least, refs):
        n = len(plan)
        self.plan, self.least = plan, least
        self.source, self.whole = refs[0], refs[1]
        self.landing, self.part = refs[2 : 2 + n], refs[2 + n : 2 + 2 * n]
        self.send, self.recv = refs[2 + 2 * n :]
        self.steps = 2 * n + 1

    def rows_at(self, start, length):
        return pl.ds(pl.multiple_of(start, self.least), length)

    def offsets(self):
        at, result = 0, [0]
        for group, before, after in self.plan:
            if after != before:
                at = at + group.place() * after
            result.append(at)
        return result

    def base(self, stage, back):
        copies = [group.count - 1 for group, _, _ in self.plan]
        return sum(copies[:stage]) + (sum(copies) if back else 0)

    def scatter(self, stage):
        group, before, after = self.plan[stage]
        held = self.source if stage == 0 else self.part[stage - 1]
        copies = []
        for step in range(1, group.count):
            other, where = group.peer(step)
            k = self.base(stage, False) + step - 1
            piece = held if after == before else held.at[self.rows_at(other * after, after)]
            copies.append(
                pltpu.make_async_remote_copy(
                    piece,
                    self.landing[stage].at[group.place()],
                    self.send.at[k],
                    self.recv.at[k],
                    device_id=where,
                    device_id_type=MESH,
                )
            )
        return copies

    def gather(self, stage):
        group, before, after = self.plan[stage]
        if after == before:
            return []
        mine = self.rows_at(self.offsets()[stage + 1], after)
        copies = []
        for step in range(1, group.count):
            _, where = group.peer(step)
            k = self.base(stage, True) + step - 1
            copies.append(
                pltpu.make_async_remote_copy(
                    self.whole.at[mine],
                    self.whole.at[mine],
                    self.send.at[k],
                    self.recv.at[k],
                    device_id=where,
                    device_id_type=MESH,
                )
            )
        return copies

    def step(self, k):
        n = len(self.plan)
        if 0 < k <= n:
            stage = k - 1
            group, before, after = self.plan[stage]
            held = self.source if stage == 0 else self.part[stage - 1]
            for copy in self.scatter(stage):
                copy.wait()
            own = held[...] if after == before else held[self.rows_at(group.place() * after, after)]
            self.landing[stage][group.place()] = own
            total = self.landing[stage][0]
            for j in range(1, group.count):
                total = total + self.landing[stage][j]
            self.part[stage][...] = total
            if stage == n - 1:
                self.whole[self.rows_at(self.offsets()[n], after)] = total
        elif k > n:
            for copy in self.gather(2 * n - k):
                copy.wait()
        if k < n:
            for copy in self.scatter(k):
                copy.start()
        elif k < 2 * n:
            for copy in self.gather(2 * n - 1 - k):
                copy.start()


def greet(groups, sides):
    barrier = pltpu.get_barrier_semaphore()
    expected = 0
    for group in groups:
        for step in range(1, group.count):
            pl.semaphore_signal(barrier, inc=1, device_id=group.peer(step)[1], device_id_type=MESH)
            expected = expected + 1
    for where, there in sides:
        expected = expected + there.astype(jnp.int32)

        @pl.when(there)
        def _(where=where):
            pl.semaphore_signal(barrier, inc=1, device_id=where, device_id_type=MESH)

    return expected


def running(block):
    row = iota(block.shape, 0)
    for shift in (1, 2, 4):
        block = block + jnp.where(row >= shift, pltpu.roll(block, shift, 0), 0.0)
    return block


def running_back(block):
    row = iota(block.shape, 0)
    for shift in (1, 2, 4):
        block = block + jnp.where(row < 8 - shift, pltpu.roll(block, 8 - shift, 0), 0.0)
    return block


def total(block):
    return jnp.sum(block, 0, keepdims=True)


def pack(owned, net, choose_e, choose_d, big, encoder, middle, viewer, colour, scalars):
    def rounded(group, value):
        return jnp.where(owned[group], value, 0.0).astype(BF16)

    big[ROW_M : ROW_M + 256] = rounded(1, middle[net])
    views = rounded(2, viewer[:, net, :])
    big[ROW_V : ROW_V + 128, 0:128] = views[0:128]
    big[ROW_V : ROW_V + 128, 128:256] = views[128:256]
    row = rounded(4, scalars[net : net + 1]).astype(F32)
    block = iota((16, 256), 0)
    tail = jnp.concatenate([row[:, 768:], jnp.zeros((1, 124), F32)], 1)
    picked = jnp.where(block == 0, row[:, 512:768], jnp.where(block == 1, row[:, 256:512], 0.0))
    big[ROW_S : ROW_S + 16] = jnp.where(block == 2, tail, picked).astype(BF16)
    first = dot(choose_e, rounded(0, encoder[:, net, :]))
    first = jnp.where(iota((64, 256), 0) == 63, row[:, :256], first)
    big[ROW_E : ROW_E + 64] = first.astype(BF16)
    big[ROW_D : ROW_D + 32, 0:128] = dot(choose_d, views[256:]).astype(BF16)
    paint = jnp.concatenate([rounded(3, colour[:, net, :]).astype(F32), jnp.zeros((29, 128), F32)], 0)
    big[ROW_D : ROW_D + 32, 128:256] = paint.astype(BF16)
    big[ROW_D + 32 : ROWS] = jnp.zeros((ROWS - ROW_D - 32, 256), BF16)


def step_kernel(
    sizes, groups, plans, owners, camera, ray_mask, direction, target, levels, bins, anchors,
    encoder, middle, viewer, colour, scalars, result,
    enc, h1, h2, hv, raw, depth, weight, passed, back, hist, w_e, w_m, w_mt, w_v, w_vt, w_c, w_ct, bias, per_ray,
    g_e, g_m, g_v, g_c, g_r, turned, mine, halo, send, recv, *sums,
):
    tile_rows, tile_cols = camera.shape
    lanes = tile_rows * tile_cols
    cameras = anchors.shape[1]
    points = CHUNK * lanes
    per_chunk = CHUNK // GROUP
    tx, ty = lax.axis_index("tx"), lax.axis_index("ty")
    device = tx * sizes["ty"] + ty
    sides = (
        ({"tx": tx - 1}, tx > 0),
        ({"tx": tx + 1}, tx < sizes["tx"] - 1),
        ({"ty": ty - 1}, ty > 0),
        ({"ty": ty + 1}, ty < sizes["ty"] - 1),
    )
    sum_of = []
    at = 0
    for plan, least in plans:
        length = 4 + 2 * len(plan)
        sum_of.append(Sum(plan, least, sums[at : at + length]))
        at += length
    params, params_fine, counting = sum_of[:3]
    grads, grads_fine = sum_of[3:5], sum_of[5:7]
    expected = greet(groups, sides[:2])

    choose_e = selector(64, encoder.shape[0], LPOS, 32, BF16)
    choose_d = selector(32, viewer.shape[0] - 256, LDIR, 16, BF16)
    trees = (encoder, middle, viewer, colour, scalars)
    owned = [[owners[net, group] == device for group in range(5)] for net in range(2)]
    pack(owned[0], 0, choose_e, choose_d, params.source, *trees)
    pl.semaphore_wait(pltpu.get_barrier_semaphore(), expected)
    params.step(0)

    tall = jnp.concatenate(
        [direction[k] for k in range(3)]
        + [target[k] for k in range(3)]
        + [ray_mask[...].astype(F32), camera[...].astype(F32)],
        0,
    )
    repeat = (iota((tile_cols, lanes), 1) % tile_cols == iota((tile_cols, lanes), 0)).astype(F32)
    wide = dot(tall, repeat, HIGH)
    keep = iota((tile_rows, lanes), 1) // tile_cols == iota((tile_rows, lanes), 0)
    rows = [
        jnp.sum(jnp.where(keep, wide[k * tile_rows : k * tile_rows + tile_rows], 0.0), 0, keepdims=True)
        for k in range(8)
    ]
    mask, camera_row = rows[6], rows[7]
    target_rows = rows[3:6]
    number = iota((128, lanes), 0)
    picks = camera_row == number.astype(F32)
    counting.source[...] = dot_nt(
        jnp.broadcast_to(mask, (8, lanes)).astype(BF16), (picks | (number == 127)).astype(BF16)
    )
    picks = picks.astype(F32)
    counting.step(0)
    pack(owned[1], 1, choose_e, choose_d, params_fine.source, *trees)

    centres = jnp.concatenate([anchors[...], jnp.zeros((3, 128 - cameras), F32)], 1)
    origin = dot(centres, picks, HIGH)
    basis = jnp.concatenate([origin] + rows[0:3] + [jnp.zeros((2, lanes), F32)], 0)
    row8 = iota((8, lanes), 0)
    row32 = iota((32, lanes), 0)
    lift = iota((40, 8), 0)
    third = jnp.where(lift < 32, lift % 3, jnp.where(lift == 38, 2, -9))
    o_all = dot((third == iota((40, 8), 1)).astype(F32), basis, HIGH)
    d_all = dot((third + 3 == iota((40, 8), 1)).astype(F32), basis, HIGH)
    o_main, d_main = o_all[:32], d_all[:32]
    o_last, d_last = jnp.where(row8 == 7, 1.0 / shrink, o_all[32:]), d_all[32:]
    half_pi = jnp.float32(math.pi) * 0.5
    scale = jnp.zeros((32, lanes), F32)
    for level in range(LPOS):
        scale = jnp.where((row32 >= 3 * level) & (row32 < 3 * level + 3), half_pi * (2.0**level), scale)

    row16 = iota((16, lanes), 0)
    scale_d = scale[:16]
    sin_d, cos_d = sin_cos_twice(d_main[:16] * scale_d)
    top = jnp.where(row16 >= 12, jnp.where(row16 < 15, d_main[:16], 0.0), sin_d)
    bottom = jnp.where(row16 >= 12, jnp.where(row16 == 12, 1.0, 0.0), cos_d)
    view_code = jnp.concatenate([top, bottom], 0).astype(BF16)

    samples_fine = levels.shape[1]
    blocks_of = (SC // GROUP, samples_fine // GROUP)
    first_block = (0, blocks_of[0])
    for b in range(blocks_of[0]):
        depth[b] = near_plane + (far_plane - near_plane) * ((row8 + b * GROUP).astype(F32) + 0.5) / SC
    levels_turned = levels[...].astype(F32).T
    for b in range(blocks_of[1]):
        at = levels_turned[b * GROUP : b * GROUP + GROUP]
        depth[blocks_of[0] + b] = near_plane + (far_plane - near_plane) * (at + 0.5) / NT
    bins_turned = bins[...].astype(F32).T

    def encode(b, carry):
        for s in range(GROUP):
            t = depth[b, s : s + 1]
            place = (o_main + t * d_main) * shrink
            wave, cowave = sin_cos_twice(place * scale)
            wave = jnp.where(row32 >= 30, place, wave)
            extra = (o_last + t * d_last) * shrink
            end = jnp.where(row8 >= 6, extra, cowave[24:])
            cowave = jnp.concatenate([cowave[:24], end], 0)
            enc[b, 0:32, s * lanes : s * lanes + lanes] = wave.astype(BF16)
            enc[b, 32:64, s * lanes : s * lanes + lanes] = cowave.astype(BF16)
        return carry

    all_blocks = sum(blocks_of)
    done = 0
    for k in range(1, params.steps):
        until = all_blocks * PACE[min(k, len(PACE) - 1)] // PACE[-1]
        if until > done:
            lax.fori_loop(done, until, encode, 0)
        done = until
        params.step(k)
        if k < counting.steps:
            counting.step(k)

    count = counting.whole[...]
    mask_floor = jnp.maximum(count[0:1, 127:128], 1.0)
    inverse = 1.0 / jnp.maximum(count, 1.0)
    ray_weight = dot(inverse, picks, HIGH)[0:1] * mask / cameras
    ones = jnp.full((16, points), 1.0, BF16)
    loss = jnp.zeros((1, lanes), F32)

    chunks_of = [n // per_chunk for n in blocks_of]

    def at_chunks(moved, pairs, over):
        return [(part, k, over * eighth // 8) for k, eighth in pairs for part in moved]

    half = params.steps // 2
    beside = {
        (0, "forward"): at_chunks([params_fine], [(0, 0), (1, 2), (2, 6)][:half], chunks_of[0]),
        (0, "backward"): at_chunks([params_fine], [(k, min(2 + 4 * (k > half + 1), 6)) for k in range(half, params.steps - 1)], chunks_of[0]),
        (1, "forward"): at_chunks(grads, [(0, 0), (1, 1), (2, 4), (3, 7)][: half + 1], chunks_of[1]),
        (1, "backward"): at_chunks(grads, [(k, min(1 + 2 * (k - half - 1), 7)) for k in range(half + 1, params.steps)], chunks_of[1]),
    }

    def send_on(net, name, c):
        for spot in sorted({spot for _, _, spot in beside[(net, name)]}):

            @pl.when(c == spot)
            def _(spot=spot):
                for moved, k, where in beside[(net, name)]:
                    if where == spot:
                        moved.step(k)

    for net in range(2):
        blocks, first, chunks = blocks_of[net], first_block[net], chunks_of[net]
        held = (params, params_fine)[net].whole
        middle_now = held[ROW_M : ROW_M + 256]
        w_m[...] = middle_now
        w_mt[...] = middle_now.astype(F32).T.astype(BF16)
        misc32 = held[ROW_S : ROW_S + 16].astype(F32)
        row = iota((16, 256), 0)
        views = held[ROW_V : ROW_V + 128]
        w_vt[0:128, 0:128] = views[:, 0:128]
        w_vt[128:256, 0:128] = views[:, 128:256]
        w_v[0:128, 0:128] = views[:, 0:128].astype(F32).T.astype(BF16)
        w_v[0:128, 128:256] = views[:, 128:256].astype(F32).T.astype(BF16)
        w_v[128:144] = jnp.where(row == 0, misc32, 0.0).astype(BF16)
        sigma_t = jnp.concatenate([jnp.zeros((3, 256), F32), misc32[0:1], jnp.zeros((124, 256), F32)], 0).T
        w_vt[:, 128:144] = sigma_t[:, :16].astype(BF16)
        w_e[...] = held[ROW_E : ROW_E + 64].astype(F32).T.astype(BF16)
        last = held[ROW_D : ROW_D + 32].astype(F32)
        paint = last[:16, 128:]
        tail = misc32[2:3]
        sigma_bias = tail[:, 0:1]
        lane = iota((16, 128), 1)
        row_c = iota((16, 128), 0)
        tint_bias = jnp.zeros((16, 128), F32)
        for k in range(3):
            tint_bias = jnp.where((row_c == k) & (lane == 0), tail[:, 129 + k : 130 + k], tint_bias)
        w_c[:, 0:128] = paint.astype(BF16)
        w_c[:, 128:144] = tint_bias[:, :16].astype(BF16)
        w_ct[...] = jnp.concatenate([paint, jnp.zeros((112, 128), F32)], 0).T[:, :16].astype(BF16)
        bias[...] = jnp.broadcast_to(misc32[1:2], (128, 256)).T
        views_d = last[:, :128]
        shifted = pltpu.roll(jnp.broadcast_to(tail, (8, 256)), 255, 1)[0:1, :128]
        views_d = jnp.where(iota((32, 128), 0) == 28, shifted, views_d)
        per_ray[...] = dot_tn(views_d.astype(BF16), view_code)

        def code_of(c):
            start = first + c * per_chunk
            return jnp.concatenate([enc[start + i] for i in range(per_chunk)], 1)

        def forward(c, carry):
            send_on(net, "forward", c)
            one = jnp.maximum(dot(w_e[...], code_of(c)).astype(BF16), 0)
            h1[c] = one
            two = dot(w_m[...], one) + jnp.tile(bias[...], (1, points // 128))
            two = jnp.maximum(two.astype(BF16), 0)
            h2[c] = two
            out = dot(w_v[...], two)
            view = out[:128] + jnp.tile(per_ray[...], (1, CHUNK))
            view = jnp.maximum(view.astype(BF16), 0)
            hv[c] = view
            paint = dot(w_c[...], jnp.concatenate([view, ones], 0))
            for s in range(CHUNK):
                part = slice(s * lanes, s * lanes + lanes)
                b, r = c * per_chunk + s // GROUP, s % GROUP
                for k in range(3):
                    raw[k, b, r : r + 1] = paint[k : k + 1, part]
                raw[3, b, r : r + 1] = out[128:129, part]
            return carry

        lax.fori_loop(0, chunks, forward, 0)

        before = jnp.zeros((1, lanes), F32)
        shade = [jnp.zeros((8, lanes), F32) for _ in range(3)]
        far, opaque = jnp.zeros((8, lanes), F32), jnp.zeros((8, lanes), F32)

        def spacing(b):
            t = depth[first + b]
            after = depth[first + b + 1, 0:1] if b + 1 < blocks else jnp.full((1, lanes), far_plane, F32)
            return jnp.where(row8 == 7, after, pltpu.roll(t, 7, 0)) - t

        for b in range(blocks):
            zs = raw[3, b] + sigma_bias
            density = jnp.maximum(zs, 0.0) + jnp.log1p(jnp.exp(-jnp.abs(zs)))
            q = density * spacing(b)
            inclusive = running(q) + before
            before = inclusive[7:8]
            lit = jnp.exp(-(inclusive - q))
            w = lit * (1.0 - jnp.exp(-q))
            weight[b] = w
            passed[b] = jnp.exp(-inclusive)
            if net == 1:
                back[3, b] = density * mask
            for k in range(3):
                tint = jax.nn.sigmoid(raw[k, b])
                raw[k, b] = tint
                shade[k] = shade[k] + w * tint
            far = far + w * depth[first + b]
            opaque = opaque + w
        shade = [total(x) for x in shade]
        far, opaque = total(far), total(opaque)
        miss = [shade[k] - target_rows[k] for k in range(3)]
        loss = loss + ray_weight * (miss[0] * miss[0] + miss[1] * miss[1] + miss[2] * miss[2])
        seed = [2.0 * ray_weight * miss[k] for k in range(3)]
        seed_depth = seed_opaque = None
        if net == 1:
            for k in range(3):
                mine[k : k + 1] = shade[k]
            mine[3:4] = far
            mine[4:5] = mask
            mine[5:8] = jnp.zeros((3, lanes), F32)

            def across(i, slot):
                return pltpu.make_async_remote_copy(
                    mine, halo.at[slot], send.at[i], recv.at[slot], device_id=sides[i][0], device_id_type=MESH
                )

            for i in range(4):
                pl.when(sides[i][1])(lambda i=i: across(i, i).start())

            def count_bin(b, carry):
                sums = jnp.zeros((8, lanes), F32)
                for s in range(blocks):
                    sums = sums + jnp.where(bins_turned[s * GROUP : s * GROUP + GROUP] == b.astype(F32), back[3, s], 0.0)
                hist[b] = sums[:, :128]
                for k in range(1, lanes // 128):
                    hist[b] += sums[:, k * 128 : k * 128 + 128]
                return carry

            lax.fori_loop(0, NHIST, count_bin, 0)
            binned = dot_nt(jnp.full((8, 128), 1.0, F32), jnp.sum(hist[...], 1), HIGH)[0:1] / mask_floor
            solid = 0.01 + 0.98 * opaque
            entropy = -mask * (solid * jnp.log(solid) + (1.0 - solid) * jnp.log(1.0 - solid))
            seed_opaque = -(entropy_weight / mask_floor) * mask * 0.98 * (jnp.log(solid) - jnp.log(1.0 - solid))
            for i in range(4):
                @pl.when(sides[i][1])
                def _(i=i):
                    across(i, i).wait_send()
                    across(i, i ^ 1).wait_recv()

            values = mine[...]
            lane = iota((8, lanes), 1)
            col, tile_row = lane % tile_cols, lane // tile_cols

            def beyond(i, inner, shift, wrap):
                other = jnp.where(
                    inner, pltpu.roll(values, shift % lanes, 1), pltpu.roll(halo[i ^ 1], wrap % lanes, 1)
                )
                return jnp.where(inner | sides[i][1], other, 0.0)

            smooth = jnp.zeros((8, lanes), F32)
            pull = jnp.zeros((8, lanes), F32)
            for i, inner, shift, wrap in (
                (0, col > 0, 1, 1 - tile_cols),
                (1, col < tile_cols - 1, -1, tile_cols - 1),
                (2, tile_row > 0, tile_cols, tile_cols - lanes),
                (3, tile_row < tile_rows - 1, -tile_cols, lanes - tile_cols),
            ):
                other = beyond(i, inner, shift, wrap)
                pair = other[4:5] * mask
                gap = jnp.where(row8 < 4, values - other, 0.0)
                pull = pull + pair * gap
                if i % 2 == 1:
                    smooth = smooth + pair * gap * gap
            pull = (2.0 * smooth_weight / mask_floor) * pull
            seed = [seed[k] + pull[k : k + 1] for k in range(3)]
            seed_depth = pull[3:4]
            loss = loss + (smooth_weight * total(smooth) + entropy_weight * entropy) / mask_floor

        later = jnp.zeros((1, lanes), F32)
        for b in reversed(range(blocks)):
            w = weight[b]
            tint = [raw[k, b] for k in range(3)]
            pulled = seed[0] * tint[0] + seed[1] * tint[1] + seed[2] * tint[2]
            if net == 1:
                pulled = pulled + seed_depth * depth[first + b] + seed_opaque
            weighted = pulled * w
            onward = running_back(weighted) + later
            later = onward[0:1]
            dq = pulled * passed[b] - (onward - weighted)
            back[3, b] = dq * spacing(b) * jax.nn.sigmoid(raw[3, b] + sigma_bias)
            for k in range(3):
                back[k, b] = w * seed[k] * tint[k] * (1.0 - tint[k])

        for ref in (g_e, g_m, g_v, g_c, g_r):
            ref[...] = jnp.zeros_like(ref)

        def backward(c, carry):
            send_on(net, "backward", c)
            parts = []
            for s in range(CHUNK):
                b, r = c * per_chunk + s // GROUP, s % GROUP
                parts.append(jnp.concatenate([back[k, b, r : r + 1] for k in range(4)] + [jnp.zeros((12, lanes), F32)], 0))
            gate = jnp.concatenate(parts, 1).astype(BF16)
            view = hv[c]
            gv = jnp.where(view > 0, dot(w_ct[...], gate).astype(BF16), 0)
            sums = g_r[...]
            for s in range(CHUNK):
                sums = sums + gv[:, s * lanes : s * lanes + lanes].astype(F32)
            g_r[...] = sums
            g_c[...] += dot_nt(jnp.concatenate([view, ones], 0), gate)
            both = jnp.concatenate([gv, gate], 0)
            two = h2[c]
            turned[...] = two.T
            g_v[...] += dot(both, turned[...])
            g2 = jnp.where(two > 0, dot(w_vt[...], both).astype(BF16), 0)
            one = h1[c]
            g_m[...] += dot_nt(jnp.concatenate([one, ones], 0), g2)
            g1 = jnp.where(one > 0, dot(w_mt[...], g2).astype(BF16), 0)
            turned[...] = g1.T
            g_e[...] += dot(code_of(c), turned[...])
            return carry

        lax.fori_loop(0, chunks, backward, 0)
        if net == 0:
            params_fine.step(params.steps - 1)

        tints = jnp.concatenate([g_c[...], jnp.zeros((144, 112), F32)], 1)
        tints, sums_c = tints[:128].T[:16], tints[128:136].T[:16, 0:1]
        upper, lower = [part.source for part in (grads, grads_fine)[net]]
        upper[...] = g_m[0:256]
        lower[ROW_V - 256 : ROW_V - 128] = g_v[0:128]
        lane = iota((16, 256), 1)
        grad_misc = jnp.where(row == 0, g_v[131:132], jnp.where(row == 1, g_m[256:257], 0.0))
        for k, spot in ((3, 0), (0, 129), (1, 130), (2, 131)):
            grad_misc = jnp.where((row == 2) & (lane == spot), sums_c[k : k + 1], grad_misc)
        lower[ROW_S - 256 : ROW_S - 240] = grad_misc
        lower[ROW_E - 256 : ROW_E - 192] = g_e[...]
        lower[ROW_D - 256 : ROW_D - 224, 0:128] = dot_nt(view_code.astype(F32), g_r[...], HIGH)
        lower[ROW_D - 256 : ROW_D - 224, 128:256] = jnp.concatenate([tints, jnp.zeros((16, 128), F32)], 0)
        lower[ROW_D - 224 : ROWS - 256] = jnp.zeros((ROWS - ROW_D - 32, 256), F32)
    rest = grads_fine[1].source
    rest[ROW_D - 224 : ROW_D - 223, 0:NHIST] = binned
    fold = loss[:, :128]
    for k in range(1, lanes // 128):
        fold = fold + loss[:, k * 128 : k * 128 + 128]
    rest[ROW_D - 223 : ROW_D - 222, 0:128] = fold
    for k in range(params.steps):
        for part in grads_fine:
            part.step(k)
    for i, part in enumerate(grads + grads_fine):
        result[i * 256 : i * 256 + 256] = part.whole[...]


def adamw_update(weight, moment, square, gradient):
    moment_next = beta_first * moment + (1.0 - beta_first) * gradient
    square_next = beta_second * square + (1.0 - beta_second) * gradient * gradient
    first_hat = moment_next / (1.0 - beta_first**step_count)
    second_hat = square_next / (1.0 - beta_second**step_count)
    weight_next = weight - learn_rate * (
        first_hat / (jnp.sqrt(second_hat) + adam_epsilon) + decay_rate * weight
    )
    return (weight_next, moment_next, square_next)


def update_kernel(tiles_y, owners, grads, *refs):
    given, loss, histogram, taken = refs[0:15], refs[15], refs[16], refs[17:32]
    held, arrived, left = refs[32:47], refs[47], refs[48]
    device = lax.axis_index("tx") * tiles_y + lax.axis_index("ty")
    order = (1, 2, 0, 4, 3)
    for group in order:
        for i in (group, group + 5, group + 10):
            pltpu.make_async_copy(given[i], held[i], arrived.at[i]).start()
    histogram[...] = grads[ROWS + ROW_D + 32 : ROWS + ROW_D + 33, 0:NHIST]
    loss[...] = jnp.sum(grads[ROWS + ROW_D + 33 : ROWS + ROW_D + 34, 0:128], 1, keepdims=True)

    def step(group, at, gradient):
        trio = (held[group], held[group + 5], held[group + 10])
        for ref, now in zip(trio, adamw_update(*[ref[at] for ref in trio], gradient)):
            ref[at] = now

    every = slice(None)

    def update(group, net):
        base = net * ROWS
        last = grads[base + ROW_D : base + ROW_D + 32]
        if group == 0:
            choose = selector(64, held[0].shape[0], LPOS, 32, F32)
            step(0, (every, net, every), dot_tn(choose, grads[base + ROW_E : base + ROW_E + 64], HIGH))
        elif group == 1:
            step(1, (net,), grads[base + ROW_M : base + ROW_M + 256].T)
        elif group == 2:
            views = grads[base + ROW_V : base + ROW_V + 128]
            step(2, (slice(0, 128), net, every), views[:, 0:128].T)
            step(2, (slice(128, 256), net, every), views[:, 128:256].T)
            rest = slice(256, held[2].shape[0])
            choose = selector(32, held[2].shape[0] - 256, LDIR, 16, F32)
            step(2, (rest, net, every), dot_tn(choose, last[:, :128], HIGH))
        elif group == 3:
            step(3, (every, net, every), last[0:3, 128:])
        else:
            misc = grads[base + ROW_S : base + ROW_S + 16]
            spot = slice(net, net + 1)
            step(4, (spot, slice(0, 256)), grads[base + ROW_E + 63 : base + ROW_E + 64])
            step(4, (spot, slice(256, 512)), misc[1:2])
            step(4, (spot, slice(512, 768)), misc[0:1])
            bias = jnp.concatenate([last[28:29, :128], jnp.zeros((1, 128), F32)], 1)
            bias = pltpu.roll(jnp.broadcast_to(bias, (8, 256)), 1, 1)[0:1]
            step(4, (spot, slice(768, 900)), (misc[2:3] + bias)[:, :132])

    for group in order:
        trio = (group, group + 5, group + 10)
        for i in trio:
            pltpu.make_async_copy(given[i], held[i], arrived.at[i]).wait()
        for net in range(2):
            pl.when(owners[net, group] == device)(functools.partial(update, group, net))
        for i in trio:
            pltpu.make_async_copy(held[i], taken[i], left.at[i]).start()
    for i in range(15):
        pltpu.make_async_copy(held[i], taken[i], left.at[i]).wait()


ANY_SPEC = pl.BlockSpec(memory_space=pl.ANY)
VMEM_SPEC = pl.BlockSpec(memory_space=pltpu.VMEM)
SMEM_SPEC = pl.BlockSpec(memory_space=pltpu.SMEM)


def per_device(sizes, camera, ray_mask, ray_direction, anchors, target, fine_levels, density_bins, owners, *trees):
    turns = ((2, 0, 1), (0, 1, 2), (2, 0, 1), (1, 0, 2), (0, 1))
    states = [jnp.transpose(x[0], turns[i % 5]) for i, x in enumerate(trees)]
    lanes = camera.shape[0] * camera.shape[1]
    samples = fine_levels.shape[0]
    levels = jnp.transpose(fine_levels, (1, 2, 0)).reshape(lanes, samples)
    bins = jnp.transpose(density_bins, (1, 2, 0)).reshape(lanes, samples)

    groups = groups_of(sizes)
    turned_round = groups[:1] + groups[:0:-1]
    param_plan = plan_of(groups, ROWS, 16, groups[2:])
    upper, lower = plan_of(groups, 256, 8), plan_of(turned_round, 256, 8)
    plans = [(param_plan, 16), (param_plan, 16), (plan_of(groups, 8, 8, groups), 8)]
    plans += [(upper, 8), (lower, 8)] * 2
    sums = []
    for (plan, _), dtype, width in zip(plans, (BF16, BF16) + (F32,) * 5, (256, 256, 128) + (256,) * 4):
        sums += sum_scratch(plan, dtype, width)
    points = CHUNK * lanes
    chunks = samples // CHUNK
    blocks = samples // GROUP
    grads = pl.pallas_call(
        functools.partial(step_kernel, sizes, groups, plans),
        out_shape=jax.ShapeDtypeStruct((2 * ROWS, 256), F32),
        in_specs=[SMEM_SPEC] + [VMEM_SPEC] * 12,
        out_specs=VMEM_SPEC,
        scratch_shapes=[
            pltpu.VMEM((blocks + SC // GROUP, 64, GROUP * lanes), BF16),
            pltpu.VMEM((chunks, 256, points), BF16),
            pltpu.VMEM((chunks, 256, points), BF16),
            pltpu.VMEM((chunks, 128, points), BF16),
            pltpu.VMEM((4, blocks, GROUP, lanes), F32),
            pltpu.VMEM((blocks + SC // GROUP, GROUP, lanes), F32),
            pltpu.VMEM((blocks, GROUP, lanes), F32),
            pltpu.VMEM((blocks, GROUP, lanes), F32),
            pltpu.VMEM((4, blocks, GROUP, lanes), F32),
            pltpu.VMEM((NHIST, 8, 128), F32),
            pltpu.VMEM((256, 64), BF16),
            pltpu.VMEM((256, 256), BF16),
            pltpu.VMEM((256, 256), BF16),
            pltpu.VMEM((144, 256), BF16),
            pltpu.VMEM((256, 144), BF16),
            pltpu.VMEM((16, 144), BF16),
            pltpu.VMEM((128, 16), BF16),
            pltpu.VMEM((256, 128), F32),
            pltpu.VMEM((128, lanes), F32),
            pltpu.VMEM((64, 256), F32),
            pltpu.VMEM((272, 256), F32),
            pltpu.VMEM((144, 256), F32),
            pltpu.VMEM((144, 16), F32),
            pltpu.VMEM((128, lanes), F32),
            pltpu.VMEM((points, 256), BF16),
            pltpu.VMEM((8, lanes), F32),
            pltpu.VMEM((4, 8, lanes), F32),
            pltpu.SemaphoreType.DMA((4,)),
            pltpu.SemaphoreType.DMA((4,)),
        ]
        + sums,
        compiler_params=pltpu.CompilerParams(collective_id=0, has_side_effects=True, vmem_limit_bytes=LIMIT),
        name="step",
    )(owners.T, camera, ray_mask, ray_direction, target, levels, bins, anchors, *states[:5])

    results = pl.pallas_call(
        functools.partial(update_kernel, sizes["ty"]),
        out_shape=[jax.ShapeDtypeStruct((1, 1), F32), jax.ShapeDtypeStruct((1, NHIST), F32)]
        + [jax.ShapeDtypeStruct(x.shape, F32) for x in states],
        in_specs=[SMEM_SPEC, VMEM_SPEC] + [ANY_SPEC] * 15,
        out_specs=[VMEM_SPEC] * 2 + [ANY_SPEC] * 15,
        scratch_shapes=[pltpu.VMEM(x.shape, F32) for x in states]
        + [pltpu.SemaphoreType.DMA((15,)), pltpu.SemaphoreType.DMA((15,))],
        name="update",
    )(owners.T, grads, *states)
    turned = []
    for i, x in enumerate(results[2:]):
        turn = turns[i % 5]
        turned.append(jnp.transpose(x, [turn.index(d) for d in range(len(turn))])[None])
    return (results[0].reshape(()), results[1].reshape(NHIST)) + tuple(turned)


def solution(mesh):
    sizes = dict(mesh.shape)
    tiled, tiled3 = P("ty", "tx"), P(None, "ty", "tx")
    slots = P(("tx", "ty"), None, None, None)
    trees = (slots, slots, slots, slots, P(("tx", "ty"), None, None))
    return jax.shard_map(
        functools.partial(per_device, sizes),
        mesh=mesh,
        in_specs=(tiled, tiled, tiled3, P(), tiled3, tiled3, tiled3, P()) + trees * 3,
        out_specs=(P(), P()) + trees * 3,
        check_vma=False,
    )
```

```python
import functools
import math

import jax
import jax.numpy as jnp
from jax import lax
from jax.experimental import pallas as pl
from jax.experimental.pallas import tpu as pltpu
from jax.sharding import PartitionSpec as P

LPOS = 10
LDIR = 4
SC = 64
NT = 1024
NHIST = 64

near_plane = 2.0
far_plane = 6.0
shrink = 0.125
smooth_weight = 0.1
entropy_weight = 0.1
beta_first = 0.9
beta_second = 0.999
adam_epsilon = 1e-08
decay_rate = 0.01
learn_rate = 0.05
step_count = 10

MESH = pl.DeviceIdType.MESH
F32 = jnp.float32
BF16 = jnp.bfloat16
HIGH = lax.Precision.HIGHEST
GROUP = 8
CHUNK = 16
ROWS = 512
LIMIT = 67_000_000
PACE = (0, 0, 7, 19, 19, 24, 24)

ROW_M, ROW_V, ROW_S, ROW_E, ROW_D = 0, 256, 384, 400, 464

PI_A = 3.140625
PI_B = 0.0009670257568359375
PI_C = math.pi - PI_A - PI_B
SIN = (-0.16666656732559204, 0.008333015255630016, -0.00019806479394901544, 2.5997517241194146e-06)
COS = (-0.5, 0.04166664183139801, -0.0013888400280848145, 2.4761729946476407e-05, -2.607421833999979e-07)


def dot(a, b, precision=None):
    return lax.dot_general(a, b, (((1,), (0,)), ((), ())), preferred_element_type=F32, precision=precision)


def dot_nt(a, b, precision=None):
    return lax.dot_general(a, b, (((1,), (1,)), ((), ())), preferred_element_type=F32, precision=precision)


def dot_tn(a, b, precision=None):
    return lax.dot_general(a, b, (((0,), (0,)), ((), ())), preferred_element_type=F32, precision=precision)


def iota(shape, axis):
    return lax.broadcasted_iota(jnp.int32, shape, axis)


def sin_cos_twice(y):
    k = jnp.round(y * (1.0 / math.pi))
    y = ((y - k * PI_A) - k * PI_B) - k * PI_C
    t = y * y
    s = y * (1.0 + t * (SIN[0] + t * (SIN[1] + t * (SIN[2] + t * SIN[3]))))
    c = 1.0 + t * (COS[0] + t * (COS[1] + t * (COS[2] + t * (COS[3] + t * COS[4]))))
    d = s + s
    return d * c, 1.0 - d * s


def code_column(row, levels, pad):
    half = row % pad
    third = 3 * levels
    wave = 3 + 6 * (half // 3) + half % 3 + jnp.where(row >= pad, 3, 0)
    if levels == LPOS:
        rest = jnp.where(row == 30, 0, jnp.where(row == 31, 1, jnp.where(row == 62, 2, -1)))
    else:
        rest = jnp.where((row >= 12) & (row < 15), row - 12, jnp.where(row == 28, -1, -2))
    return jnp.where(half < third, wave, rest)


def selector(rows, columns, levels, pad, dtype):
    return (iota((rows, columns), 1) == code_column(iota((rows, columns), 0), levels, pad)).astype(dtype)


class Members:
    def __init__(self, axis, count, spread):
        self.axis, self.count, self.spread = axis, count, spread

    def place(self):
        return (lax.axis_index(self.axis) // self.spread) % self.count

    def peer(self, step):
        me = self.place()
        other = (me + step) % self.count
        return other, {self.axis: lax.axis_index(self.axis) + (other - me) * self.spread}


def groups_of(sizes):
    cores = 2 if sizes["tx"] % 2 == 0 else 1
    groups = [Members("tx", cores, 1), Members("ty", sizes["ty"], 1), Members("tx", sizes["tx"] // cores, cores)]
    return [g for g in groups if g.count > 1]


def plan_of(groups, rows, least, whole=()):
    plan = []
    for group in groups:
        after = rows // group.count if rows % (group.count * least) == 0 and group not in whole else rows
        plan.append((group, rows, after))
        rows = after
    return plan


def sum_scratch(plan, dtype, width, beyond):
    copies = sum(group.count - 1 for group, _, _ in plan)
    rows = plan[0][1]
    return (
        [pltpu.VMEM((rows + beyond, width), dtype), pltpu.VMEM((rows, width), dtype)]
        + [pltpu.VMEM((group.count, after, width), dtype) for group, _, after in plan]
        + [pltpu.VMEM((after, width), dtype) for _, _, after in plan]
        + [pltpu.SemaphoreType.DMA((2 * copies,)), pltpu.SemaphoreType.DMA((2 * copies,))]
    )


class Sum:
    def __init__(self, plan, least, refs):
        n = len(plan)
        self.plan, self.least = plan, least
        self.source, self.whole = refs[0], refs[1]
        self.landing, self.part = refs[2 : 2 + n], refs[2 + n : 2 + 2 * n]
        self.send, self.recv = refs[2 + 2 * n :]
        self.steps = 2 * n + 1

    def rows_at(self, start, length):
        return pl.ds(pl.multiple_of(start, self.least), length)

    def offsets(self):
        at, result = 0, [0]
        for group, before, after in self.plan:
            if after != before:
                at = at + group.place() * after
            result.append(at)
        return result

    def base(self, stage, back):
        copies = [group.count - 1 for group, _, _ in self.plan]
        return sum(copies[:stage]) + (sum(copies) if back else 0)

    def scatter(self, stage):
        group, before, after = self.plan[stage]
        held = self.source if stage == 0 else self.part[stage - 1]
        copies = []
        for step in range(1, group.count):
            other, where = group.peer(step)
            k = self.base(stage, False) + step - 1
            piece = held if after == before else held.at[self.rows_at(other * after, after)]
            copies.append(
                pltpu.make_async_remote_copy(
                    piece,
                    self.landing[stage].at[group.place()],
                    self.send.at[k],
                    self.recv.at[k],
                    device_id=where,
                    device_id_type=MESH,
                )
            )
        return copies

    def gather(self, stage):
        group, before, after = self.plan[stage]
        if after == before:
            return []
        mine = self.rows_at(self.offsets()[stage + 1], after)
        copies = []
        for step in range(1, group.count):
            _, where = group.peer(step)
            k = self.base(stage, True) + step - 1
            copies.append(
                pltpu.make_async_remote_copy(
                    self.whole.at[mine],
                    self.whole.at[mine],
                    self.send.at[k],
                    self.recv.at[k],
                    device_id=where,
                    device_id_type=MESH,
                )
            )
        return copies

    def step(self, k):
        n = len(self.plan)
        if 0 < k <= n:
            stage = k - 1
            group, before, after = self.plan[stage]
            held = self.source if stage == 0 else self.part[stage - 1]
            for copy in self.scatter(stage):
                copy.wait()
            own = held[...] if after == before else held[self.rows_at(group.place() * after, after)]
            self.landing[stage][group.place()] = own
            total = self.landing[stage][0]
            for j in range(1, group.count):
                total = total + self.landing[stage][j]
            self.part[stage][...] = total
            if stage == n - 1:
                self.whole[self.rows_at(self.offsets()[n], after)] = total
        elif k > n:
            for copy in self.gather(2 * n - k):
                copy.wait()
        if k < n:
            for copy in self.scatter(k):
                copy.start()
        elif k < 2 * n:
            for copy in self.gather(2 * n - 1 - k):
                copy.start()


def greet(groups, sides):
    barrier = pltpu.get_barrier_semaphore()
    expected = 0
    for group in groups:
        for step in range(1, group.count):
            pl.semaphore_signal(barrier, inc=1, device_id=group.peer(step)[1], device_id_type=MESH)
            expected = expected + 1
    for where, there in sides:
        expected = expected + there.astype(jnp.int32)

        @pl.when(there)
        def _(where=where):
            pl.semaphore_signal(barrier, inc=1, device_id=where, device_id_type=MESH)

    return expected


def running(block):
    row = iota(block.shape, 0)
    for shift in (1, 2, 4):
        block = block + jnp.where(row >= shift, pltpu.roll(block, shift, 0), 0.0)
    return block


def running_back(block):
    row = iota(block.shape, 0)
    for shift in (1, 2, 4):
        block = block + jnp.where(row < 8 - shift, pltpu.roll(block, 8 - shift, 0), 0.0)
    return block


def total(block):
    return jnp.sum(block, 0, keepdims=True)


def pack(owned, net, choose_e, choose_d, big, encoder, middle, viewer, colour, scalars):
    def rounded(group, value):
        return jnp.where(owned[group], value, 0.0).astype(BF16)

    big[ROW_M : ROW_M + 256] = rounded(1, middle[net])
    views = rounded(2, viewer[:, net, :])
    big[ROW_V : ROW_V + 128, 0:128] = views[0:128]
    big[ROW_V : ROW_V + 128, 128:256] = views[128:256]
    row = rounded(4, scalars[net : net + 1]).astype(F32)
    block = iota((16, 256), 0)
    tail = jnp.concatenate([row[:, 768:], jnp.zeros((1, 124), F32)], 1)
    picked = jnp.where(block == 0, row[:, 512:768], jnp.where(block == 1, row[:, 256:512], 0.0))
    big[ROW_S : ROW_S + 16] = jnp.where(block == 2, tail, picked).astype(BF16)
    first = dot(choose_e, rounded(0, encoder[:, net, :]))
    first = jnp.where(iota((64, 256), 0) == 63, row[:, :256], first)
    big[ROW_E : ROW_E + 64] = first.astype(BF16)
    big[ROW_D : ROW_D + 32, 0:128] = dot(choose_d, views[256:]).astype(BF16)
    paint = jnp.concatenate([rounded(3, colour[:, net, :]).astype(F32), jnp.zeros((29, 128), F32)], 0)
    big[ROW_D : ROW_D + 32, 128:256] = paint.astype(BF16)
    big[ROW_D + 32 : ROWS] = jnp.zeros((ROWS - ROW_D - 32, 256), BF16)


def step_kernel(
    sizes, groups, plans, owners, camera, ray_mask, direction, target, levels, bins, anchors,
    encoder, middle, viewer, colour, scalars, result,
    enc, h1, h2, hv, raw, depth, back, hist, w_e, w_mt, w_v, w_vt, w_c, w_ct, bias, per_ray,
    g_c, g_r, turned, mine, halo, send, recv, leaving, entering, *sums,
):
    local, sums = sums[:7], sums[7:]
    tile_rows, tile_cols = camera.shape
    lanes = tile_rows * tile_cols
    cameras = anchors.shape[1]
    points = CHUNK * lanes
    per_chunk = CHUNK // GROUP
    tx, ty = lax.axis_index("tx"), lax.axis_index("ty")
    device = tx * sizes["ty"] + ty
    sides = (
        ({"tx": tx - 1}, tx > 0),
        ({"tx": tx + 1}, tx < sizes["tx"] - 1),
        ({"ty": ty - 1}, ty > 0),
        ({"ty": ty + 1}, ty < sizes["ty"] - 1),
    )
    sum_of = []
    at = 0
    for plan, least in plans:
        length = 4 + 2 * len(plan)
        sum_of.append(Sum(plan, least, sums[at : at + length]))
        at += length
    params, params_fine, counting = sum_of[:3]
    grads, grads_fine = sum_of[3:5], sum_of[5:7]
    expected = greet(groups, sides[:2])
    given = (encoder, middle, viewer, colour, scalars, levels, bins)
    inward = [pltpu.make_async_copy(x, here, entering.at[i]) for i, (x, here) in enumerate(zip(given, local))]
    for copy in inward:
        copy.start()
    for copy in inward[:5]:
        copy.wait()
    encoder, middle, viewer, colour, scalars, levels, bins = local

    choose_e = selector(64, encoder.shape[0], LPOS, 32, BF16)
    choose_d = selector(32, viewer.shape[0] - 256, LDIR, 16, BF16)
    trees = (encoder, middle, viewer, colour, scalars)
    owned = [[owners[net, group] == device for group in range(5)] for net in range(2)]
    pack(owned[0], 0, choose_e, choose_d, params.source, *trees)
    pl.semaphore_wait(pltpu.get_barrier_semaphore(), expected)
    params.step(0)

    tall = jnp.concatenate(
        [direction[k] for k in range(3)]
        + [target[k] for k in range(3)]
        + [ray_mask[...].astype(F32), camera[...].astype(F32)],
        0,
    )
    repeat = (iota((tile_cols, lanes), 1) % tile_cols == iota((tile_cols, lanes), 0)).astype(F32)
    wide = dot(tall, repeat, HIGH)
    keep = iota((tile_rows, lanes), 1) // tile_cols == iota((tile_rows, lanes), 0)
    rows = [
        jnp.sum(jnp.where(keep, wide[k * tile_rows : k * tile_rows + tile_rows], 0.0), 0, keepdims=True)
        for k in range(8)
    ]
    mask, camera_row = rows[6], rows[7]
    target_rows = rows[3:6]
    number = iota((128, lanes), 0)
    picks = camera_row == number.astype(F32)
    counting.source[...] = dot_nt(
        jnp.broadcast_to(mask, (8, lanes)).astype(BF16), (picks | (number == 127)).astype(BF16)
    )
    picks = picks.astype(F32)
    counting.step(0)
    pack(owned[1], 1, choose_e, choose_d, params_fine.source, *trees)

    centres = jnp.concatenate([anchors[...], jnp.zeros((3, 128 - cameras), F32)], 1)
    origin = dot(centres, picks, HIGH)
    basis = jnp.concatenate([origin] + rows[0:3] + [jnp.zeros((2, lanes), F32)], 0)
    row8 = iota((8, lanes), 0)
    row32 = iota((32, lanes), 0)
    lift = iota((40, 8), 0)
    third = jnp.where(lift < 32, lift % 3, jnp.where(lift == 38, 2, -9))
    o_all = dot((third == iota((40, 8), 1)).astype(F32), basis, HIGH)
    d_all = dot((third + 3 == iota((40, 8), 1)).astype(F32), basis, HIGH)
    o_main, d_main = o_all[:32], d_all[:32]
    o_last, d_last = jnp.where(row8 == 7, 1.0 / shrink, o_all[32:]), d_all[32:]
    half_pi = jnp.float32(math.pi) * 0.5
    scale = jnp.zeros((32, lanes), F32)
    for level in range(LPOS):
        scale = jnp.where((row32 >= 3 * level) & (row32 < 3 * level + 3), half_pi * (2.0**level), scale)

    row16 = iota((16, lanes), 0)
    scale_d = scale[:16]
    sin_d, cos_d = sin_cos_twice(d_main[:16] * scale_d)
    top = jnp.where(row16 >= 12, jnp.where(row16 < 15, d_main[:16], 0.0), sin_d)
    bottom = jnp.where(row16 >= 12, jnp.where(row16 == 12, 1.0, 0.0), cos_d)
    view_code = jnp.concatenate([top, bottom], 0).astype(BF16)

    for copy in inward[5:]:
        copy.wait()
    samples_fine = levels.shape[1]
    blocks_of = (SC // GROUP, samples_fine // GROUP)
    first_block = (0, blocks_of[0])
    for b in range(blocks_of[0]):
        depth[b] = near_plane + (far_plane - near_plane) * ((row8 + b * GROUP).astype(F32) + 0.5) / SC
    levels_turned = levels[...].astype(F32).T
    for b in range(blocks_of[1]):
        at = levels_turned[b * GROUP : b * GROUP + GROUP]
        depth[blocks_of[0] + b] = near_plane + (far_plane - near_plane) * (at + 0.5) / NT
    bins_turned = bins[...].astype(F32).T

    def encode(b, carry):
        for s in range(GROUP):
            t = depth[b, s : s + 1]
            place = (o_main + t * d_main) * shrink
            wave, cowave = sin_cos_twice(place * scale)
            wave = jnp.where(row32 >= 30, place, wave)
            extra = (o_last + t * d_last) * shrink
            end = jnp.where(row8 >= 6, extra, cowave[24:])
            cowave = jnp.concatenate([cowave[:24], end], 0)
            enc[b, 0:32, s * lanes : s * lanes + lanes] = wave.astype(BF16)
            enc[b, 32:64, s * lanes : s * lanes + lanes] = cowave.astype(BF16)
        return carry

    all_blocks = sum(blocks_of)
    done = 0
    for k in range(1, params.steps):
        until = all_blocks * PACE[min(k, len(PACE) - 1)] // PACE[-1]
        if until > done:
            lax.fori_loop(done, until, encode, 0)
        done = until
        params.step(k)
        if k < counting.steps:
            counting.step(k)

    count = counting.whole[...]
    mask_floor = jnp.maximum(count[0:1, 127:128], 1.0)
    inverse = 1.0 / jnp.maximum(count, 1.0)
    ray_weight = dot(inverse, picks, HIGH)[0:1] * mask / cameras
    ones = jnp.full((16, points), 1.0, BF16)
    loss = jnp.zeros((1, lanes), F32)

    chunks_of = [n // per_chunk for n in blocks_of]

    def at_chunks(moved, pairs, over):
        return [(part, k, over * eighth // 8) for k, eighth in pairs for part in moved]

    half = params.steps // 2
    beside = {
        (0, "forward"): at_chunks([params_fine], [(0, 0), (1, 2), (2, 6)][:half], chunks_of[0]),
        (0, "backward"): at_chunks([params_fine], [(k, min(2 + 4 * (k > half + 1), 6)) for k in range(half, params.steps - 1)], chunks_of[0]),
        (1, "forward"): at_chunks(grads, [(0, 0), (1, 1), (2, 4), (3, 7)][: half + 1], chunks_of[1]),
        (1, "backward"): at_chunks(grads, [(k, min(1 + 2 * (k - half - 1), 7)) for k in range(half + 1, params.steps)], chunks_of[1]),
    }

    def send_on(net, name, c):
        for spot in sorted({spot for _, _, spot in beside[(net, name)]}):

            @pl.when(c == spot)
            def _(spot=spot):
                for moved, k, where in beside[(net, name)]:
                    if where == spot:
                        moved.step(k)

    for net in range(2):
        blocks, first, chunks = blocks_of[net], first_block[net], chunks_of[net]
        held = (params, params_fine)[net].whole
        w_mt[...] = held[ROW_M : ROW_M + 256].astype(F32).T.astype(BF16)
        misc32 = held[ROW_S : ROW_S + 16].astype(F32)
        row = iota((16, 256), 0)
        views = held[ROW_V : ROW_V + 128]
        w_vt[0:128, 0:128] = views[:, 0:128]
        w_vt[128:256, 0:128] = views[:, 128:256]
        w_v[0:128, 0:128] = views[:, 0:128].astype(F32).T.astype(BF16)
        w_v[0:128, 128:256] = views[:, 128:256].astype(F32).T.astype(BF16)
        w_v[128:144] = jnp.where(row == 0, misc32, 0.0).astype(BF16)
        sigma_t = jnp.concatenate([jnp.zeros((3, 256), F32), misc32[0:1], jnp.zeros((124, 256), F32)], 0).T
        w_vt[:, 128:144] = sigma_t[:, :16].astype(BF16)
        w_e[...] = held[ROW_E : ROW_E + 64].astype(F32).T.astype(BF16)
        last = held[ROW_D : ROW_D + 32].astype(F32)
        paint = last[:16, 128:]
        tail = misc32[2:3]
        sigma_bias = tail[:, 0:1]
        lane = iota((16, 128), 1)
        row_c = iota((16, 128), 0)
        tint_bias = jnp.zeros((16, 128), F32)
        for k in range(3):
            tint_bias = jnp.where((row_c == k) & (lane == 0), tail[:, 129 + k : 130 + k], tint_bias)
        w_c[:, 0:128] = paint.astype(BF16)
        w_c[:, 128:144] = tint_bias[:, :16].astype(BF16)
        w_ct[...] = jnp.concatenate([paint, jnp.zeros((112, 128), F32)], 0).T[:, :16].astype(BF16)
        bias[...] = jnp.broadcast_to(misc32[1:2], (128, 256)).T
        views_d = last[:, :128]
        shifted = pltpu.roll(jnp.broadcast_to(tail, (8, 256)), 255, 1)[0:1, :128]
        views_d = jnp.where(iota((32, 128), 0) == 28, shifted, views_d)
        per_ray[...] = dot_tn(views_d.astype(BF16), view_code)

        def code_of(c):
            start = first + c * per_chunk
            return jnp.concatenate([enc[start + i] for i in range(per_chunk)], 1)

        def forward(c, carry):
            send_on(net, "forward", c)
            one = jnp.maximum(dot(w_e[...], code_of(c)).astype(BF16), 0)
            h1[c] = one
            two = dot(held[ROW_M : ROW_M + 256], one) + jnp.tile(bias[...], (1, points // 128))
            two = jnp.maximum(two.astype(BF16), 0)
            h2[c] = two
            out = dot(w_v[...], two)
            view = out[:128] + jnp.tile(per_ray[...], (1, CHUNK))
            view = jnp.maximum(view.astype(BF16), 0)
            hv[c] = view
            paint = dot(w_c[...], jnp.concatenate([view, ones], 0))
            for s in range(CHUNK):
                part = slice(s * lanes, s * lanes + lanes)
                b, r = c * per_chunk + s // GROUP, s % GROUP
                for k in range(3):
                    raw[k, b, r : r + 1] = paint[k : k + 1, part]
                raw[3, b, r : r + 1] = out[128:129, part]
            return carry

        lax.fori_loop(0, chunks, forward, 0)

        before = jnp.zeros((1, lanes), F32)
        shade = [jnp.zeros((8, lanes), F32) for _ in range(3)]
        far, opaque = jnp.zeros((8, lanes), F32), jnp.zeros((8, lanes), F32)

        def spacing(b):
            t = depth[first + b]
            after = depth[first + b + 1, 0:1] if b + 1 < blocks else jnp.full((1, lanes), far_plane, F32)
            return jnp.where(row8 == 7, after, pltpu.roll(t, 7, 0)) - t

        for b in range(blocks):
            zs = raw[3, b] + sigma_bias
            density = jnp.maximum(zs, 0.0) + jnp.log1p(jnp.exp(-jnp.abs(zs)))
            q = density * spacing(b)
            inclusive = running(q) + before
            before = inclusive[7:8]
            lit = jnp.exp(-(inclusive - q))
            w = lit * (1.0 - jnp.exp(-q))
            back[0, b] = w
            back[1, b] = jnp.exp(-inclusive)
            if net == 1:
                back[3, b] = density * mask
            for k in range(3):
                tint = jax.nn.sigmoid(raw[k, b])
                raw[k, b] = tint
                shade[k] = shade[k] + w * tint
            far = far + w * depth[first + b]
            opaque = opaque + w
        shade = [total(x) for x in shade]
        far, opaque = total(far), total(opaque)
        miss = [shade[k] - target_rows[k] for k in range(3)]
        loss = loss + ray_weight * (miss[0] * miss[0] + miss[1] * miss[1] + miss[2] * miss[2])
        seed = [2.0 * ray_weight * miss[k] for k in range(3)]
        seed_depth = seed_opaque = None
        if net == 1:
            for k in range(3):
                mine[k : k + 1] = shade[k]
            mine[3:4] = far
            mine[4:5] = mask
            mine[5:8] = jnp.zeros((3, lanes), F32)

            def across(i, slot):
                return pltpu.make_async_remote_copy(
                    mine, halo.at[slot], send.at[i], recv.at[slot], device_id=sides[i][0], device_id_type=MESH
                )

            for i in range(4):
                pl.when(sides[i][1])(lambda i=i: across(i, i).start())

            def count_bin(b, carry):
                sums = jnp.zeros((8, lanes), F32)
                for s in range(blocks):
                    sums = sums + jnp.where(bins_turned[s * GROUP : s * GROUP + GROUP] == b.astype(F32), back[3, s], 0.0)
                folded = sums[:, :128]
                for k in range(1, lanes // 128):
                    folded = folded + sums[:, k * 128 : k * 128 + 128]
                hist[b] = total(folded)
                return carry

            lax.fori_loop(0, NHIST, count_bin, 0)
            binned = dot_nt(jnp.full((8, 128), 1.0, F32), jnp.sum(hist[...], 1), HIGH)[0:1] / mask_floor
            solid = 0.01 + 0.98 * opaque
            entropy = -mask * (solid * jnp.log(solid) + (1.0 - solid) * jnp.log(1.0 - solid))
            seed_opaque = -(entropy_weight / mask_floor) * mask * 0.98 * (jnp.log(solid) - jnp.log(1.0 - solid))
            for i in range(4):
                @pl.when(sides[i][1])
                def _(i=i):
                    across(i, i).wait_send()
                    across(i, i ^ 1).wait_recv()

            values = mine[...]
            lane = iota((8, lanes), 1)
            col, tile_row = lane % tile_cols, lane // tile_cols

            def beyond(i, inner, shift, wrap):
                other = jnp.where(
                    inner, pltpu.roll(values, shift % lanes, 1), pltpu.roll(halo[i ^ 1], wrap % lanes, 1)
                )
                return jnp.where(inner | sides[i][1], other, 0.0)

            smooth = jnp.zeros((8, lanes), F32)
            pull = jnp.zeros((8, lanes), F32)
            for i, inner, shift, wrap in (
                (0, col > 0, 1, 1 - tile_cols),
                (1, col < tile_cols - 1, -1, tile_cols - 1),
                (2, tile_row > 0, tile_cols, tile_cols - lanes),
                (3, tile_row < tile_rows - 1, -tile_cols, lanes - tile_cols),
            ):
                other = beyond(i, inner, shift, wrap)
                pair = other[4:5] * mask
                gap = jnp.where(row8 < 4, values - other, 0.0)
                pull = pull + pair * gap
                if i % 2 == 1:
                    smooth = smooth + pair * gap * gap
            pull = (2.0 * smooth_weight / mask_floor) * pull
            seed = [seed[k] + pull[k : k + 1] for k in range(3)]
            seed_depth = pull[3:4]
            loss = loss + (smooth_weight * total(smooth) + entropy_weight * entropy) / mask_floor

        later = jnp.zeros((1, lanes), F32)
        for b in reversed(range(blocks)):
            w, passed = back[0, b], back[1, b]
            tint = [raw[k, b] for k in range(3)]
            pulled = seed[0] * tint[0] + seed[1] * tint[1] + seed[2] * tint[2]
            if net == 1:
                pulled = pulled + seed_depth * depth[first + b] + seed_opaque
            weighted = pulled * w
            onward = running_back(weighted) + later
            later = onward[0:1]
            dq = pulled * passed - (onward - weighted)
            back[3, b] = dq * spacing(b) * jax.nn.sigmoid(raw[3, b] + sigma_bias)
            for k in range(3):
                back[k, b] = w * seed[k] * tint[k] * (1.0 - tint[k])

        upper, lower = [part.source for part in (grads, grads_fine)[net]]
        g_m = upper
        g_v, g_e = lower.at[ROW_V - 256 : ROW_V - 112], lower.at[ROW_E - 256 : ROW_E - 192]
        for ref in (upper, lower, g_c, g_r):
            ref[...] = jnp.zeros_like(ref)

        def backward(c, carry):
            send_on(net, "backward", c)
            parts = []
            for s in range(CHUNK):
                b, r = c * per_chunk + s // GROUP, s % GROUP
                parts.append(jnp.concatenate([back[k, b, r : r + 1] for k in range(4)] + [jnp.zeros((12, lanes), F32)], 0))
            gate = jnp.concatenate(parts, 1).astype(BF16)
            view = hv[c]
            gv = jnp.where(view > 0, dot(w_ct[...], gate).astype(BF16), 0)
            sums = g_r[...]
            for s in range(CHUNK):
                sums = sums + gv[:, s * lanes : s * lanes + lanes].astype(F32)
            g_r[...] = sums
            g_c[...] += dot_nt(jnp.concatenate([view, ones], 0), gate)
            both = jnp.concatenate([gv, gate], 0)
            two = h2[c]
            turned[...] = two.T
            g_v[...] += dot(both, turned[...])
            g2 = jnp.where(two > 0, dot(w_vt[...], both).astype(BF16), 0)
            one = h1[c]
            g_m[...] += dot_nt(jnp.concatenate([one, ones], 0), g2)
            g1 = jnp.where(one > 0, dot(w_mt[...], g2).astype(BF16), 0)
            turned[...] = g1.T
            g_e[...] += dot(code_of(c), turned[...])
            return carry

        lax.fori_loop(0, chunks, backward, 0)
        if net == 0:
            params_fine.step(params.steps - 1)

        tints = jnp.concatenate([g_c[...], jnp.zeros((144, 112), F32)], 1)
        tints, sums_c = tints[:128].T[:16], tints[128:136].T[:16, 0:1]
        lane = iota((16, 256), 1)
        grad_misc = jnp.where(row == 0, lower[131:132], jnp.where(row == 1, upper[256:257], 0.0))
        for k, spot in ((3, 0), (0, 129), (1, 130), (2, 131)):
            grad_misc = jnp.where((row == 2) & (lane == spot), sums_c[k : k + 1], grad_misc)
        lower[ROW_S - 256 : ROW_S - 240] = grad_misc
        lower[ROW_D - 256 : ROW_D - 224, 0:128] = dot_nt(view_code.astype(F32), g_r[...], HIGH)
        lower[ROW_D - 256 : ROW_D - 224, 128:256] = jnp.concatenate([tints, jnp.zeros((16, 128), F32)], 0)
    rest = grads_fine[1].source
    rest[ROW_D - 224 : ROW_D - 223, 0:NHIST] = binned
    fold = loss[:, :128]
    for k in range(1, lanes // 128):
        fold = fold + loss[:, k * 128 : k * 128 + 128]
    rest[ROW_D - 223 : ROW_D - 222, 0:128] = fold
    for k in range(params.steps):
        for part in grads_fine:
            part.step(k)
    outward = [
        pltpu.make_async_copy(part.whole, result.at[pl.ds(i * 256, 256)], leaving.at[i])
        for i, part in enumerate(grads + grads_fine)
    ]
    for copy in outward:
        copy.start()
    for copy in outward:
        copy.wait()


def adamw_update(weight, moment, square, gradient):
    moment_next = beta_first * moment + (1.0 - beta_first) * gradient
    square_next = beta_second * square + (1.0 - beta_second) * gradient * gradient
    first_hat = moment_next / (1.0 - beta_first**step_count)
    second_hat = square_next / (1.0 - beta_second**step_count)
    weight_next = weight - learn_rate * (
        first_hat / (jnp.sqrt(second_hat) + adam_epsilon) + decay_rate * weight
    )
    return (weight_next, moment_next, square_next)


def update_kernel(tiles_y, owners, grads, *refs):
    given, loss, histogram, taken = refs[0:15], refs[15], refs[16], refs[17:32]
    held, arrived, left = refs[32:47], refs[47], refs[48]
    device = lax.axis_index("tx") * tiles_y + lax.axis_index("ty")
    order = (1, 2, 0, 4, 3)
    for group in order:
        for i in (group, group + 5, group + 10):
            pltpu.make_async_copy(given[i], held[i], arrived.at[i]).start()
    histogram[...] = grads[ROWS + ROW_D + 32 : ROWS + ROW_D + 33, 0:NHIST]
    loss[...] = jnp.sum(grads[ROWS + ROW_D + 33 : ROWS + ROW_D + 34, 0:128], 1, keepdims=True)

    def step(group, at, gradient):
        trio = (held[group], held[group + 5], held[group + 10])
        for ref, now in zip(trio, adamw_update(*[ref[at] for ref in trio], gradient)):
            ref[at] = now

    every = slice(None)

    def update(group, net):
        base = net * ROWS
        last = grads[base + ROW_D : base + ROW_D + 32]
        if group == 0:
            choose = selector(64, held[0].shape[0], LPOS, 32, F32)
            step(0, (every, net, every), dot_tn(choose, grads[base + ROW_E : base + ROW_E + 64], HIGH))
        elif group == 1:
            step(1, (net,), grads[base + ROW_M : base + ROW_M + 256].T)
        elif group == 2:
            views = grads[base + ROW_V : base + ROW_V + 128]
            step(2, (slice(0, 128), net, every), views[:, 0:128].T)
            step(2, (slice(128, 256), net, every), views[:, 128:256].T)
            rest = slice(256, held[2].shape[0])
            choose = selector(32, held[2].shape[0] - 256, LDIR, 16, F32)
            step(2, (rest, net, every), dot_tn(choose, last[:, :128], HIGH))
        elif group == 3:
            step(3, (every, net, every), last[0:3, 128:])
        else:
            misc = grads[base + ROW_S : base + ROW_S + 16]
            spot = slice(net, net + 1)
            step(4, (spot, slice(0, 256)), grads[base + ROW_E + 63 : base + ROW_E + 64])
            step(4, (spot, slice(256, 512)), misc[1:2])
            step(4, (spot, slice(512, 768)), misc[0:1])
            bias = jnp.concatenate([last[28:29, :128], jnp.zeros((1, 128), F32)], 1)
            bias = pltpu.roll(jnp.broadcast_to(bias, (8, 256)), 1, 1)[0:1]
            step(4, (spot, slice(768, 900)), (misc[2:3] + bias)[:, :132])

    for group in order:
        trio = (group, group + 5, group + 10)
        for i in trio:
            pltpu.make_async_copy(given[i], held[i], arrived.at[i]).wait()
        for net in range(2):
            pl.when(owners[net, group] == device)(functools.partial(update, group, net))
        for i in trio:
            pltpu.make_async_copy(held[i], taken[i], left.at[i]).start()
    for i in range(15):
        pltpu.make_async_copy(held[i], taken[i], left.at[i]).wait()


ANY_SPEC = pl.BlockSpec(memory_space=pl.ANY)
VMEM_SPEC = pl.BlockSpec(memory_space=pltpu.VMEM)
SMEM_SPEC = pl.BlockSpec(memory_space=pltpu.SMEM)


def per_device(sizes, camera, ray_mask, ray_direction, anchors, target, fine_levels, density_bins, owners, *trees):
    turns = ((2, 0, 1), (0, 1, 2), (2, 0, 1), (1, 0, 2), (0, 1))
    states = [jnp.transpose(x[0], turns[i % 5]) for i, x in enumerate(trees)]
    lanes = camera.shape[0] * camera.shape[1]
    samples = fine_levels.shape[0]
    levels = jnp.transpose(fine_levels, (1, 2, 0)).reshape(lanes, samples)
    bins = jnp.transpose(density_bins, (1, 2, 0)).reshape(lanes, samples)

    groups = groups_of(sizes)
    turned_round = groups[:1] + groups[:0:-1]
    param_plan = plan_of(groups, ROWS, 16, groups[2:])
    upper, lower = plan_of(groups, 256, 8, groups[2:]), plan_of(turned_round, 256, 8, turned_round[2:])
    plans = [(param_plan, 16), (param_plan, 16), (plan_of(groups, 8, 8, groups), 8)]
    plans += [(upper, 8), (lower, 8)] * 2
    sums = []
    kinds = [(BF16, 256, 0)] * 2 + [(F32, 128, 0)] + [(F32, 256, 16), (F32, 256, 0)] * 2
    for (plan, _), kind in zip(plans, kinds):
        sums += sum_scratch(plan, *kind)
    points = CHUNK * lanes
    chunks = samples // CHUNK
    blocks = samples // GROUP
    grads = pl.pallas_call(
        functools.partial(step_kernel, sizes, groups, plans),
        out_shape=jax.ShapeDtypeStruct((2 * ROWS, 256), F32),
        in_specs=[SMEM_SPEC] + [VMEM_SPEC] * 4 + [ANY_SPEC] * 2 + [VMEM_SPEC] + [ANY_SPEC] * 5,
        out_specs=ANY_SPEC,
        scratch_shapes=[
            pltpu.VMEM((blocks + SC // GROUP, 64, GROUP * lanes), BF16),
            pltpu.VMEM((chunks, 256, points), BF16),
            pltpu.VMEM((chunks, 256, points), BF16),
            pltpu.VMEM((chunks, 128, points), BF16),
            pltpu.VMEM((4, blocks, GROUP, lanes), F32),
            pltpu.VMEM((blocks + SC // GROUP, GROUP, lanes), F32),
            pltpu.VMEM((4, blocks, GROUP, lanes), F32),
            pltpu.VMEM((NHIST, 1, 128), F32),
            pltpu.VMEM((256, 64), BF16),
            pltpu.VMEM((256, 256), BF16),
            pltpu.VMEM((144, 256), BF16),
            pltpu.VMEM((256, 144), BF16),
            pltpu.VMEM((16, 144), BF16),
            pltpu.VMEM((128, 16), BF16),
            pltpu.VMEM((256, 128), F32),
            pltpu.VMEM((128, lanes), F32),
            pltpu.VMEM((144, 16), F32),
            pltpu.VMEM((128, lanes), F32),
            pltpu.VMEM((points, 256), BF16),
            pltpu.VMEM((8, lanes), F32),
            pltpu.VMEM((4, 8, lanes), F32),
            pltpu.SemaphoreType.DMA((4,)),
            pltpu.SemaphoreType.DMA((4,)),
            pltpu.SemaphoreType.DMA((4,)),
            pltpu.SemaphoreType.DMA((7,)),
        ]
        + [pltpu.VMEM(x.shape, x.dtype) for x in states[:5] + [levels, bins]]
        + sums,
        compiler_params=pltpu.CompilerParams(collective_id=0, has_side_effects=True, vmem_limit_bytes=LIMIT),
        name="step",
    )(owners.T, camera, ray_mask, ray_direction, target, levels, bins, anchors, *states[:5])

    results = pl.pallas_call(
        functools.partial(update_kernel, sizes["ty"]),
        out_shape=[jax.ShapeDtypeStruct((1, 1), F32), jax.ShapeDtypeStruct((1, NHIST), F32)]
        + [jax.ShapeDtypeStruct(x.shape, F32) for x in states],
        in_specs=[SMEM_SPEC, VMEM_SPEC] + [ANY_SPEC] * 15,
        out_specs=[VMEM_SPEC] * 2 + [ANY_SPEC] * 15,
        scratch_shapes=[pltpu.VMEM(x.shape, F32) for x in states]
        + [pltpu.SemaphoreType.DMA((15,)), pltpu.SemaphoreType.DMA((15,))],
        name="update",
    )(owners.T, grads, *states)
    turned = []
    for i, x in enumerate(results[2:]):
        turn = turns[i % 5]
        turned.append(jnp.transpose(x, [turn.index(d) for d in range(len(turn))])[None])
    return (results[0].reshape(()), results[1].reshape(NHIST)) + tuple(turned)


def solution(mesh):
    sizes = dict(mesh.shape)
    tiled, tiled3 = P("ty", "tx"), P(None, "ty", "tx")
    slots = P(("tx", "ty"), None, None, None)
    trees = (slots, slots, slots, slots, P(("tx", "ty"), None, None))
    return jax.shard_map(
        functools.partial(per_device, sizes),
        mesh=mesh,
        in_specs=(tiled, tiled, tiled3, P(), tiled3, tiled3, tiled3, P()) + trees * 3,
        out_specs=(P(), P()) + trees * 3,
        check_vma=False,
    )
```

```python
import functools
import math

import jax
import jax.numpy as jnp
from jax import lax
from jax.experimental import pallas as pl
from jax.experimental.pallas import tpu as pltpu
from jax.sharding import PartitionSpec as P

LPOS = 10
LDIR = 4
SC = 64
NT = 1024
NHIST = 64

near_plane = 2.0
far_plane = 6.0
shrink = 0.125
smooth_weight = 0.1
entropy_weight = 0.1
beta_first = 0.9
beta_second = 0.999
adam_epsilon = 1e-08
decay_rate = 0.01
learn_rate = 0.05
step_count = 10

MESH = pl.DeviceIdType.MESH
F32 = jnp.float32
BF16 = jnp.bfloat16
HIGH = lax.Precision.HIGHEST
GROUP = 8
CHUNK = 16
ROWS = 512
LIMIT = 67_000_000
PACE = (0, 0, 7, 19, 19, 24, 24)

ROW_M, ROW_V, ROW_S, ROW_E, ROW_D = 0, 256, 384, 400, 464

PI_A = 3.140625
PI_B = 0.0009670257568359375
PI_C = math.pi - PI_A - PI_B
SIN = (-0.16666656732559204, 0.008333015255630016, -0.00019806479394901544, 2.5997517241194146e-06)
COS = (-0.5, 0.04166664183139801, -0.0013888400280848145, 2.4761729946476407e-05, -2.607421833999979e-07)


def dot(a, b, precision=None):
    return lax.dot_general(a, b, (((1,), (0,)), ((), ())), preferred_element_type=F32, precision=precision)


def dot_nt(a, b, precision=None):
    return lax.dot_general(a, b, (((1,), (1,)), ((), ())), preferred_element_type=F32, precision=precision)


def dot_tn(a, b, precision=None):
    return lax.dot_general(a, b, (((0,), (0,)), ((), ())), preferred_element_type=F32, precision=precision)


def iota(shape, axis):
    return lax.broadcasted_iota(jnp.int32, shape, axis)


def sin_cos_twice(y):
    k = jnp.round(y * (1.0 / math.pi))
    y = ((y - k * PI_A) - k * PI_B) - k * PI_C
    t = y * y
    s = y * (1.0 + t * (SIN[0] + t * (SIN[1] + t * (SIN[2] + t * SIN[3]))))
    c = 1.0 + t * (COS[0] + t * (COS[1] + t * (COS[2] + t * (COS[3] + t * COS[4]))))
    d = s + s
    return d * c, 1.0 - d * s


def code_column(row, levels, pad):
    half = row % pad
    third = 3 * levels
    wave = 3 + 6 * (half // 3) + half % 3 + jnp.where(row >= pad, 3, 0)
    if levels == LPOS:
        rest = jnp.where(row == 30, 0, jnp.where(row == 31, 1, jnp.where(row == 62, 2, -1)))
    else:
        rest = jnp.where((row >= 12) & (row < 15), row - 12, jnp.where(row == 28, -1, -2))
    return jnp.where(half < third, wave, rest)


def selector(rows, columns, levels, pad, dtype):
    return (iota((rows, columns), 1) == code_column(iota((rows, columns), 0), levels, pad)).astype(dtype)


class Members:
    def __init__(self, axis, count, spread):
        self.axis, self.count, self.spread = axis, count, spread

    def place(self):
        return (lax.axis_index(self.axis) // self.spread) % self.count

    def peer(self, step):
        me = self.place()
        other = (me + step) % self.count
        return other, {self.axis: lax.axis_index(self.axis) + (other - me) * self.spread}


def groups_of(sizes):
    cores = 2 if sizes["tx"] % 2 == 0 else 1
    groups = [Members("tx", cores, 1), Members("ty", sizes["ty"], 1), Members("tx", sizes["tx"] // cores, cores)]
    return [g for g in groups if g.count > 1]


def plan_of(groups, rows, least, whole=()):
    plan = []
    for group in groups:
        after = rows // group.count if rows % (group.count * least) == 0 and group not in whole else rows
        plan.append((group, rows, after))
        rows = after
    return plan


def sum_scratch(plan, dtype, width, beyond):
    copies = sum(group.count - 1 for group, _, _ in plan)
    rows = plan[0][1]
    return (
        [pltpu.VMEM((rows + beyond, width), dtype), pltpu.VMEM((rows, width), dtype)]
        + [pltpu.VMEM((group.count, after, width), dtype) for group, _, after in plan]
        + [pltpu.VMEM((after, width), dtype) for _, _, after in plan]
        + [pltpu.SemaphoreType.DMA((2 * copies,)), pltpu.SemaphoreType.DMA((2 * copies,))]
    )


class Sum:
    def __init__(self, plan, least, refs):
        n = len(plan)
        self.plan, self.least = plan, least
        self.source, self.whole = refs[0], refs[1]
        self.landing, self.part = refs[2 : 2 + n], refs[2 + n : 2 + 2 * n]
        self.send, self.recv = refs[2 + 2 * n :]
        self.steps = 2 * n + 1

    def rows_at(self, start, length):
        return pl.ds(pl.multiple_of(start, self.least), length)

    def offsets(self):
        at, result = 0, [0]
        for group, before, after in self.plan:
            if after != before:
                at = at + group.place() * after
            result.append(at)
        return result

    def base(self, stage, back):
        copies = [group.count - 1 for group, _, _ in self.plan]
        return sum(copies[:stage]) + (sum(copies) if back else 0)

    def scatter(self, stage):
        group, before, after = self.plan[stage]
        held = self.source if stage == 0 else self.part[stage - 1]
        copies = []
        for step in range(1, group.count):
            other, where = group.peer(step)
            k = self.base(stage, False) + step - 1
            piece = held if after == before else held.at[self.rows_at(other * after, after)]
            copies.append(
                pltpu.make_async_remote_copy(
                    piece,
                    self.landing[stage].at[group.place()],
                    self.send.at[k],
                    self.recv.at[k],
                    device_id=where,
                    device_id_type=MESH,
                )
            )
        return copies

    def gather(self, stage):
        group, before, after = self.plan[stage]
        if after == before:
            return []
        mine = self.rows_at(self.offsets()[stage + 1], after)
        copies = []
        for step in range(1, group.count):
            _, where = group.peer(step)
            k = self.base(stage, True) + step - 1
            copies.append(
                pltpu.make_async_remote_copy(
                    self.whole.at[mine],
                    self.whole.at[mine],
                    self.send.at[k],
                    self.recv.at[k],
                    device_id=where,
                    device_id_type=MESH,
                )
            )
        return copies

    def step(self, k):
        n = len(self.plan)
        if 0 < k <= n:
            stage = k - 1
            group, before, after = self.plan[stage]
            held = self.source if stage == 0 else self.part[stage - 1]
            for copy in self.scatter(stage):
                copy.wait()
            own = held[...] if after == before else held[self.rows_at(group.place() * after, after)]
            self.landing[stage][group.place()] = own
            total = self.landing[stage][0]
            for j in range(1, group.count):
                total = total + self.landing[stage][j]
            self.part[stage][...] = total
            if stage == n - 1:
                self.whole[self.rows_at(self.offsets()[n], after)] = total
        elif k > n:
            for copy in self.gather(2 * n - k):
                copy.wait()
        if k < n:
            for copy in self.scatter(k):
                copy.start()
        elif k < 2 * n:
            for copy in self.gather(2 * n - 1 - k):
                copy.start()


def greet(groups, sides):
    barrier = pltpu.get_barrier_semaphore()
    expected = 0
    for group in groups:
        for step in range(1, group.count):
            pl.semaphore_signal(barrier, inc=1, device_id=group.peer(step)[1], device_id_type=MESH)
            expected = expected + 1
    for where, there in sides:
        expected = expected + there.astype(jnp.int32)

        @pl.when(there)
        def _(where=where):
            pl.semaphore_signal(barrier, inc=1, device_id=where, device_id_type=MESH)

    return expected


def running(block):
    row = iota(block.shape, 0)
    for shift in (1, 2, 4):
        block = block + jnp.where(row >= shift, pltpu.roll(block, shift, 0), 0.0)
    return block


def running_back(block):
    row = iota(block.shape, 0)
    for shift in (1, 2, 4):
        block = block + jnp.where(row < 8 - shift, pltpu.roll(block, 8 - shift, 0), 0.0)
    return block


def total(block):
    return jnp.sum(block, 0, keepdims=True)


def pack(owned, net, choose_e, choose_d, big, encoder, middle, viewer, colour, scalars):
    def rounded(group, value):
        return jnp.where(owned[group], value, 0.0).astype(BF16)

    big[ROW_M : ROW_M + 256] = rounded(1, middle[net])
    views = rounded(2, viewer[:, net, :])
    big[ROW_V : ROW_V + 128, 0:128] = views[0:128]
    big[ROW_V : ROW_V + 128, 128:256] = views[128:256]
    row = rounded(4, scalars[net : net + 1]).astype(F32)
    block = iota((16, 256), 0)
    tail = jnp.concatenate([row[:, 768:], jnp.zeros((1, 124), F32)], 1)
    picked = jnp.where(block == 0, row[:, 512:768], jnp.where(block == 1, row[:, 256:512], 0.0))
    big[ROW_S : ROW_S + 16] = jnp.where(block == 2, tail, picked).astype(BF16)
    first = dot(choose_e, rounded(0, encoder[:, net, :]))
    first = jnp.where(iota((64, 256), 0) == 63, row[:, :256], first)
    big[ROW_E : ROW_E + 64] = first.astype(BF16)
    big[ROW_D : ROW_D + 32, 0:128] = dot(choose_d, views[256:]).astype(BF16)
    paint = jnp.concatenate([rounded(3, colour[:, net, :]).astype(F32), jnp.zeros((29, 128), F32)], 0)
    big[ROW_D : ROW_D + 32, 128:256] = paint.astype(BF16)
    big[ROW_D + 32 : ROWS] = jnp.zeros((ROWS - ROW_D - 32, 256), BF16)


def step_kernel(
    sizes, groups, plans, owners, camera, ray_mask, direction, target, levels, bins, anchors,
    encoder, middle, viewer, colour, scalars, result,
    enc, h1, h2, hv, raw, depth, back, hist, w_e, w_mt, w_v, w_vt, w_c, w_ct, bias, per_ray,
    g_c, g_r, turned, mine, halo, send, recv, leaving, entering, *sums,
):
    local, sums = sums[:13], sums[13:]
    tile_rows, tile_cols = camera.shape
    lanes = tile_rows * tile_cols
    cameras = anchors.shape[1]
    points = CHUNK * lanes
    per_chunk = CHUNK // GROUP
    tx, ty = lax.axis_index("tx"), lax.axis_index("ty")
    device = tx * sizes["ty"] + ty
    sides = (
        ({"tx": tx - 1}, tx > 0),
        ({"tx": tx + 1}, tx < sizes["tx"] - 1),
        ({"ty": ty - 1}, ty > 0),
        ({"ty": ty + 1}, ty < sizes["ty"] - 1),
    )
    sum_of = []
    at = 0
    for plan, least in plans:
        length = 4 + 2 * len(plan)
        sum_of.append(Sum(plan, least, sums[at : at + length]))
        at += length
    params, params_fine, counting = sum_of[:3]
    grads, grads_fine = sum_of[3:5], sum_of[5:7]
    expected = greet(groups, sides[:2])
    given = (
        owners, encoder, middle, viewer, colour, scalars,
        camera, ray_mask, direction, target, anchors, levels, bins,
    )
    inward = [pltpu.make_async_copy(x, here, entering.at[i]) for i, (x, here) in enumerate(zip(given, local))]
    for copy in inward:
        copy.start()
    for copy in inward[:6]:
        copy.wait()
    owners, encoder, middle, viewer, colour, scalars, camera, ray_mask, direction, target, anchors, levels, bins = local

    choose_e = selector(64, encoder.shape[0], LPOS, 32, BF16)
    choose_d = selector(32, viewer.shape[0] - 256, LDIR, 16, BF16)
    trees = (encoder, middle, viewer, colour, scalars)
    owned = [[owners[net, group] == device for group in range(5)] for net in range(2)]
    pack(owned[0], 0, choose_e, choose_d, params.source, *trees)
    pl.semaphore_wait(pltpu.get_barrier_semaphore(), expected)
    params.step(0)

    for copy in inward[6:]:
        copy.wait()
    tall = jnp.concatenate(
        [direction[k] for k in range(3)]
        + [target[k] for k in range(3)]
        + [ray_mask[...].astype(F32), camera[...].astype(F32)],
        0,
    )
    repeat = (iota((tile_cols, lanes), 1) % tile_cols == iota((tile_cols, lanes), 0)).astype(F32)
    wide = dot(tall, repeat, HIGH)
    keep = iota((tile_rows, lanes), 1) // tile_cols == iota((tile_rows, lanes), 0)
    rows = [
        jnp.sum(jnp.where(keep, wide[k * tile_rows : k * tile_rows + tile_rows], 0.0), 0, keepdims=True)
        for k in range(8)
    ]
    mask, camera_row = rows[6], rows[7]
    target_rows = rows[3:6]
    number = iota((128, lanes), 0)
    picks = camera_row == number.astype(F32)
    counting.source[...] = dot_nt(
        jnp.broadcast_to(mask, (8, lanes)).astype(BF16), (picks | (number == 127)).astype(BF16)
    )
    picks = picks.astype(F32)
    counting.step(0)
    pack(owned[1], 1, choose_e, choose_d, params_fine.source, *trees)

    centres = jnp.concatenate([anchors[...], jnp.zeros((3, 128 - cameras), F32)], 1)
    origin = dot(centres, picks, HIGH)
    basis = jnp.concatenate([origin] + rows[0:3] + [jnp.zeros((2, lanes), F32)], 0)
    row8 = iota((8, lanes), 0)
    row32 = iota((32, lanes), 0)
    lift = iota((40, 8), 0)
    third = jnp.where(lift < 32, lift % 3, jnp.where(lift == 38, 2, -9))
    o_all = dot((third == iota((40, 8), 1)).astype(F32), basis, HIGH)
    d_all = dot((third + 3 == iota((40, 8), 1)).astype(F32), basis, HIGH)
    o_main, d_main = o_all[:32], d_all[:32]
    o_last, d_last = jnp.where(row8 == 7, 1.0 / shrink, o_all[32:]), d_all[32:]
    half_pi = jnp.float32(math.pi) * 0.5
    scale = jnp.zeros((32, lanes), F32)
    for level in range(LPOS):
        scale = jnp.where((row32 >= 3 * level) & (row32 < 3 * level + 3), half_pi * (2.0**level), scale)

    row16 = iota((16, lanes), 0)
    scale_d = scale[:16]
    sin_d, cos_d = sin_cos_twice(d_main[:16] * scale_d)
    top = jnp.where(row16 >= 12, jnp.where(row16 < 15, d_main[:16], 0.0), sin_d)
    bottom = jnp.where(row16 >= 12, jnp.where(row16 == 12, 1.0, 0.0), cos_d)
    view_code = jnp.concatenate([top, bottom], 0).astype(BF16)

    samples_fine = levels.shape[1]
    blocks_of = (SC // GROUP, samples_fine // GROUP)
    first_block = (0, blocks_of[0])
    for b in range(blocks_of[0]):
        depth[b] = near_plane + (far_plane - near_plane) * ((row8 + b * GROUP).astype(F32) + 0.5) / SC
    levels_turned = levels[...].astype(F32).T
    for b in range(blocks_of[1]):
        at = levels_turned[b * GROUP : b * GROUP + GROUP]
        depth[blocks_of[0] + b] = near_plane + (far_plane - near_plane) * (at + 0.5) / NT
    bins_turned = bins[...].astype(F32).T

    def encode(b, carry):
        for s in range(GROUP):
            t = depth[b, s : s + 1]
            place = (o_main + t * d_main) * shrink
            wave, cowave = sin_cos_twice(place * scale)
            wave = jnp.where(row32 >= 30, place, wave)
            extra = (o_last + t * d_last) * shrink
            end = jnp.where(row8 >= 6, extra, cowave[24:])
            cowave = jnp.concatenate([cowave[:24], end], 0)
            enc[b, 0:32, s * lanes : s * lanes + lanes] = wave.astype(BF16)
            enc[b, 32:64, s * lanes : s * lanes + lanes] = cowave.astype(BF16)
        return carry

    all_blocks = sum(blocks_of)
    done = 0
    for k in range(1, params.steps):
        until = all_blocks * PACE[min(k, len(PACE) - 1)] // PACE[-1]
        if until > done:
            lax.fori_loop(done, until, encode, 0)
        done = until
        params.step(k)
        if k < counting.steps:
            counting.step(k)

    count = counting.whole[...]
    mask_floor = jnp.maximum(count[0:1, 127:128], 1.0)
    inverse = 1.0 / jnp.maximum(count, 1.0)
    ray_weight = dot(inverse, picks, HIGH)[0:1] * mask / cameras
    ones = jnp.full((16, points), 1.0, BF16)
    loss = jnp.zeros((1, lanes), F32)

    chunks_of = [n // per_chunk for n in blocks_of]

    def at_chunks(moved, pairs, over):
        return [(part, k, over * eighth // 8) for k, eighth in pairs for part in moved]

    half = params.steps // 2
    beside = {
        (0, "forward"): at_chunks([params_fine], [(0, 0), (1, 2), (2, 6)][:half], chunks_of[0]),
        (0, "backward"): at_chunks([params_fine], [(k, min(2 + 4 * (k > half + 1), 6)) for k in range(half, params.steps - 1)], chunks_of[0]),
        (1, "forward"): at_chunks(grads, [(0, 0), (1, 1), (2, 4), (3, 7)][: half + 1], chunks_of[1]),
        (1, "backward"): at_chunks(grads, [(k, min(1 + 2 * (k - half - 1), 7)) for k in range(half + 1, params.steps)], chunks_of[1]),
    }

    def send_on(net, name, c):
        for spot in sorted({spot for _, _, spot in beside[(net, name)]}):

            @pl.when(c == spot)
            def _(spot=spot):
                for moved, k, where in beside[(net, name)]:
                    if where == spot:
                        moved.step(k)

    for net in range(2):
        blocks, first, chunks = blocks_of[net], first_block[net], chunks_of[net]
        held = (params, params_fine)[net].whole
        w_mt[...] = held[ROW_M : ROW_M + 256].astype(F32).T.astype(BF16)
        misc32 = held[ROW_S : ROW_S + 16].astype(F32)
        row = iota((16, 256), 0)
        views = held[ROW_V : ROW_V + 128]
        w_vt[0:128, 0:128] = views[:, 0:128]
        w_vt[128:256, 0:128] = views[:, 128:256]
        w_v[0:128, 0:128] = views[:, 0:128].astype(F32).T.astype(BF16)
        w_v[0:128, 128:256] = views[:, 128:256].astype(F32).T.astype(BF16)
        w_v[128:144] = jnp.where(row == 0, misc32, 0.0).astype(BF16)
        sigma_t = jnp.concatenate([jnp.zeros((3, 256), F32), misc32[0:1], jnp.zeros((124, 256), F32)], 0).T
        w_vt[:, 128:144] = sigma_t[:, :16].astype(BF16)
        w_e[...] = held[ROW_E : ROW_E + 64].astype(F32).T.astype(BF16)
        last = held[ROW_D : ROW_D + 32].astype(F32)
        paint = last[:16, 128:]
        tail = misc32[2:3]
        sigma_bias = tail[:, 0:1]
        lane = iota((16, 128), 1)
        row_c = iota((16, 128), 0)
        tint_bias = jnp.zeros((16, 128), F32)
        for k in range(3):
            tint_bias = jnp.where((row_c == k) & (lane == 0), tail[:, 129 + k : 130 + k], tint_bias)
        w_c[:, 0:128] = paint.astype(BF16)
        w_c[:, 128:144] = tint_bias[:, :16].astype(BF16)
        w_ct[...] = jnp.concatenate([paint, jnp.zeros((112, 128), F32)], 0).T[:, :16].astype(BF16)
        bias[...] = jnp.broadcast_to(misc32[1:2], (128, 256)).T
        views_d = last[:, :128]
        shifted = pltpu.roll(jnp.broadcast_to(tail, (8, 256)), 255, 1)[0:1, :128]
        views_d = jnp.where(iota((32, 128), 0) == 28, shifted, views_d)
        per_ray[...] = dot_tn(views_d.astype(BF16), view_code)

        def code_of(c):
            start = first + c * per_chunk
            return jnp.concatenate([enc[start + i] for i in range(per_chunk)], 1)

        def forward(c, carry):
            send_on(net, "forward", c)
            one = jnp.maximum(dot(w_e[...], code_of(c)).astype(BF16), 0)
            h1[c] = one
            two = dot(held[ROW_M : ROW_M + 256], one) + jnp.tile(bias[...], (1, points // 128))
            two = jnp.maximum(two.astype(BF16), 0)
            h2[c] = two
            out = dot(w_v[...], two)
            view = out[:128] + jnp.tile(per_ray[...], (1, CHUNK))
            view = jnp.maximum(view.astype(BF16), 0)
            hv[c] = view
            paint = dot(w_c[...], jnp.concatenate([view, ones], 0))
            for s in range(CHUNK):
                part = slice(s * lanes, s * lanes + lanes)
                b, r = c * per_chunk + s // GROUP, s % GROUP
                for k in range(3):
                    raw[k, b, r : r + 1] = paint[k : k + 1, part]
                raw[3, b, r : r + 1] = out[128:129, part]
            return carry

        lax.fori_loop(0, chunks, forward, 0)

        before = jnp.zeros((1, lanes), F32)
        shade = [jnp.zeros((8, lanes), F32) for _ in range(3)]
        far, opaque = jnp.zeros((8, lanes), F32), jnp.zeros((8, lanes), F32)

        def spacing(b):
            t = depth[first + b]
            after = depth[first + b + 1, 0:1] if b + 1 < blocks else jnp.full((1, lanes), far_plane, F32)
            return jnp.where(row8 == 7, after, pltpu.roll(t, 7, 0)) - t

        for b in range(blocks):
            zs = raw[3, b] + sigma_bias
            density = jnp.maximum(zs, 0.0) + jnp.log1p(jnp.exp(-jnp.abs(zs)))
            q = density * spacing(b)
            inclusive = running(q) + before
            before = inclusive[7:8]
            lit = jnp.exp(-(inclusive - q))
            w = lit * (1.0 - jnp.exp(-q))
            back[0, b] = w
            back[1, b] = jnp.exp(-inclusive)
            if net == 1:
                back[3, b] = density * mask
            for k in range(3):
                tint = jax.nn.sigmoid(raw[k, b])
                raw[k, b] = tint
                shade[k] = shade[k] + w * tint
            far = far + w * depth[first + b]
            opaque = opaque + w
        shade = [total(x) for x in shade]
        far, opaque = total(far), total(opaque)
        miss = [shade[k] - target_rows[k] for k in range(3)]
        loss = loss + ray_weight * (miss[0] * miss[0] + miss[1] * miss[1] + miss[2] * miss[2])
        seed = [2.0 * ray_weight * miss[k] for k in range(3)]
        seed_depth = seed_opaque = None
        if net == 1:
            for k in range(3):
                mine[k : k + 1] = shade[k]
            mine[3:4] = far
            mine[4:5] = mask
            mine[5:8] = jnp.zeros((3, lanes), F32)

            def across(i, slot):
                return pltpu.make_async_remote_copy(
                    mine, halo.at[slot], send.at[i], recv.at[slot], device_id=sides[i][0], device_id_type=MESH
                )

            for i in range(4):
                pl.when(sides[i][1])(lambda i=i: across(i, i).start())

            def count_bin(b, carry):
                sums = jnp.zeros((8, lanes), F32)
                for s in range(blocks):
                    sums = sums + jnp.where(bins_turned[s * GROUP : s * GROUP + GROUP] == b.astype(F32), back[3, s], 0.0)
                folded = sums[:, :128]
                for k in range(1, lanes // 128):
                    folded = folded + sums[:, k * 128 : k * 128 + 128]
                hist[b] = total(folded)
                return carry

            lax.fori_loop(0, NHIST, count_bin, 0)
            binned = dot_nt(jnp.full((8, 128), 1.0, F32), jnp.sum(hist[...], 1), HIGH)[0:1] / mask_floor
            solid = 0.01 + 0.98 * opaque
            entropy = -mask * (solid * jnp.log(solid) + (1.0 - solid) * jnp.log(1.0 - solid))
            seed_opaque = -(entropy_weight / mask_floor) * mask * 0.98 * (jnp.log(solid) - jnp.log(1.0 - solid))
            for i in range(4):
                @pl.when(sides[i][1])
                def _(i=i):
                    across(i, i).wait_send()
                    across(i, i ^ 1).wait_recv()

            values = mine[...]
            lane = iota((8, lanes), 1)
            col, tile_row = lane % tile_cols, lane // tile_cols

            def beyond(i, inner, shift, wrap):
                other = jnp.where(
                    inner, pltpu.roll(values, shift % lanes, 1), pltpu.roll(halo[i ^ 1], wrap % lanes, 1)
                )
                return jnp.where(inner | sides[i][1], other, 0.0)

            smooth = jnp.zeros((8, lanes), F32)
            pull = jnp.zeros((8, lanes), F32)
            for i, inner, shift, wrap in (
                (0, col > 0, 1, 1 - tile_cols),
                (1, col < tile_cols - 1, -1, tile_cols - 1),
                (2, tile_row > 0, tile_cols, tile_cols - lanes),
                (3, tile_row < tile_rows - 1, -tile_cols, lanes - tile_cols),
            ):
                other = beyond(i, inner, shift, wrap)
                pair = other[4:5] * mask
                gap = jnp.where(row8 < 4, values - other, 0.0)
                pull = pull + pair * gap
                if i % 2 == 1:
                    smooth = smooth + pair * gap * gap
            pull = (2.0 * smooth_weight / mask_floor) * pull
            seed = [seed[k] + pull[k : k + 1] for k in range(3)]
            seed_depth = pull[3:4]
            loss = loss + (smooth_weight * total(smooth) + entropy_weight * entropy) / mask_floor

        later = jnp.zeros((1, lanes), F32)
        for b in reversed(range(blocks)):
            w, passed = back[0, b], back[1, b]
            tint = [raw[k, b] for k in range(3)]
            pulled = seed[0] * tint[0] + seed[1] * tint[1] + seed[2] * tint[2]
            if net == 1:
                pulled = pulled + seed_depth * depth[first + b] + seed_opaque
            weighted = pulled * w
            onward = running_back(weighted) + later
            later = onward[0:1]
            dq = pulled * passed - (onward - weighted)
            back[3, b] = dq * spacing(b) * jax.nn.sigmoid(raw[3, b] + sigma_bias)
            for k in range(3):
                back[k, b] = w * seed[k] * tint[k] * (1.0 - tint[k])

        upper, lower = [part.source for part in (grads, grads_fine)[net]]
        g_m = upper
        g_v, g_e = lower.at[ROW_V - 256 : ROW_V - 112], lower.at[ROW_E - 256 : ROW_E - 192]
        for ref in (upper, lower, g_c, g_r):
            ref[...] = jnp.zeros_like(ref)

        def backward(c, carry):
            send_on(net, "backward", c)
            parts = []
            for s in range(CHUNK):
                b, r = c * per_chunk + s // GROUP, s % GROUP
                parts.append(jnp.concatenate([back[k, b, r : r + 1] for k in range(4)] + [jnp.zeros((12, lanes), F32)], 0))
            gate = jnp.concatenate(parts, 1).astype(BF16)
            view = hv[c]
            gv = jnp.where(view > 0, dot(w_ct[...], gate).astype(BF16), 0)
            sums = g_r[...]
            for s in range(CHUNK):
                sums = sums + gv[:, s * lanes : s * lanes + lanes].astype(F32)
            g_r[...] = sums
            g_c[...] += dot_nt(jnp.concatenate([view, ones], 0), gate)
            both = jnp.concatenate([gv, gate], 0)
            two = h2[c]
            turned[...] = two.T
            g_v[...] += dot(both, turned[...])
            g2 = jnp.where(two > 0, dot(w_vt[...], both).astype(BF16), 0)
            one = h1[c]
            g_m[...] += dot_nt(jnp.concatenate([one, ones], 0), g2)
            g1 = jnp.where(one > 0, dot(w_mt[...], g2).astype(BF16), 0)
            turned[...] = g1.T
            g_e[...] += dot(code_of(c), turned[...])
            return carry

        lax.fori_loop(0, chunks, backward, 0)
        if net == 0:
            params_fine.step(params.steps - 1)
        else:
            grads_fine[0].step(0)

        tints = jnp.concatenate([g_c[...], jnp.zeros((144, 112), F32)], 1)
        tints, sums_c = tints[:128].T[:16], tints[128:136].T[:16, 0:1]
        lane = iota((16, 256), 1)
        grad_misc = jnp.where(row == 0, lower[131:132], jnp.where(row == 1, upper[256:257], 0.0))
        for k, spot in ((3, 0), (0, 129), (1, 130), (2, 131)):
            grad_misc = jnp.where((row == 2) & (lane == spot), sums_c[k : k + 1], grad_misc)
        lower[ROW_S - 256 : ROW_S - 240] = grad_misc
        lower[ROW_D - 256 : ROW_D - 224, 0:128] = dot_nt(view_code.astype(F32), g_r[...], HIGH)
        lower[ROW_D - 256 : ROW_D - 224, 128:256] = jnp.concatenate([tints, jnp.zeros((16, 128), F32)], 0)
    rest = grads_fine[1].source
    rest[ROW_D - 224 : ROW_D - 223, 0:NHIST] = binned
    fold = loss[:, :128]
    for k in range(1, lanes // 128):
        fold = fold + loss[:, k * 128 : k * 128 + 128]
    rest[ROW_D - 223 : ROW_D - 222, 0:128] = fold
    grads_fine[1].step(0)
    for k in range(1, params.steps):
        for part in grads_fine:
            part.step(k)
    outward = [
        pltpu.make_async_copy(part.whole, result.at[pl.ds(i * 256, 256)], leaving.at[i])
        for i, part in enumerate(grads + grads_fine)
    ]
    for copy in outward:
        copy.start()
    for copy in outward:
        copy.wait()


def adamw_update(weight, moment, square, gradient):
    moment_next = beta_first * moment + (1.0 - beta_first) * gradient
    square_next = beta_second * square + (1.0 - beta_second) * gradient * gradient
    first_hat = moment_next / (1.0 - beta_first**step_count)
    second_hat = square_next / (1.0 - beta_second**step_count)
    weight_next = weight - learn_rate * (
        first_hat / (jnp.sqrt(second_hat) + adam_epsilon) + decay_rate * weight
    )
    return (weight_next, moment_next, square_next)


def update_kernel(tiles_y, owners_given, grads_given, *refs):
    given, outs, taken = refs[0:15], refs[15:17], refs[17:32]
    held = refs[32:47]
    grads, owners, loss, histogram, arrived, left, ends = refs[47:]
    device = lax.axis_index("tx") * tiles_y + lax.axis_index("ty")
    order = (1, 2, 0, 4, 3)
    fetch = [
        pltpu.make_async_copy(grads_given, grads, ends.at[0]),
        pltpu.make_async_copy(owners_given, owners, ends.at[1]),
    ]
    for copy in fetch:
        copy.start()
    for group in order:
        for i in (group, group + 5, group + 10):
            pltpu.make_async_copy(given[i], held[i], arrived.at[i]).start()
    for copy in fetch:
        copy.wait()
    histogram[...] = grads[ROWS + ROW_D + 32 : ROWS + ROW_D + 33, 0:NHIST]
    loss[...] = jnp.sum(grads[ROWS + ROW_D + 33 : ROWS + ROW_D + 34, 0:128], 1, keepdims=True)
    figures = [
        pltpu.make_async_copy(loss, outs[0], ends.at[2]),
        pltpu.make_async_copy(histogram, outs[1], ends.at[3]),
    ]
    for copy in figures:
        copy.start()

    def step(group, at, gradient):
        trio = (held[group], held[group + 5], held[group + 10])
        for ref, now in zip(trio, adamw_update(*[ref[at] for ref in trio], gradient)):
            ref[at] = now

    every = slice(None)

    def update(group, net):
        base = net * ROWS
        last = grads[base + ROW_D : base + ROW_D + 32]
        if group == 0:
            choose = selector(64, held[0].shape[0], LPOS, 32, F32)
            step(0, (every, net, every), dot_tn(choose, grads[base + ROW_E : base + ROW_E + 64], HIGH))
        elif group == 1:
            step(1, (net,), grads[base + ROW_M : base + ROW_M + 256].T)
        elif group == 2:
            views = grads[base + ROW_V : base + ROW_V + 128]
            step(2, (slice(0, 128), net, every), views[:, 0:128].T)
            step(2, (slice(128, 256), net, every), views[:, 128:256].T)
            rest = slice(256, held[2].shape[0])
            choose = selector(32, held[2].shape[0] - 256, LDIR, 16, F32)
            step(2, (rest, net, every), dot_tn(choose, last[:, :128], HIGH))
        elif group == 3:
            step(3, (every, net, every), last[0:3, 128:])
        else:
            misc = grads[base + ROW_S : base + ROW_S + 16]
            spot = slice(net, net + 1)
            step(4, (spot, slice(0, 256)), grads[base + ROW_E + 63 : base + ROW_E + 64])
            step(4, (spot, slice(256, 512)), misc[1:2])
            step(4, (spot, slice(512, 768)), misc[0:1])
            bias = jnp.concatenate([last[28:29, :128], jnp.zeros((1, 128), F32)], 1)
            bias = pltpu.roll(jnp.broadcast_to(bias, (8, 256)), 1, 1)[0:1]
            step(4, (spot, slice(768, 900)), (misc[2:3] + bias)[:, :132])

    for group in order:
        trio = (group, group + 5, group + 10)
        for i in trio:
            pltpu.make_async_copy(given[i], held[i], arrived.at[i]).wait()
        for net in range(2):
            pl.when(owners[net, group] == device)(functools.partial(update, group, net))
        for i in trio:
            pltpu.make_async_copy(held[i], taken[i], left.at[i]).start()
    for i in range(15):
        pltpu.make_async_copy(held[i], taken[i], left.at[i]).wait()
    for copy in figures:
        copy.wait()


ANY_SPEC = pl.BlockSpec(memory_space=pl.ANY)
VMEM_SPEC = pl.BlockSpec(memory_space=pltpu.VMEM)
SMEM_SPEC = pl.BlockSpec(memory_space=pltpu.SMEM)


def per_device(sizes, camera, ray_mask, ray_direction, anchors, target, fine_levels, density_bins, owners, *trees):
    turns = ((2, 0, 1), (0, 1, 2), (2, 0, 1), (1, 0, 2), (0, 1))
    states = [jnp.transpose(x[0], turns[i % 5]) for i, x in enumerate(trees)]
    lanes = camera.shape[0] * camera.shape[1]
    samples = fine_levels.shape[0]
    levels = jnp.transpose(fine_levels, (1, 2, 0)).reshape(lanes, samples)
    bins = jnp.transpose(density_bins, (1, 2, 0)).reshape(lanes, samples)

    groups = groups_of(sizes)
    turned_round = groups[:1] + groups[:0:-1]
    param_plan = plan_of(groups, ROWS, 16, groups[2:])
    upper, lower = plan_of(groups, 256, 8, groups[2:]), plan_of(turned_round, 256, 8, turned_round[2:])
    plans = [(param_plan, 16), (param_plan, 16), (plan_of(groups, 8, 8, groups), 8)]
    plans += [(upper, 8), (lower, 8)] * 2
    sums = []
    kinds = [(BF16, 256, 0)] * 2 + [(F32, 128, 0)] + [(F32, 256, 16), (F32, 256, 0)] * 2
    for (plan, _), kind in zip(plans, kinds):
        sums += sum_scratch(plan, *kind)
    points = CHUNK * lanes
    chunks = samples // CHUNK
    blocks = samples // GROUP
    small = [camera, ray_mask, ray_direction, target, anchors]
    grads = pl.pallas_call(
        functools.partial(step_kernel, sizes, groups, plans),
        out_shape=jax.ShapeDtypeStruct((2 * ROWS, 256), F32),
        in_specs=[ANY_SPEC] * 13,
        out_specs=ANY_SPEC,
        scratch_shapes=[
            pltpu.VMEM((blocks + SC // GROUP, 64, GROUP * lanes), BF16),
            pltpu.VMEM((chunks, 256, points), BF16),
            pltpu.VMEM((chunks, 256, points), BF16),
            pltpu.VMEM((chunks, 128, points), BF16),
            pltpu.VMEM((4, blocks, GROUP, lanes), F32),
            pltpu.VMEM((blocks + SC // GROUP, GROUP, lanes), F32),
            pltpu.VMEM((4, blocks, GROUP, lanes), F32),
            pltpu.VMEM((NHIST, 1, 128), F32),
            pltpu.VMEM((256, 64), BF16),
            pltpu.VMEM((256, 256), BF16),
            pltpu.VMEM((144, 256), BF16),
            pltpu.VMEM((256, 144), BF16),
            pltpu.VMEM((16, 144), BF16),
            pltpu.VMEM((128, 16), BF16),
            pltpu.VMEM((256, 128), F32),
            pltpu.VMEM((128, lanes), F32),
            pltpu.VMEM((144, 16), F32),
            pltpu.VMEM((128, lanes), F32),
            pltpu.VMEM((points, 256), BF16),
            pltpu.VMEM((8, lanes), F32),
            pltpu.VMEM((4, 8, lanes), F32),
            pltpu.SemaphoreType.DMA((4,)),
            pltpu.SemaphoreType.DMA((4,)),
            pltpu.SemaphoreType.DMA((4,)),
            pltpu.SemaphoreType.DMA((13,)),
            pltpu.SMEM((2, 5), jnp.int32),
        ]
        + [pltpu.VMEM(x.shape, x.dtype) for x in states[:5] + small + [levels, bins]]
        + sums,
        compiler_params=pltpu.CompilerParams(collective_id=0, has_side_effects=True, vmem_limit_bytes=LIMIT),
        name="step",
    )(owners.T, camera, ray_mask, ray_direction, target, levels, bins, anchors, *states[:5])

    results = pl.pallas_call(
        functools.partial(update_kernel, sizes["ty"]),
        out_shape=[jax.ShapeDtypeStruct((1, 1), F32), jax.ShapeDtypeStruct((1, NHIST), F32)]
        + [jax.ShapeDtypeStruct(x.shape, F32) for x in states],
        in_specs=[ANY_SPEC] * 17,
        out_specs=[ANY_SPEC] * 17,
        scratch_shapes=[pltpu.VMEM(x.shape, F32) for x in states]
        + [
            pltpu.VMEM((2 * ROWS, 256), F32),
            pltpu.SMEM((2, 5), jnp.int32),
            pltpu.VMEM((1, 1), F32),
            pltpu.VMEM((1, NHIST), F32),
            pltpu.SemaphoreType.DMA((15,)),
            pltpu.SemaphoreType.DMA((15,)),
            pltpu.SemaphoreType.DMA((4,)),
        ],
        name="update",
    )(owners.T, grads, *states)
    turned = []
    for i, x in enumerate(results[2:]):
        turn = turns[i % 5]
        turned.append(jnp.transpose(x, [turn.index(d) for d in range(len(turn))])[None])
    return (results[0].reshape(()), results[1].reshape(NHIST)) + tuple(turned)


def solution(mesh):
    sizes = dict(mesh.shape)
    tiled, tiled3 = P("ty", "tx"), P(None, "ty", "tx")
    slots = P(("tx", "ty"), None, None, None)
    trees = (slots, slots, slots, slots, P(("tx", "ty"), None, None))
    return jax.shard_map(
        functools.partial(per_device, sizes),
        mesh=mesh,
        in_specs=(tiled, tiled, tiled3, P(), tiled3, tiled3, tiled3, P()) + trees * 3,
        out_specs=(P(), P()) + trees * 3,
        check_vma=False,
    )
```

```python
import functools
import math

import jax
import jax.numpy as jnp
from jax import lax
from jax.experimental import pallas as pl
from jax.experimental.pallas import tpu as pltpu
from jax.sharding import PartitionSpec as P

LPOS = 10
LDIR = 4
SC = 64
NT = 1024
NHIST = 64

near_plane = 2.0
far_plane = 6.0
shrink = 0.125
smooth_weight = 0.1
entropy_weight = 0.1
beta_first = 0.9
beta_second = 0.999
adam_epsilon = 1e-08
decay_rate = 0.01
learn_rate = 0.05
step_count = 10

MESH = pl.DeviceIdType.MESH
F32 = jnp.float32
BF16 = jnp.bfloat16
HIGH = lax.Precision.HIGHEST
GROUP = 8
CHUNK = 16
ROWS = 512
LIMIT = 67_000_000
PACE = (0, 0, 7, 19, 19, 24, 24)

ROW_M, ROW_V, ROW_S, ROW_E, ROW_D = 0, 256, 384, 400, 464

PI_A = 3.140625
PI_B = 0.0009670257568359375
PI_C = math.pi - PI_A - PI_B
SIN = (-0.16666656732559204, 0.008333015255630016, -0.00019806479394901544, 2.5997517241194146e-06)
COS = (-0.5, 0.04166664183139801, -0.0013888400280848145, 2.4761729946476407e-05, -2.607421833999979e-07)


def dot(a, b, precision=None):
    return lax.dot_general(a, b, (((1,), (0,)), ((), ())), preferred_element_type=F32, precision=precision)


def dot_nt(a, b, precision=None):
    return lax.dot_general(a, b, (((1,), (1,)), ((), ())), preferred_element_type=F32, precision=precision)


def dot_tn(a, b, precision=None):
    return lax.dot_general(a, b, (((0,), (0,)), ((), ())), preferred_element_type=F32, precision=precision)


def iota(shape, axis):
    return lax.broadcasted_iota(jnp.int32, shape, axis)


def sin_cos_twice(y):
    k = jnp.round(y * (1.0 / math.pi))
    y = ((y - k * PI_A) - k * PI_B) - k * PI_C
    t = y * y
    s = y * (1.0 + t * (SIN[0] + t * (SIN[1] + t * (SIN[2] + t * SIN[3]))))
    c = 1.0 + t * (COS[0] + t * (COS[1] + t * (COS[2] + t * (COS[3] + t * COS[4]))))
    d = s + s
    return d * c, 1.0 - d * s


def code_column(row, levels, pad):
    half = row % pad
    third = 3 * levels
    wave = 3 + 6 * (half // 3) + half % 3 + jnp.where(row >= pad, 3, 0)
    if levels == LPOS:
        rest = jnp.where(row == 30, 0, jnp.where(row == 31, 1, jnp.where(row == 62, 2, -1)))
    else:
        rest = jnp.where((row >= 12) & (row < 15), row - 12, jnp.where(row == 28, -1, -2))
    return jnp.where(half < third, wave, rest)


def selector(rows, columns, levels, pad, dtype):
    return (iota((rows, columns), 1) == code_column(iota((rows, columns), 0), levels, pad)).astype(dtype)


class Members:
    def __init__(self, axis, count, spread):
        self.axis, self.count, self.spread = axis, count, spread

    def place(self):
        return (lax.axis_index(self.axis) // self.spread) % self.count

    def peer(self, step):
        me = self.place()
        other = (me + step) % self.count
        return other, {self.axis: lax.axis_index(self.axis) + (other - me) * self.spread}


def groups_of(sizes):
    cores = 2 if sizes["tx"] % 2 == 0 else 1
    groups = [Members("tx", cores, 1), Members("ty", sizes["ty"], 1), Members("tx", sizes["tx"] // cores, cores)]
    return [g for g in groups if g.count > 1]


def plan_of(groups, rows, least, whole=()):
    plan = []
    for group in groups:
        after = rows // group.count if rows % (group.count * least) == 0 and group not in whole else rows
        plan.append((group, rows, after))
        rows = after
    return plan


def sum_scratch(plan, dtype, width, beyond):
    copies = sum(group.count - 1 for group, _, _ in plan)
    rows = plan[0][1]
    return (
        [pltpu.VMEM((rows + beyond, width), dtype), pltpu.VMEM((rows, width), dtype)]
        + [pltpu.VMEM((group.count, after, width), dtype) for group, _, after in plan]
        + [pltpu.VMEM((after, width), dtype) for _, _, after in plan]
        + [pltpu.SemaphoreType.DMA((2 * copies,)), pltpu.SemaphoreType.DMA((2 * copies,))]
    )


class Sum:
    def __init__(self, plan, least, refs):
        n = len(plan)
        self.plan, self.least = plan, least
        self.source, self.whole = refs[0], refs[1]
        self.landing, self.part = refs[2 : 2 + n], refs[2 + n : 2 + 2 * n]
        self.send, self.recv = refs[2 + 2 * n :]
        self.steps = 2 * n + 1

    def rows_at(self, start, length):
        return pl.ds(pl.multiple_of(start, self.least), length)

    def offsets(self):
        at, result = 0, [0]
        for group, before, after in self.plan:
            if after != before:
                at = at + group.place() * after
            result.append(at)
        return result

    def base(self, stage, back):
        copies = [group.count - 1 for group, _, _ in self.plan]
        return sum(copies[:stage]) + (sum(copies) if back else 0)

    def scatter(self, stage):
        group, before, after = self.plan[stage]
        held = self.source if stage == 0 else self.part[stage - 1]
        copies = []
        for step in range(1, group.count):
            other, where = group.peer(step)
            k = self.base(stage, False) + step - 1
            piece = held if after == before else held.at[self.rows_at(other * after, after)]
            copies.append(
                pltpu.make_async_remote_copy(
                    piece,
                    self.landing[stage].at[group.place()],
                    self.send.at[k],
                    self.recv.at[k],
                    device_id=where,
                    device_id_type=MESH,
                )
            )
        return copies

    def gather(self, stage):
        group, before, after = self.plan[stage]
        if after == before:
            return []
        mine = self.rows_at(self.offsets()[stage + 1], after)
        copies = []
        for step in range(1, group.count):
            _, where = group.peer(step)
            k = self.base(stage, True) + step - 1
            copies.append(
                pltpu.make_async_remote_copy(
                    self.whole.at[mine],
                    self.whole.at[mine],
                    self.send.at[k],
                    self.recv.at[k],
                    device_id=where,
                    device_id_type=MESH,
                )
            )
        return copies

    def step(self, k):
        n = len(self.plan)
        if 0 < k <= n:
            stage = k - 1
            group, before, after = self.plan[stage]
            held = self.source if stage == 0 else self.part[stage - 1]
            for copy in self.scatter(stage):
                copy.wait()
            own = held[...] if after == before else held[self.rows_at(group.place() * after, after)]
            self.landing[stage][group.place()] = own
            total = self.landing[stage][0]
            for j in range(1, group.count):
                total = total + self.landing[stage][j]
            self.part[stage][...] = total
            if stage == n - 1:
                self.whole[self.rows_at(self.offsets()[n], after)] = total
        elif k > n:
            for copy in self.gather(2 * n - k):
                copy.wait()
        if k < n:
            for copy in self.scatter(k):
                copy.start()
        elif k < 2 * n:
            for copy in self.gather(2 * n - 1 - k):
                copy.start()


def greet(groups, sides):
    barrier = pltpu.get_barrier_semaphore()
    expected = 0
    for group in groups:
        for step in range(1, group.count):
            pl.semaphore_signal(barrier, inc=1, device_id=group.peer(step)[1], device_id_type=MESH)
            expected = expected + 1
    for where, there in sides:
        expected = expected + there.astype(jnp.int32)

        @pl.when(there)
        def _(where=where):
            pl.semaphore_signal(barrier, inc=1, device_id=where, device_id_type=MESH)

    return expected


def running(block):
    row = iota(block.shape, 0)
    for shift in (1, 2, 4):
        block = block + jnp.where(row >= shift, pltpu.roll(block, shift, 0), 0.0)
    return block


def running_back(block):
    row = iota(block.shape, 0)
    for shift in (1, 2, 4):
        block = block + jnp.where(row < 8 - shift, pltpu.roll(block, 8 - shift, 0), 0.0)
    return block


def total(block):
    return jnp.sum(block, 0, keepdims=True)


def pack(owned, net, choose_e, choose_d, big, encoder, middle, viewer, colour, scalars):
    def rounded(group, value):
        return jnp.where(owned[group], value, 0.0).astype(BF16)

    big[ROW_M : ROW_M + 256] = rounded(1, middle[net])
    views = rounded(2, viewer[:, net, :])
    big[ROW_V : ROW_V + 128, 0:128] = views[0:128]
    big[ROW_V : ROW_V + 128, 128:256] = views[128:256]
    row = rounded(4, scalars[net : net + 1]).astype(F32)
    block = iota((16, 256), 0)
    tail = jnp.concatenate([row[:, 768:], jnp.zeros((1, 124), F32)], 1)
    picked = jnp.where(block == 0, row[:, 512:768], jnp.where(block == 1, row[:, 256:512], 0.0))
    big[ROW_S : ROW_S + 16] = jnp.where(block == 2, tail, picked).astype(BF16)
    first = dot(choose_e, rounded(0, encoder[:, net, :]))
    first = jnp.where(iota((64, 256), 0) == 63, row[:, :256], first)
    big[ROW_E : ROW_E + 64] = first.astype(BF16)
    big[ROW_D : ROW_D + 32, 0:128] = dot(choose_d, views[256:]).astype(BF16)
    paint = jnp.concatenate([rounded(3, colour[:, net, :]).astype(F32), jnp.zeros((29, 128), F32)], 0)
    big[ROW_D : ROW_D + 32, 128:256] = paint.astype(BF16)
    big[ROW_D + 32 : ROWS] = jnp.zeros((ROWS - ROW_D - 32, 256), BF16)


def step_kernel(
    sizes, groups, plans, owners, camera, ray_mask, direction, target, levels, bins, anchors,
    encoder, middle, viewer, colour, scalars, result,
    enc, h1, h2, hv, raw, depth, back, hist, w_e, w_mt, w_v, w_vt, w_c, w_ct, bias, per_ray,
    g_c, g_r, turned, mine, halo, send, recv, leaving, entering, *sums,
):
    local, sums = sums[:13], sums[13:]
    tile_rows, tile_cols = camera.shape
    lanes = tile_rows * tile_cols
    cameras = anchors.shape[1]
    points = CHUNK * lanes
    per_chunk = CHUNK // GROUP
    tx, ty = lax.axis_index("tx"), lax.axis_index("ty")
    device = tx * sizes["ty"] + ty
    sides = (
        ({"tx": tx - 1}, tx > 0),
        ({"tx": tx + 1}, tx < sizes["tx"] - 1),
        ({"ty": ty - 1}, ty > 0),
        ({"ty": ty + 1}, ty < sizes["ty"] - 1),
    )
    sum_of = []
    at = 0
    for plan, least in plans:
        length = 4 + 2 * len(plan)
        sum_of.append(Sum(plan, least, sums[at : at + length]))
        at += length
    params, params_fine, counting = sum_of[:3]
    grads, grads_fine = sum_of[3:5], sum_of[5:7]
    expected = greet(groups, sides[:2])
    given = (
        owners, encoder, middle, viewer, colour, scalars,
        camera, ray_mask, direction, target, anchors, levels, bins,
    )
    inward = [pltpu.make_async_copy(x, here, entering.at[i]) for i, (x, here) in enumerate(zip(given, local))]
    for copy in inward:
        copy.start()
    for copy in inward[:6]:
        copy.wait()
    owners, encoder, middle, viewer, colour, scalars, camera, ray_mask, direction, target, anchors, levels, bins = local

    choose_e = selector(64, encoder.shape[0], LPOS, 32, BF16)
    choose_d = selector(32, viewer.shape[0] - 256, LDIR, 16, BF16)
    trees = (encoder, middle, viewer, colour, scalars)
    owned = [[owners[net, group] == device for group in range(5)] for net in range(2)]
    pack(owned[0], 0, choose_e, choose_d, params.source, *trees)
    pl.semaphore_wait(pltpu.get_barrier_semaphore(), expected)
    params.step(0)

    for copy in inward[6:]:
        copy.wait()
    tall = jnp.concatenate(
        [direction[k] for k in range(3)]
        + [target[k] for k in range(3)]
        + [ray_mask[...].astype(F32), camera[...].astype(F32)],
        0,
    )
    repeat = (iota((tile_cols, lanes), 1) % tile_cols == iota((tile_cols, lanes), 0)).astype(F32)
    wide = dot(tall, repeat, HIGH)
    keep = iota((tile_rows, lanes), 1) // tile_cols == iota((tile_rows, lanes), 0)
    rows = [
        jnp.sum(jnp.where(keep, wide[k * tile_rows : k * tile_rows + tile_rows], 0.0), 0, keepdims=True)
        for k in range(8)
    ]
    mask, camera_row = rows[6], rows[7]
    target_rows = rows[3:6]
    number = iota((128, lanes), 0)
    picks = camera_row == number.astype(F32)
    counting.source[...] = dot_nt(
        jnp.broadcast_to(mask, (8, lanes)).astype(BF16), (picks | (number == 127)).astype(BF16)
    )
    picks = picks.astype(F32)
    counting.step(0)
    pack(owned[1], 1, choose_e, choose_d, params_fine.source, *trees)

    centres = jnp.concatenate([anchors[...], jnp.zeros((3, 128 - cameras), F32)], 1)
    origin = dot(centres, picks, HIGH)
    basis = jnp.concatenate([origin] + rows[0:3] + [jnp.zeros((2, lanes), F32)], 0)
    row8 = iota((8, lanes), 0)
    row32 = iota((32, lanes), 0)
    lift = iota((40, 8), 0)
    third = jnp.where(lift < 32, lift % 3, jnp.where(lift == 38, 2, -9))
    o_all = dot((third == iota((40, 8), 1)).astype(F32), basis, HIGH)
    d_all = dot((third + 3 == iota((40, 8), 1)).astype(F32), basis, HIGH)
    o_main, d_main = o_all[:32], d_all[:32]
    o_last, d_last = jnp.where(row8 == 7, 1.0 / shrink, o_all[32:]), d_all[32:]
    half_pi = jnp.float32(math.pi) * 0.5
    scale = jnp.zeros((32, lanes), F32)
    for level in range(LPOS):
        scale = jnp.where((row32 >= 3 * level) & (row32 < 3 * level + 3), half_pi * (2.0**level), scale)

    row16 = iota((16, lanes), 0)
    scale_d = scale[:16]
    sin_d, cos_d = sin_cos_twice(d_main[:16] * scale_d)
    top = jnp.where(row16 >= 12, jnp.where(row16 < 15, d_main[:16], 0.0), sin_d)
    bottom = jnp.where(row16 >= 12, jnp.where(row16 == 12, 1.0, 0.0), cos_d)
    view_code = jnp.concatenate([top, bottom], 0).astype(BF16)

    samples_fine = levels.shape[1]
    blocks_of = (SC // GROUP, samples_fine // GROUP)
    first_block = (0, blocks_of[0])
    for b in range(blocks_of[0]):
        depth[b] = near_plane + (far_plane - near_plane) * ((row8 + b * GROUP).astype(F32) + 0.5) / SC
    levels_turned = levels[...].astype(F32).T
    for b in range(blocks_of[1]):
        at = levels_turned[b * GROUP : b * GROUP + GROUP]
        depth[blocks_of[0] + b] = near_plane + (far_plane - near_plane) * (at + 0.5) / NT
    bins_turned = bins[...].astype(F32).T

    def encode(b, carry):
        for s in range(GROUP):
            t = depth[b, s : s + 1]
            place = (o_main + t * d_main) * shrink
            wave, cowave = sin_cos_twice(place * scale)
            wave = jnp.where(row32 >= 30, place, wave)
            extra = (o_last + t * d_last) * shrink
            end = jnp.where(row8 >= 6, extra, cowave[24:])
            cowave = jnp.concatenate([cowave[:24], end], 0)
            enc[b, 0:32, s * lanes : s * lanes + lanes] = wave.astype(BF16)
            enc[b, 32:64, s * lanes : s * lanes + lanes] = cowave.astype(BF16)
        return carry

    all_blocks = sum(blocks_of)
    done = 0
    for k in range(1, params.steps):
        until = all_blocks * PACE[min(k, len(PACE) - 1)] // PACE[-1]
        if until > done:
            lax.fori_loop(done, until, encode, 0)
        done = until
        params.step(k)
        if k < counting.steps:
            counting.step(k)

    count = counting.whole[...]
    mask_floor = jnp.maximum(count[0:1, 127:128], 1.0)
    inverse = 1.0 / jnp.maximum(count, 1.0)
    ray_weight = dot(inverse, picks, HIGH)[0:1] * mask / cameras
    ones = jnp.full((16, points), 1.0, BF16)
    loss = jnp.zeros((1, lanes), F32)

    chunks_of = [n // per_chunk for n in blocks_of]

    def at_chunks(moved, pairs, over):
        return [(part, k, over * eighth // 8) for k, eighth in pairs for part in moved]

    half = params.steps // 2
    beside = {
        (0, "forward"): at_chunks([params_fine], [(0, 0), (1, 2), (2, 6)][:half], chunks_of[0]),
        (0, "backward"): at_chunks([params_fine], [(k, min(2 + 4 * (k > half + 1), 6)) for k in range(half, params.steps - 1)], chunks_of[0]),
        (1, "forward"): at_chunks(grads, [(0, 0), (1, 1), (2, 4), (3, 7)][: half + 1], chunks_of[1]),
        (1, "backward"): at_chunks(grads, [(k, min(1 + 2 * (k - half - 1), 7)) for k in range(half + 1, params.steps)], chunks_of[1]),
    }

    def send_on(net, name, c):
        for spot in sorted({spot for _, _, spot in beside[(net, name)]}):

            @pl.when(c == spot)
            def _(spot=spot):
                for moved, k, where in beside[(net, name)]:
                    if where == spot:
                        moved.step(k)

    for net in range(2):
        blocks, first, chunks = blocks_of[net], first_block[net], chunks_of[net]
        held = (params, params_fine)[net].whole
        w_mt[...] = held[ROW_M : ROW_M + 256].astype(F32).T.astype(BF16)
        misc32 = held[ROW_S : ROW_S + 16].astype(F32)
        row = iota((16, 256), 0)
        views = held[ROW_V : ROW_V + 128]
        w_vt[0:128, 0:128] = views[:, 0:128]
        w_vt[128:256, 0:128] = views[:, 128:256]
        w_v[0:128, 0:128] = views[:, 0:128].astype(F32).T.astype(BF16)
        w_v[0:128, 128:256] = views[:, 128:256].astype(F32).T.astype(BF16)
        w_v[128:144] = jnp.where(row == 0, misc32, 0.0).astype(BF16)
        sigma_t = jnp.concatenate([jnp.zeros((3, 256), F32), misc32[0:1], jnp.zeros((124, 256), F32)], 0).T
        w_vt[:, 128:144] = sigma_t[:, :16].astype(BF16)
        w_e[...] = held[ROW_E : ROW_E + 64].astype(F32).T.astype(BF16)
        last = held[ROW_D : ROW_D + 32].astype(F32)
        paint = last[:16, 128:]
        tail = misc32[2:3]
        sigma_bias = tail[:, 0:1]
        lane = iota((16, 128), 1)
        row_c = iota((16, 128), 0)
        tint_bias = jnp.zeros((16, 128), F32)
        for k in range(3):
            tint_bias = jnp.where((row_c == k) & (lane == 0), tail[:, 129 + k : 130 + k], tint_bias)
        w_c[:, 0:128] = paint.astype(BF16)
        w_c[:, 128:144] = tint_bias[:, :16].astype(BF16)
        w_ct[...] = jnp.concatenate([paint, jnp.zeros((112, 128), F32)], 0).T[:, :16].astype(BF16)
        bias[...] = jnp.broadcast_to(misc32[1:2], (128, 256)).T
        views_d = last[:, :128]
        shifted = pltpu.roll(jnp.broadcast_to(tail, (8, 256)), 255, 1)[0:1, :128]
        views_d = jnp.where(iota((32, 128), 0) == 28, shifted, views_d)
        per_ray[...] = dot_tn(views_d.astype(BF16), view_code)

        def code_of(c):
            start = first + c * per_chunk
            return jnp.concatenate([enc[start + i] for i in range(per_chunk)], 1)

        def forward(c, carry):
            send_on(net, "forward", c)
            one = jnp.maximum(dot(w_e[...], code_of(c)).astype(BF16), 0)
            h1[c] = one
            two = dot(held[ROW_M : ROW_M + 256], one) + jnp.tile(bias[...], (1, points // 128))
            two = jnp.maximum(two.astype(BF16), 0)
            h2[c] = two
            out = dot(w_v[...], two)
            view = out[:128] + jnp.tile(per_ray[...], (1, CHUNK))
            view = jnp.maximum(view.astype(BF16), 0)
            hv[c] = view
            paint = dot(w_c[...], jnp.concatenate([view, ones], 0))
            for s in range(CHUNK):
                part = slice(s * lanes, s * lanes + lanes)
                b, r = c * per_chunk + s // GROUP, s % GROUP
                for k in range(3):
                    raw[k, b, r : r + 1] = paint[k : k + 1, part]
                raw[3, b, r : r + 1] = out[128:129, part]
            return carry

        lax.fori_loop(0, chunks, forward, 0)

        upper, lower = [part.source for part in (grads, grads_fine)[net]]
        g_m = upper
        g_v, g_e = lower.at[ROW_V - 256 : ROW_V - 112], lower.at[ROW_E - 256 : ROW_E - 192]

        def clear():
            for ref in (upper, lower, g_c, g_r):
                ref[...] = jnp.zeros_like(ref)

        before = jnp.zeros((1, lanes), F32)
        shade = [jnp.zeros((8, lanes), F32) for _ in range(3)]
        far, opaque = jnp.zeros((8, lanes), F32), jnp.zeros((8, lanes), F32)

        def spacing(b):
            t = depth[first + b]
            after = depth[first + b + 1, 0:1] if b + 1 < blocks else jnp.full((1, lanes), far_plane, F32)
            return jnp.where(row8 == 7, after, pltpu.roll(t, 7, 0)) - t

        for b in range(blocks):
            zs = raw[3, b] + sigma_bias
            density = jnp.maximum(zs, 0.0) + jnp.log1p(jnp.exp(-jnp.abs(zs)))
            q = density * spacing(b)
            inclusive = running(q) + before
            before = inclusive[7:8]
            lit = jnp.exp(-(inclusive - q))
            w = lit * (1.0 - jnp.exp(-q))
            back[0, b] = w
            back[1, b] = jnp.exp(-inclusive)
            if net == 1:
                back[3, b] = density * mask
            for k in range(3):
                tint = jax.nn.sigmoid(raw[k, b])
                raw[k, b] = tint
                shade[k] = shade[k] + w * tint
            far = far + w * depth[first + b]
            opaque = opaque + w
        shade = [total(x) for x in shade]
        far, opaque = total(far), total(opaque)
        miss = [shade[k] - target_rows[k] for k in range(3)]
        loss = loss + ray_weight * (miss[0] * miss[0] + miss[1] * miss[1] + miss[2] * miss[2])
        seed = [2.0 * ray_weight * miss[k] for k in range(3)]
        seed_depth = seed_opaque = None
        if net == 0:
            clear()
        else:
            for k in range(3):
                mine[k : k + 1] = shade[k]
            mine[3:4] = far
            mine[4:5] = mask
            mine[5:8] = jnp.zeros((3, lanes), F32)

            def across(i, slot):
                return pltpu.make_async_remote_copy(
                    mine, halo.at[slot], send.at[i], recv.at[slot], device_id=sides[i][0], device_id_type=MESH
                )

            for i in range(4):
                pl.when(sides[i][1])(lambda i=i: across(i, i).start())
            clear()

            def count_bin(b, carry):
                sums = jnp.zeros((8, lanes), F32)
                for s in range(blocks):
                    sums = sums + jnp.where(bins_turned[s * GROUP : s * GROUP + GROUP] == b.astype(F32), back[3, s], 0.0)
                folded = sums[:, :128]
                for k in range(1, lanes // 128):
                    folded = folded + sums[:, k * 128 : k * 128 + 128]
                hist[b] = total(folded)
                return carry

            lax.fori_loop(0, NHIST, count_bin, 0)
            binned = dot_nt(jnp.full((8, 128), 1.0, F32), jnp.sum(hist[...], 1), HIGH)[0:1] / mask_floor
            solid = 0.01 + 0.98 * opaque
            entropy = -mask * (solid * jnp.log(solid) + (1.0 - solid) * jnp.log(1.0 - solid))
            seed_opaque = -(entropy_weight / mask_floor) * mask * 0.98 * (jnp.log(solid) - jnp.log(1.0 - solid))
            for i in range(4):
                @pl.when(sides[i][1])
                def _(i=i):
                    across(i, i).wait_send()
                    across(i, i ^ 1).wait_recv()

            values = mine[...]
            lane = iota((8, lanes), 1)
            col, tile_row = lane % tile_cols, lane // tile_cols

            def beyond(i, inner, shift, wrap):
                other = jnp.where(
                    inner, pltpu.roll(values, shift % lanes, 1), pltpu.roll(halo[i ^ 1], wrap % lanes, 1)
                )
                return jnp.where(inner | sides[i][1], other, 0.0)

            smooth = jnp.zeros((8, lanes), F32)
            pull = jnp.zeros((8, lanes), F32)
            for i, inner, shift, wrap in (
                (0, col > 0, 1, 1 - tile_cols),
                (1, col < tile_cols - 1, -1, tile_cols - 1),
                (2, tile_row > 0, tile_cols, tile_cols - lanes),
                (3, tile_row < tile_rows - 1, -tile_cols, lanes - tile_cols),
            ):
                other = beyond(i, inner, shift, wrap)
                pair = other[4:5] * mask
                gap = jnp.where(row8 < 4, values - other, 0.0)
                pull = pull + pair * gap
                if i % 2 == 1:
                    smooth = smooth + pair * gap * gap
            pull = (2.0 * smooth_weight / mask_floor) * pull
            seed = [seed[k] + pull[k : k + 1] for k in range(3)]
            seed_depth = pull[3:4]
            loss = loss + (smooth_weight * total(smooth) + entropy_weight * entropy) / mask_floor

        later = jnp.zeros((1, lanes), F32)
        for b in reversed(range(blocks)):
            w, passed = back[0, b], back[1, b]
            tint = [raw[k, b] for k in range(3)]
            pulled = seed[0] * tint[0] + seed[1] * tint[1] + seed[2] * tint[2]
            if net == 1:
                pulled = pulled + seed_depth * depth[first + b] + seed_opaque
            weighted = pulled * w
            onward = running_back(weighted) + later
            later = onward[0:1]
            dq = pulled * passed - (onward - weighted)
            back[3, b] = dq * spacing(b) * jax.nn.sigmoid(raw[3, b] + sigma_bias)
            for k in range(3):
                back[k, b] = w * seed[k] * tint[k] * (1.0 - tint[k])

        def backward(c, carry):
            send_on(net, "backward", c)
            parts = []
            for s in range(CHUNK):
                b, r = c * per_chunk + s // GROUP, s % GROUP
                parts.append(jnp.concatenate([back[k, b, r : r + 1] for k in range(4)] + [jnp.zeros((12, lanes), F32)], 0))
            gate = jnp.concatenate(parts, 1).astype(BF16)
            view = hv[c]
            gv = jnp.where(view > 0, dot(w_ct[...], gate).astype(BF16), 0)
            sums = g_r[...]
            for s in range(CHUNK):
                sums = sums + gv[:, s * lanes : s * lanes + lanes].astype(F32)
            g_r[...] = sums
            g_c[...] += dot_nt(jnp.concatenate([view, ones], 0), gate)
            both = jnp.concatenate([gv, gate], 0)
            two = h2[c]
            turned[...] = two.T
            g_v[...] += dot(both, turned[...])
            g2 = jnp.where(two > 0, dot(w_vt[...], both).astype(BF16), 0)
            one = h1[c]
            g_m[...] += dot_nt(jnp.concatenate([one, ones], 0), g2)
            g1 = jnp.where(one > 0, dot(w_mt[...], g2).astype(BF16), 0)
            turned[...] = g1.T
            g_e[...] += dot(code_of(c), turned[...])
            return carry

        lax.fori_loop(0, chunks, backward, 0)
        if net == 0:
            params_fine.step(params.steps - 1)
        else:
            grads_fine[0].step(0)

        tints = jnp.concatenate([g_c[...], jnp.zeros((144, 112), F32)], 1)
        tints, sums_c = tints[:128].T[:16], tints[128:136].T[:16, 0:1]
        lane = iota((16, 256), 1)
        grad_misc = jnp.where(row == 0, lower[131:132], jnp.where(row == 1, upper[256:257], 0.0))
        for k, spot in ((3, 0), (0, 129), (1, 130), (2, 131)):
            grad_misc = jnp.where((row == 2) & (lane == spot), sums_c[k : k + 1], grad_misc)
        lower[ROW_S - 256 : ROW_S - 240] = grad_misc
        lower[ROW_D - 256 : ROW_D - 224, 0:128] = dot_nt(view_code.astype(F32), g_r[...], HIGH)
        lower[ROW_D - 256 : ROW_D - 224, 128:256] = jnp.concatenate([tints, jnp.zeros((16, 128), F32)], 0)
    rest = grads_fine[1].source
    rest[ROW_D - 224 : ROW_D - 223, 0:NHIST] = binned
    fold = loss[:, :128]
    for k in range(1, lanes // 128):
        fold = fold + loss[:, k * 128 : k * 128 + 128]
    rest[ROW_D - 223 : ROW_D - 222, 0:128] = fold
    grads_fine[1].step(0)
    for k in range(1, params.steps):
        for part in grads_fine:
            part.step(k)
    outward = [
        pltpu.make_async_copy(part.whole, result.at[pl.ds(i * 256, 256)], leaving.at[i])
        for i, part in enumerate(grads + grads_fine)
    ]
    for copy in outward:
        copy.start()
    for copy in outward:
        copy.wait()


def adamw_update(weight, moment, square, gradient):
    moment_next = beta_first * moment + (1.0 - beta_first) * gradient
    square_next = beta_second * square + (1.0 - beta_second) * gradient * gradient
    first_hat = moment_next / (1.0 - beta_first**step_count)
    second_hat = square_next / (1.0 - beta_second**step_count)
    weight_next = weight - learn_rate * (
        first_hat / (jnp.sqrt(second_hat) + adam_epsilon) + decay_rate * weight
    )
    return (weight_next, moment_next, square_next)


def update_kernel(tiles_y, owners_given, grads_given, *refs):
    given, outs, taken = refs[0:15], refs[15:17], refs[17:32]
    held = refs[32:47]
    grads, owners, loss, histogram, arrived, left, ends = refs[47:]
    device = lax.axis_index("tx") * tiles_y + lax.axis_index("ty")
    order = (1, 2, 0, 4, 3)
    fetch = [
        pltpu.make_async_copy(grads_given, grads, ends.at[0]),
        pltpu.make_async_copy(owners_given, owners, ends.at[1]),
    ]
    for copy in fetch:
        copy.start()
    for group in order:
        for i in (group, group + 5, group + 10):
            pltpu.make_async_copy(given[i], held[i], arrived.at[i]).start()
    for copy in fetch:
        copy.wait()
    histogram[...] = grads[ROWS + ROW_D + 32 : ROWS + ROW_D + 33, 0:NHIST]
    loss[...] = jnp.sum(grads[ROWS + ROW_D + 33 : ROWS + ROW_D + 34, 0:128], 1, keepdims=True)
    figures = [
        pltpu.make_async_copy(loss, outs[0], ends.at[2]),
        pltpu.make_async_copy(histogram, outs[1], ends.at[3]),
    ]
    for copy in figures:
        copy.start()

    def step(group, at, gradient):
        trio = (held[group], held[group + 5], held[group + 10])
        for ref, now in zip(trio, adamw_update(*[ref[at] for ref in trio], gradient)):
            ref[at] = now

    every = slice(None)

    def update(group, net):
        base = net * ROWS
        last = grads[base + ROW_D : base + ROW_D + 32]
        if group == 0:
            choose = selector(64, held[0].shape[0], LPOS, 32, F32)
            step(0, (every, net, every), dot_tn(choose, grads[base + ROW_E : base + ROW_E + 64], HIGH))
        elif group == 1:
            step(1, (net,), grads[base + ROW_M : base + ROW_M + 256].T)
        elif group == 2:
            views = grads[base + ROW_V : base + ROW_V + 128]
            step(2, (slice(0, 128), net, every), views[:, 0:128].T)
            step(2, (slice(128, 256), net, every), views[:, 128:256].T)
            rest = slice(256, held[2].shape[0])
            choose = selector(32, held[2].shape[0] - 256, LDIR, 16, F32)
            step(2, (rest, net, every), dot_tn(choose, last[:, :128], HIGH))
        elif group == 3:
            step(3, (every, net, every), last[0:3, 128:])
        else:
            misc = grads[base + ROW_S : base + ROW_S + 16]
            spot = slice(net, net + 1)
            step(4, (spot, slice(0, 256)), grads[base + ROW_E + 63 : base + ROW_E + 64])
            step(4, (spot, slice(256, 512)), misc[1:2])
            step(4, (spot, slice(512, 768)), misc[0:1])
            bias = jnp.concatenate([last[28:29, :128], jnp.zeros((1, 128), F32)], 1)
            bias = pltpu.roll(jnp.broadcast_to(bias, (8, 256)), 1, 1)[0:1]
            step(4, (spot, slice(768, 900)), (misc[2:3] + bias)[:, :132])

    def send(group):
        for i in (group, group + 5, group + 10):
            pltpu.make_async_copy(held[i], taken[i], left.at[i]).start()

    mine = [(owners[0, group] == device) | (owners[1, group] == device) for group in range(5)]
    for group in order:
        for i in (group, group + 5, group + 10):
            pltpu.make_async_copy(given[i], held[i], arrived.at[i]).wait()
        pl.when(jnp.logical_not(mine[group]))(functools.partial(send, group))
    for group in order:
        for net in range(2):
            pl.when(owners[net, group] == device)(functools.partial(update, group, net))
        pl.when(mine[group])(functools.partial(send, group))
    for i in range(15):
        pltpu.make_async_copy(held[i], taken[i], left.at[i]).wait()
    for copy in figures:
        copy.wait()


ANY_SPEC = pl.BlockSpec(memory_space=pl.ANY)
VMEM_SPEC = pl.BlockSpec(memory_space=pltpu.VMEM)
SMEM_SPEC = pl.BlockSpec(memory_space=pltpu.SMEM)


def per_device(sizes, camera, ray_mask, ray_direction, anchors, target, fine_levels, density_bins, owners, *trees):
    turns = ((2, 0, 1), (0, 1, 2), (2, 0, 1), (1, 0, 2), (0, 1))
    states = [jnp.transpose(x[0], turns[i % 5]) for i, x in enumerate(trees)]
    lanes = camera.shape[0] * camera.shape[1]
    samples = fine_levels.shape[0]
    levels = jnp.transpose(fine_levels, (1, 2, 0)).reshape(lanes, samples)
    bins = jnp.transpose(density_bins, (1, 2, 0)).reshape(lanes, samples)

    groups = groups_of(sizes)
    turned_round = groups[:1] + groups[:0:-1]
    param_plan = plan_of(groups, ROWS, 16, groups[2:])
    upper, lower = plan_of(groups, 256, 8, groups[2:]), plan_of(turned_round, 256, 8, turned_round[2:])
    plans = [(param_plan, 16), (param_plan, 16), (plan_of(groups, 8, 8, groups), 8)]
    plans += [(upper, 8), (lower, 8)] * 2
    sums = []
    kinds = [(BF16, 256, 0)] * 2 + [(F32, 128, 0)] + [(F32, 256, 16), (F32, 256, 0)] * 2
    for (plan, _), kind in zip(plans, kinds):
        sums += sum_scratch(plan, *kind)
    points = CHUNK * lanes
    chunks = samples // CHUNK
    blocks = samples // GROUP
    small = [camera, ray_mask, ray_direction, target, anchors]
    grads = pl.pallas_call(
        functools.partial(step_kernel, sizes, groups, plans),
        out_shape=jax.ShapeDtypeStruct((2 * ROWS, 256), F32),
        in_specs=[ANY_SPEC] * 13,
        out_specs=ANY_SPEC,
        scratch_shapes=[
            pltpu.VMEM((blocks + SC // GROUP, 64, GROUP * lanes), BF16),
            pltpu.VMEM((chunks, 256, points), BF16),
            pltpu.VMEM((chunks, 256, points), BF16),
            pltpu.VMEM((chunks, 128, points), BF16),
            pltpu.VMEM((4, blocks, GROUP, lanes), F32),
            pltpu.VMEM((blocks + SC // GROUP, GROUP, lanes), F32),
            pltpu.VMEM((4, blocks, GROUP, lanes), F32),
            pltpu.VMEM((NHIST, 1, 128), F32),
            pltpu.VMEM((256, 64), BF16),
            pltpu.VMEM((256, 256), BF16),
            pltpu.VMEM((144, 256), BF16),
            pltpu.VMEM((256, 144), BF16),
            pltpu.VMEM((16, 144), BF16),
            pltpu.VMEM((128, 16), BF16),
            pltpu.VMEM((256, 128), F32),
            pltpu.VMEM((128, lanes), F32),
            pltpu.VMEM((144, 16), F32),
            pltpu.VMEM((128, lanes), F32),
            pltpu.VMEM((points, 256), BF16),
            pltpu.VMEM((8, lanes), F32),
            pltpu.VMEM((4, 8, lanes), F32),
            pltpu.SemaphoreType.DMA((4,)),
            pltpu.SemaphoreType.DMA((4,)),
            pltpu.SemaphoreType.DMA((4,)),
            pltpu.SemaphoreType.DMA((13,)),
            pltpu.SMEM((2, 5), jnp.int32),
        ]
        + [pltpu.VMEM(x.shape, x.dtype) for x in states[:5] + small + [levels, bins]]
        + sums,
        compiler_params=pltpu.CompilerParams(collective_id=0, has_side_effects=True, vmem_limit_bytes=LIMIT),
        name="step",
    )(owners.T, camera, ray_mask, ray_direction, target, levels, bins, anchors, *states[:5])

    results = pl.pallas_call(
        functools.partial(update_kernel, sizes["ty"]),
        out_shape=[jax.ShapeDtypeStruct((1, 1), F32), jax.ShapeDtypeStruct((1, NHIST), F32)]
        + [jax.ShapeDtypeStruct(x.shape, F32) for x in states],
        in_specs=[ANY_SPEC] * 17,
        out_specs=[ANY_SPEC] * 17,
        scratch_shapes=[pltpu.VMEM(x.shape, F32) for x in states]
        + [
            pltpu.VMEM((2 * ROWS, 256), F32),
            pltpu.SMEM((2, 5), jnp.int32),
            pltpu.VMEM((1, 1), F32),
            pltpu.VMEM((1, NHIST), F32),
            pltpu.SemaphoreType.DMA((15,)),
            pltpu.SemaphoreType.DMA((15,)),
            pltpu.SemaphoreType.DMA((4,)),
        ],
        name="update",
    )(owners.T, grads, *states)
    turned = []
    for i, x in enumerate(results[2:]):
        turn = turns[i % 5]
        turned.append(jnp.transpose(x, [turn.index(d) for d in range(len(turn))])[None])
    return (results[0].reshape(()), results[1].reshape(NHIST)) + tuple(turned)


def solution(mesh):
    sizes = dict(mesh.shape)
    tiled, tiled3 = P("ty", "tx"), P(None, "ty", "tx")
    slots = P(("tx", "ty"), None, None, None)
    trees = (slots, slots, slots, slots, P(("tx", "ty"), None, None))
    return jax.shard_map(
        functools.partial(per_device, sizes),
        mesh=mesh,
        in_specs=(tiled, tiled, tiled3, P(), tiled3, tiled3, tiled3, P()) + trees * 3,
        out_specs=(P(), P()) + trees * 3,
        check_vma=False,
    )
```
